32 devices in a mesh: win: 2 (over x), lat: 4 (over y, core), lon: 4 (over z).
Axes of the slice: x: 2, y: 2, z: 4, core: 2. Of those that a mesh axis runs over, the one named last changes fastest.
Arguments:
- increment: float32 [2, 3, 256, 1024], P('win', None, 'lat', 'lon'), may hold values from -6 to 6
- model_weight: float32 [2, 3, 256, 1024], P('win', None, 'lat', 'lon'), may hold values from 0.25 to 4
- winds: float32 [2, 2, 256, 1024], P('win', None, 'lat', 'lon'), may hold values from -0.3 to 0.3
- reaction: float32 [2, 3, 3], P('win'), may hold values from -1 to 1
- obs_cells: int32 [2, 4, 4, 1024], P('win', 'lat', 'lon'), may hold values from 0 to 16383
- obs_weight: float32 [2, 3, 4, 4, 1024], P('win', None, 'lat', 'lon'), may hold values from 0.5 to 8
Outputs:
- hess_vec: float32 [2, 3, 256, 1024], P('win', None, 'lat', 'lon')
The draws below stay inside these ranges and needn't reach their ends.
Inputs may be any that keep to these rules, and one draw needn't show every extreme that they name: `obs_cells`: an index row * 256 + column within its tile.
All inputs are finite; a program needn't handle non-finite values.
Results may differ from the reference program's by a relative error of at most 0.00002.
Values sent between devices are 32-bit elements; how exact they have to be, the bound alone decides.
No kernel may reach another device: no remote copies, remote signals or barrier semaphores. Data moves between devices by JAX's collectives and lax.ppermute only.
A program may use at most 64 MiB of HBM per device.

```python
import math
import jax
import jax.numpy as jnp

FIELDS = 3
CLAT = 64
CLON = 256
NOBS = 1024
WINDOWS = 2
LAT_TILES = 4
LON_TILES = 4
NLAT = 256
NLON = 1024


def set_ends(values, stream_key, smallest, largest):
    dims = values.shape
    index_at = [jax.random.randint(jax.random.fold_in(stream_key, axis), (), 0, dims[axis]) for axis in range(len(dims))]
    values = values.at[tuple(index_at)].set(smallest)
    longest = dims.index(max(dims))
    index_at[longest] = (index_at[longest] + 1) % dims[longest]
    return values.at[tuple(index_at)].set(largest)


def levels(own_key, extent, cuts, low, high):
    gain = 1.0
    for dim, shards_of in cuts:
        draws = jax.random.uniform(jax.random.fold_in(jax.random.fold_in(own_key, 6), dim), (shards_of,), jnp.float32, low / len(cuts), high / len(cuts))
        gain = gain * jnp.repeat(jnp.exp(draws), extent[dim] // shards_of).reshape((-1,) + (1,) * (len(extent) - 1 - dim))
    return gain


def scatter_about(rng, extent, width, bound, shards=(), dtype=jnp.bfloat16):
    level = levels(rng, extent, shards, -0.22, 0.18) if shards else 1.0
    values = jax.random.normal(rng, extent, jnp.float32) * width * level
    return jnp.minimum(jnp.maximum(values, -bound), bound).astype(dtype)


def setup_inputs(seed: int = 0) -> dict:
    key_of = jax.random.split(jax.random.key(seed), 7)
    return {
        "increment": scatter_about(key_of[0], (WINDOWS, FIELDS, NLAT, NLON), 1.0, 6.0, ((0, 2), (2, 4), (3, 4)), jnp.float32),
        "model_weight": jnp.clip(jnp.exp(math.log(4.0) - 2.7725887 * jax.random.uniform(key_of[1], (WINDOWS, FIELDS, NLAT, NLON), jnp.float32) ** levels(key_of[1], (WINDOWS, FIELDS, NLAT, NLON), ((0, 2), (2, 4), (3, 4)), -0.2, 0.2)), 0.25, 4.0),
        "winds": jnp.clip(jax.random.uniform(key_of[2], (WINDOWS, 2, NLAT, NLON), jnp.float32, -0.3, 0.3) * levels(key_of[2], (WINDOWS, 2, NLAT, NLON), ((0, 2), (2, 4), (3, 4)), -0.4, 0.0), -0.3, 0.3),
        "reaction": scatter_about(key_of[3], (WINDOWS, FIELDS, FIELDS), 0.2, 1.0, ((0, 2),), jnp.float32),
        "obs_cells": set_ends(jax.random.randint(key_of[4], (WINDOWS, LAT_TILES, LON_TILES, NOBS), 0, CLAT * CLON), jax.random.fold_in(key_of[4], 1), 0, (CLAT * CLON) - 1).astype(jnp.int32),
        "obs_weight": jnp.clip(jnp.exp(math.log(8.0) - 2.7725887 * jax.random.uniform(key_of[5], (WINDOWS, FIELDS, LAT_TILES, LON_TILES, NOBS), jnp.float32) ** levels(key_of[5], (WINDOWS, FIELDS, LAT_TILES, LON_TILES, NOBS), ((0, 2), (2, 4), (3, 4)), -0.2, 0.2)), 0.5, 8.0),
    }


DIFFUSION = 0.15


def neighbours(field):
    padded = jnp.pad(field, ((0, 0), (1, 1), (0, 0)))
    north_side = padded[:, 2:, :]
    south_side = padded[:, :-2, :]
    east_side = jnp.roll(field, -1, axis=2)
    west_side = jnp.roll(field, 1, axis=2)
    return north_side, south_side, east_side, west_side


def mixing(reaction, field):
    return jnp.sum(reaction[:, :, None, None] * field[None], axis=1)


def tangent_step(field, winds, reaction):
    north_side, south_side, east_side, west_side = neighbours(field)
    spread = north_side + south_side + east_side + west_side
    result = (1.0 - 4.0 * DIFFUSION) * field + DIFFUSION * spread
    result = result - winds[0] * (east_side - west_side) - winds[1] * (north_side - south_side)
    return result + mixing(reaction, field)


def adjoint_step(field, winds, reaction):
    north_side, south_side, east_side, west_side = neighbours(field)
    spread = north_side + south_side + east_side + west_side
    lon_flux = neighbours(winds[0] * field)
    lat_flux = neighbours(winds[1] * field)
    result = (1.0 - 4.0 * DIFFUSION) * field + DIFFUSION * spread
    result = result + (lon_flux[2] - lon_flux[3]) + (lat_flux[0] - lat_flux[1])
    return result + mixing(reaction.T, field)


def observe(state, row_ids, column_ids, weight):
    picked = state[:, row_ids, column_ids]
    return jnp.zeros_like(state).at[:, row_ids, column_ids].add(weight * picked)


def reference(increment, model_weight, winds, reaction, obs_cells, obs_weight):
    def forward_pair(field, wind_now, mixer):
        return tangent_step(tangent_step(field, wind_now, mixer), wind_now, mixer)

    def adjoint_pair(field, wind_now, mixer):
        return adjoint_step(adjoint_step(field, wind_now, mixer), wind_now, mixer)

    forward = jax.vmap(forward_pair)(increment, winds, reaction)
    earlier = jnp.concatenate([jnp.zeros_like(forward[:1]), forward[:-1]], axis=0)
    jump = model_weight * (increment - earlier)
    later = jnp.concatenate([jump[1:], jnp.zeros_like(jump[:1])], axis=0)
    lat_base = (jnp.arange(LAT_TILES) * CLAT).astype(jnp.int32)
    lon_base = (jnp.arange(LON_TILES) * CLON).astype(jnp.int32)
    rows = (lat_base[None, :, None, None] + obs_cells // CLON).astype(jnp.int32)
    columns = (lon_base[None, None, :, None] + obs_cells % CLON).astype(jnp.int32)
    observed = jax.vmap(observe)(forward, rows, columns, obs_weight)
    source = observed - later
    back = jax.vmap(adjoint_pair)(source, winds, reaction)
    return jump + back
```

```python
import functools

import jax
import jax.numpy as jnp
from jax import lax
from jax.experimental import pallas as pl
from jax.experimental.pallas import tpu as pltpu
from jax.sharding import PartitionSpec as P

DIFFUSION = 0.15
HALO = 4
LANES = 128
F32 = jnp.float32


def even_pairs(n):
    return [(i, i ^ 1) for i in range(n)]


def odd_pairs(n):
    return [(i, (i + 1 if i % 2 else i - 1) % n) for i in range(n)]


def ring(n, step):
    return [(i, (i + step) % n) for i in range(n)]


def neighbour_swap(even_msg, odd_msg, axis):
    n = lax.axis_size(axis)
    return (
        lax.ppermute(even_msg, axis, even_pairs(n)),
        lax.ppermute(odd_msg, axis, odd_pairs(n)),
    )


def window_swap(down, up):
    n = lax.axis_size("win")
    if n == 2:
        got = lax.ppermute(down, "win", even_pairs(n))
        return got, got
    return lax.ppermute(down, "win", ring(n, -1)), lax.ppermute(up, "win", ring(n, 1))


def sub_iota(shape):
    return lax.broadcasted_iota(jnp.int32, shape, len(shape) - 2)


def lane_iota(shape):
    return lax.broadcasted_iota(jnp.int32, shape, len(shape) - 1)


def pack_columns(planes, low):
    out = None
    for j, plane in enumerate(planes):
        block = plane[:, :LANES] if low else plane[:, -LANES:]
        shift = (HALO * j if low else HALO * j + HALO) % LANES
        if shift:
            block = pltpu.roll(block, shift, 1)
        lane = lane_iota(block.shape)
        out = block if out is None else jnp.where(lane >= HALO * j, block, out)
    return out


def start_kernel(swap2, inc, wgt, wind, mix, cells, scale, hmap, row_even, row_odd, col_low, col_high, *bulk):
    fields, rows, cols = inc.shape
    nobs = cells.shape[-1]
    index = cells[...]
    row_hot = sub_iota((rows, nobs)) == index // cols
    col_hot = (sub_iota((cols, nobs)) == index % cols).astype(F32).astype(jnp.bfloat16)
    terms = []
    for f in range(fields):
        rest = scale[f]
        for _ in range(3):
            part = rest.astype(jnp.bfloat16)
            rest = rest - part.astype(F32)
            terms.append(jnp.where(row_hot, part.astype(F32), 0.0).astype(jnp.bfloat16))
    sums = lax.dot_general(
        jnp.concatenate(terms, axis=0), col_hot, (((1,), (1,)), ((), ())), preferred_element_type=F32
    )
    planes = [inc[f] for f in range(fields)] + [wind[0], wind[1]]
    for f in range(fields):
        base = 3 * f * rows
        value = sums[base : base + rows] + (
            sums[base + rows : base + 2 * rows] + sums[base + 2 * rows : base + 3 * rows]
        )
        hmap[f] = value
        planes.append(value)
    planes += [wgt[f] for f in range(fields)]
    col_low[...] = pack_columns(planes, True)
    col_high[...] = pack_columns(planes, False)
    is_even = lax.axis_index("lat") % 2 == 0
    upper = sub_iota((8, cols)) < HALO
    for m in range((len(planes) + 1) // 2):
        one, two = planes[2 * m], planes[min(2 * m + 1, len(planes) - 1)]
        first = jnp.where(upper, one[:8], pltpu.roll(two[:8], HALO, 0))
        last = jnp.where(upper, pltpu.roll(one[-8:], HALO, 0), two[-8:])
        row_even[pl.ds(8 * m, 8), :] = jnp.where(is_even, last, first)
        row_odd[pl.ds(8 * m, 8), :] = jnp.where(is_even, first, last)
    mixrows = jnp.zeros((rows, cols), F32)
    which = sub_iota((rows, cols))
    for f in range(fields):
        for g in range(fields):
            mixrows = jnp.where(which == f * fields + g, mix[f, g], mixrows)
    up = [wind[0], wind[1], mixrows]
    for f in range(fields):
        if swap2:
            sends_up = lax.axis_index("win") == 0
            bulk[0][f] = inc[f]
            bulk[0][fields + f] = jnp.where(sends_up, up[f], wgt[f])
        else:
            bulk[0][f] = inc[f]
            bulk[0][fields + f] = wgt[f]
            bulk[1][f] = inc[f]
            bulk[1][fields + f] = up[f]


def rows_kernel(count, got_even, got_odd, col_low, col_high, halo_rows, msg_even, msg_odd):
    cols = got_even.shape[-1]
    rows = col_low.shape[0]
    here = lax.axis_index("lat")
    is_even = here % 2 == 0
    upper = sub_iota((8, cols)) < HALO
    from_high = (here < lax.axis_size("lat") - 1).astype(jnp.int32)
    from_low = (here > 0).astype(jnp.int32)
    inside = jnp.where(upper, from_high, from_low) > 0
    blocks = []
    for m in range((count + 1) // 2):
        a = got_even[pl.ds(8 * m, 8), :]
        b = got_odd[pl.ds(8 * m, 8), :]
        high = jnp.where(is_even, a, b)
        low = jnp.where(is_even, b, a)
        one = jnp.where(upper, high, pltpu.roll(low, HALO, 0))
        two = jnp.where(upper, pltpu.roll(high, HALO, 0), low)
        blocks += [jnp.where(inside, one, 0.0), jnp.where(inside, two, 0.0)]
    blocks = blocks[:count]
    for j, block in enumerate(blocks):
        halo_rows[j] = block
    lon_even = lax.axis_index("lon") % 2 == 0
    low_tail = pack_columns(blocks, True)
    high_tail = pack_columns(blocks, False)
    msg_even[pl.ds(0, rows), :] = jnp.where(lon_even, col_high[...], col_low[...])
    msg_odd[pl.ds(0, rows), :] = jnp.where(lon_even, col_low[...], col_high[...])
    msg_even[pl.ds(rows, 8), :] = jnp.where(lon_even, high_tail, low_tail)
    msg_odd[pl.ds(rows, 8), :] = jnp.where(lon_even, low_tail, high_tail)


def columns_kernel(swap2, fields, count, got_even, got_odd, halo_rows, halo_cols, *msgs):
    lon_even = lax.axis_index("lon") % 2 == 0
    a = got_even[...]
    b = got_odd[...]
    east = jnp.where(lon_even, a, b)
    west = jnp.where(lon_even, b, a)
    lane = lane_iota(a.shape)
    cols = []
    for j in range(count):
        right = pltpu.roll(east, (LANES - HALO * j) % LANES, 1) if j else east
        left = pltpu.roll(west, (LANES - HALO - HALO * j) % LANES, 1)
        block = jnp.where(lane < HALO, right, jnp.where(lane >= LANES - HALO, left, 0.0))
        halo_cols[j] = block
        cols.append(block)
    first = list(range(fields))
    down = first + list(range(count - fields, count))
    up = first + [fields, fields + 1, fields + 1]
    total = a.shape[0]
    sub = sub_iota((8, halo_rows.shape[-1]))
    keep = (sub < 2) | (sub >= 6)

    def packed(chosen):
        rows = []
        for m in range(fields):
            one, two = halo_rows[chosen[2 * m]], halo_rows[chosen[2 * m + 1]]
            rows.append(jnp.where(keep, one, pltpu.roll(two, 4, 0)))
        out = cols[chosen[0]]
        for j in range(1, 2 * fields):
            moved = pltpu.roll(cols[chosen[j]], 4 * j, 1)
            out = jnp.where((lane >= 4 * j - 2) & (lane < 4 * j + 2), moved, out)
        return rows, out

    def store(ref, rows, out):
        for m, block in enumerate(rows):
            for half in range(block.shape[-1] // LANES):
                ref[pl.ds(total + 8 * (m * (block.shape[-1] // LANES) + half), 8), :] = block[
                    :, half * LANES : (half + 1) * LANES
                ]
        ref[pl.ds(0, total), :] = out

    down_rows, down_cols = packed(down)
    up_rows, up_cols = packed(up)
    if swap2:
        sends_up = lax.axis_index("win") == 0
        store(
            msgs[0],
            [jnp.where(sends_up, u, d) for u, d in zip(up_rows, down_rows)],
            jnp.where(sends_up, up_cols, down_cols),
        )
    else:
        store(msgs[0], down_rows, down_cols)
        store(msgs[1], up_rows, up_cols)


def extended(tile, rows, cols):
    return jnp.concatenate([jnp.concatenate([tile, rows], axis=0), cols], axis=1)


def row_mask(rows, width):
    here = lax.axis_index("lat")
    upper = sub_iota((8, width)) < HALO
    from_high = (here < lax.axis_size("lat") - 1).astype(jnp.int32)
    from_low = (here > 0).astype(jnp.int32)
    inside = jnp.where(upper, from_high, from_low) > 0

    def clear(field):
        return jnp.concatenate([field[:rows], jnp.where(inside, field[rows:], 0.0)], axis=0)

    return clear


def north(x):
    return pltpu.roll(x, x.shape[0] - 1, 0)


def south(x):
    return pltpu.roll(x, 1, 0)


def east_of(x):
    return pltpu.roll(x, x.shape[1] - 1, 1)


def west_of(x):
    return pltpu.roll(x, 1, 1)


def blend(mix, field, f):
    total = None
    for g in range(len(field)):
        factor = mix(f, g)
        if f == g:
            factor = factor + (1.0 - 4.0 * DIFFUSION)
        term = factor * field[g]
        total = term if total is None else total + term
    return total


def tangent(field, u, v, mix):
    kn, ks, ke, kw = DIFFUSION - v, DIFFUSION + v, DIFFUSION - u, DIFFUSION + u
    return [
        blend(mix, field, f)
        + (kn * north(x) + ks * south(x))
        + (ke * east_of(x) + kw * west_of(x))
        for f, x in enumerate(field)
    ]


def adjoint(field, u, v, mix):
    kn, ks, ke, kw = DIFFUSION + v, DIFFUSION - v, DIFFUSION + u, DIFFUSION - u
    return [
        blend(lambda a, b: mix(b, a), field, f)
        + (north(kn * x) + south(ks * x))
        + (east_of(ke * x) + west_of(kw * x))
        for f, x in enumerate(field)
    ]


def forward_kernel(inc, wind, mix, halo_rows, halo_cols, fwd):
    fields, rows, _ = inc.shape
    field = [extended(inc[f], halo_rows[f], halo_cols[f]) for f in range(fields)]
    u, v = [extended(wind[i], halo_rows[fields + i], halo_cols[fields + i]) for i in range(2)]
    clear = row_mask(rows, field[0].shape[1])
    mixer = lambda f, g: mix[f, g]
    field = [clear(x) for x in tangent(field, u, v, mixer)]
    field = tangent(field, u, v, mixer)
    for f in range(fields):
        fwd[f] = field[f]


def finish_kernel(fwd, inc, wgt, wind, mix, hmap, halo_rows, halo_cols, above, below, ring_above, ring_below, out):
    fields, rows, cols = inc.shape
    blocks = cols // LANES
    total = halo_cols.shape[1]
    here = lax.axis_index("win")
    clear = row_mask(rows, cols + LANES)

    def unpack(bulk, msg, j):
        m, second = j // 2, j % 2
        base = total + 8 * m * blocks
        block = jnp.concatenate([msg[pl.ds(base + 8 * h, 8), :] for h in range(blocks)], axis=1)
        if second:
            block = pltpu.roll(block, 4, 0)
        side = msg[pl.ds(0, total), :]
        if j:
            side = pltpu.roll(side, LANES - 4 * j, 1)
        return extended(bulk[j], block, side)

    has_later = here < lax.axis_size("win") - 1
    source = []
    for f in range(fields):
        x = fwd[f]
        later = unpack(above, ring_above, fields + f) * (unpack(above, ring_above, f) - x)
        h = extended(hmap[f], halo_rows[fields + 2 + f], halo_cols[fields + 2 + f])
        source.append(clear(h * x - jnp.where(has_later, later, 0.0)))
    u, v = [extended(wind[i], halo_rows[fields + i], halo_cols[fields + i]) for i in range(2)]
    mixer = lambda f, g: mix[f, g]
    back = [clear(x) for x in adjoint(source, u, v, mixer)]
    back = adjoint(back, u, v, mixer)

    has_earlier = here > 0
    prior = [clear(unpack(below, ring_below, f)) for f in range(fields)]
    u, v = [unpack(below, ring_below, fields + i) for i in range(2)]
    mixrows = below[2 * fields - 1]

    def prior_mix(f, g):
        return mixrows[f * fields + g : f * fields + g + 1, 0:1]

    prior = [clear(x) for x in tangent(prior, u, v, prior_mix)]
    prior = tangent(prior, u, v, prior_mix)
    for f in range(fields):
        earlier = jnp.where(has_earlier, prior[f][:rows, :cols], 0.0)
        out[f] = wgt[f] * (inc[f] - earlier) + back[f][:rows, :cols]


def vmem():
    return pl.BlockSpec(memory_space=pltpu.VMEM)


def smem():
    return pl.BlockSpec(memory_space=pltpu.SMEM)


def call(kernel, name, in_specs, shapes, flops):
    return pl.pallas_call(
        kernel,
        name=name,
        out_shape=[jax.ShapeDtypeStruct(s, F32) for s in shapes],
        in_specs=in_specs,
        out_specs=[vmem()] * len(shapes),
        cost_estimate=pl.CostEstimate(flops=flops, bytes_accessed=1 << 20, transcendentals=0),
    )


def per_device(increment, model_weight, winds, reaction, obs_cells, obs_weight):
    inc = increment[0]
    wgt = model_weight[0]
    wind = winds[0]
    mix = reaction[0]
    fields, rows, cols = inc.shape
    nobs = obs_cells.shape[-1]
    cells = obs_cells.reshape(1, nobs)
    scale = obs_weight.reshape(fields, 1, nobs)
    count = 3 * fields + 2
    pairs = (count + 1) // 2
    tall = rows + 2 * HALO
    swap2 = lax.axis_size("win") == 2
    copies = 1 if swap2 else 2

    hmap, row_even, row_odd, col_low, col_high, *bulk = call(
        functools.partial(start_kernel, swap2),
        "start",
        [vmem(), vmem(), vmem(), smem(), vmem(), vmem()],
        [(fields, rows, cols)] + [(8 * pairs, cols)] * 2 + [(rows, LANES)] * 2 + [(2 * fields, rows, cols)] * copies,
        1 << 24,
    )(inc, wgt, wind, mix, cells, scale)
    got_even, got_odd = neighbour_swap(row_even, row_odd, "lat")
    above, below = window_swap(bulk[0], bulk[-1])

    halo_rows, msg_even, msg_odd = call(
        functools.partial(rows_kernel, count),
        "rows",
        [vmem()] * 4,
        [(count, 8, cols), (tall, LANES), (tall, LANES)],
        1 << 16,
    )(got_even, got_odd, col_low, col_high)
    got_even, got_odd = neighbour_swap(msg_even, msg_odd, "lon")

    ring_shape = (tall + 8 * fields * (cols // LANES), LANES)
    halo_cols, *rings = call(
        functools.partial(columns_kernel, swap2, fields, count),
        "columns",
        [vmem()] * 3,
        [(count, tall, LANES)] + [ring_shape] * copies,
        1 << 16,
    )(got_even, got_odd, halo_rows)
    ring_above, ring_below = window_swap(rings[0], rings[-1])

    (fwd,) = call(
        forward_kernel,
        "forward",
        [vmem(), vmem(), smem(), vmem(), vmem()],
        [(fields, tall, cols + LANES)],
        1 << 24,
    )(inc, wind, mix, halo_rows, halo_cols)

    (out,) = call(
        finish_kernel,
        "finish",
        [vmem()] * 4 + [smem()] + [vmem()] * 7,
        [(fields, rows, cols)],
        1 << 25,
    )(fwd, inc, wgt, wind, mix, hmap, halo_rows, halo_cols, above, below, ring_above, ring_below)
    return out[None]


def solution(mesh):
    in_specs = (
        P("win", None, "lat", "lon"),
        P("win", None, "lat", "lon"),
        P("win", None, "lat", "lon"),
        P("win", None, None),
        P("win", "lat", "lon", None),
        P("win", None, "lat", "lon", None),
    )
    out_specs = P("win", None, "lat", "lon")
    return jax.shard_map(
        per_device, mesh=mesh, in_specs=in_specs, out_specs=out_specs, check_vma=False
    )
```

```python
import functools

import jax
import jax.numpy as jnp
from jax import lax
from jax.experimental import pallas as pl
from jax.experimental.pallas import tpu as pltpu
from jax.sharding import PartitionSpec as P

DIFFUSION = 0.15
HALO = 4
LANES = 128
F32 = jnp.float32


def even_pairs(n):
    return [(i, i ^ 1) for i in range(n)]


def odd_pairs(n):
    return [(i, (i + 1 if i % 2 else i - 1) % n) for i in range(n)]


def ring(n, step):
    return [(i, (i + step) % n) for i in range(n)]


def neighbour_swap(even_msg, odd_msg, axis):
    n = lax.axis_size(axis)
    return (
        lax.ppermute(even_msg, axis, even_pairs(n)),
        lax.ppermute(odd_msg, axis, odd_pairs(n)),
    )


def window_swap(down, up):
    n = lax.axis_size("win")
    if n == 2:
        got = lax.ppermute(down, "win", even_pairs(n))
        return got, got
    return lax.ppermute(down, "win", ring(n, -1)), lax.ppermute(up, "win", ring(n, 1))


def sub_iota(shape):
    return lax.broadcasted_iota(jnp.int32, shape, len(shape) - 2)


def lane_iota(shape):
    return lax.broadcasted_iota(jnp.int32, shape, len(shape) - 1)


def pack_columns(planes, low):
    out = None
    for j, plane in enumerate(planes):
        block = plane[:, :LANES] if low else plane[:, -LANES:]
        shift = (HALO * j if low else HALO * j + HALO) % LANES
        if shift:
            block = pltpu.roll(block, shift, 1)
        lane = lane_iota(block.shape)
        out = block if out is None else jnp.where(lane >= HALO * j, block, out)
    return out


def start_kernel(swap2, copies, *refs):
    inc_far, wgt_far, wind_far, mix_far, cells_far, scale_far, inc, wgt, wind, hmap = refs[:10]
    row_even, row_odd, col_low, col_high, mixrows = refs[10:15]
    bulk = refs[15 : 15 + copies]
    cells, scale, mix, sems = refs[15 + copies :]
    moves = [
        pltpu.make_async_copy(far, near, sems.at[i])
        for i, (far, near) in enumerate(
            [(cells_far, cells), (scale_far, scale), (inc_far, inc), (wind_far, wind), (wgt_far, wgt), (mix_far, mix)]
        )
    ]
    for move in moves:
        move.start()
    fields, rows, cols = inc.shape
    nobs = cells.shape[-1]
    moves[0].wait()
    index = cells[...]
    row_hot = sub_iota((rows, nobs)) == index // cols
    col_hot = (sub_iota((cols, nobs)) == index % cols).astype(F32).astype(jnp.bfloat16)
    terms = []
    moves[1].wait()
    for f in range(fields):
        rest = scale[f]
        for _ in range(3):
            part = rest.astype(jnp.bfloat16)
            rest = rest - part.astype(F32)
            terms.append(jnp.where(row_hot, part.astype(F32), 0.0).astype(jnp.bfloat16))
    sums = lax.dot_general(
        jnp.concatenate(terms, axis=0), col_hot, (((1,), (1,)), ((), ())), preferred_element_type=F32
    )
    for move in moves[2:]:
        move.wait()
    planes = [inc[f] for f in range(fields)] + [wind[0], wind[1]]
    for f in range(fields):
        base = 3 * f * rows
        value = sums[base : base + rows] + (
            sums[base + rows : base + 2 * rows] + sums[base + 2 * rows : base + 3 * rows]
        )
        hmap[f] = value
        planes.append(value)
    planes += [wgt[f] for f in range(fields)]
    col_low[...] = pack_columns(planes, True)
    col_high[...] = pack_columns(planes, False)
    is_even = lax.axis_index("lat") % 2 == 0
    upper = sub_iota((8, cols)) < HALO
    for m in range((len(planes) + 1) // 2):
        one, two = planes[2 * m], planes[min(2 * m + 1, len(planes) - 1)]
        first = jnp.where(upper, one[:8], pltpu.roll(two[:8], HALO, 0))
        last = jnp.where(upper, pltpu.roll(one[-8:], HALO, 0), two[-8:])
        row_even[pl.ds(8 * m, 8), :] = jnp.where(is_even, last, first)
        row_odd[pl.ds(8 * m, 8), :] = jnp.where(is_even, first, last)
    which = sub_iota(mixrows.shape)
    spread = jnp.zeros(mixrows.shape, F32)
    for f in range(fields):
        for g in range(fields):
            spread = jnp.where(which == f * fields + g, mix[f, 0, g], spread)
    mixrows[...] = spread
    used = mixrows.shape[0]
    up = [wind[0], wind[1], jnp.concatenate([spread[:, :cols], wgt[fields - 1, used:]], axis=0)]
    for f in range(fields):
        if swap2:
            sends_up = lax.axis_index("win") == 0
            bulk[0][f] = inc[f]
            bulk[0][fields + f] = jnp.where(sends_up, up[f], wgt[f])
        else:
            bulk[0][f] = inc[f]
            bulk[0][fields + f] = wgt[f]
            bulk[1][f] = inc[f]
            bulk[1][fields + f] = up[f]


def rows_kernel(count, got_even, got_odd, col_low, col_high, halo_rows, msg_even, msg_odd):
    cols = got_even.shape[-1]
    rows = col_low.shape[0]
    here = lax.axis_index("lat")
    is_even = here % 2 == 0
    upper = sub_iota((8, cols)) < HALO
    from_high = (here < lax.axis_size("lat") - 1).astype(jnp.int32)
    from_low = (here > 0).astype(jnp.int32)
    inside = jnp.where(upper, from_high, from_low) > 0
    blocks = []
    for m in range((count + 1) // 2):
        a = got_even[pl.ds(8 * m, 8), :]
        b = got_odd[pl.ds(8 * m, 8), :]
        high = jnp.where(is_even, a, b)
        low = jnp.where(is_even, b, a)
        one = jnp.where(upper, high, pltpu.roll(low, HALO, 0))
        two = jnp.where(upper, pltpu.roll(high, HALO, 0), low)
        blocks += [jnp.where(inside, one, 0.0), jnp.where(inside, two, 0.0)]
    blocks = blocks[:count]
    for j, block in enumerate(blocks):
        halo_rows[j] = block
    lon_even = lax.axis_index("lon") % 2 == 0
    low_tail = pack_columns(blocks, True)
    high_tail = pack_columns(blocks, False)
    msg_even[pl.ds(0, rows), :] = jnp.where(lon_even, col_high[...], col_low[...])
    msg_odd[pl.ds(0, rows), :] = jnp.where(lon_even, col_low[...], col_high[...])
    msg_even[pl.ds(rows, 8), :] = jnp.where(lon_even, high_tail, low_tail)
    msg_odd[pl.ds(rows, 8), :] = jnp.where(lon_even, low_tail, high_tail)


def columns_kernel(swap2, fields, count, got_even, got_odd, halo_rows, halo_cols, *msgs):
    lon_even = lax.axis_index("lon") % 2 == 0
    a = got_even[...]
    b = got_odd[...]
    east = jnp.where(lon_even, a, b)
    west = jnp.where(lon_even, b, a)
    lane = lane_iota(a.shape)
    cols = []
    for j in range(count):
        right = pltpu.roll(east, (LANES - HALO * j) % LANES, 1) if j else east
        left = pltpu.roll(west, (LANES - HALO - HALO * j) % LANES, 1)
        block = jnp.where(lane < HALO, right, jnp.where(lane >= LANES - HALO, left, 0.0))
        halo_cols[j] = block
        cols.append(block)
    first = list(range(fields))
    down = first + list(range(count - fields, count))
    up = first + [fields, fields + 1, fields + 1]
    total = a.shape[0]
    sub = sub_iota((8, halo_rows.shape[-1]))
    keep = (sub < 2) | (sub >= 6)

    def packed(chosen):
        rows = []
        for m in range(fields):
            one, two = halo_rows[chosen[2 * m]], halo_rows[chosen[2 * m + 1]]
            rows.append(jnp.where(keep, one, pltpu.roll(two, 4, 0)))
        out = cols[chosen[0]]
        for j in range(1, 2 * fields):
            moved = pltpu.roll(cols[chosen[j]], 4 * j, 1)
            out = jnp.where((lane >= 4 * j - 2) & (lane < 4 * j + 2), moved, out)
        return rows, out

    def store(ref, rows, out):
        for m, block in enumerate(rows):
            for half in range(block.shape[-1] // LANES):
                ref[pl.ds(total + 8 * (m * (block.shape[-1] // LANES) + half), 8), :] = block[
                    :, half * LANES : (half + 1) * LANES
                ]
        ref[pl.ds(0, total), :] = out

    down_rows, down_cols = packed(down)
    up_rows, up_cols = packed(up)
    if swap2:
        sends_up = lax.axis_index("win") == 0
        store(
            msgs[0],
            [jnp.where(sends_up, u, d) for u, d in zip(up_rows, down_rows)],
            jnp.where(sends_up, up_cols, down_cols),
        )
    else:
        store(msgs[0], down_rows, down_cols)
        store(msgs[1], up_rows, up_cols)


def extended(tile, rows, cols):
    return jnp.concatenate([jnp.concatenate([tile, rows], axis=0), cols], axis=1)


def row_mask(rows, width):
    here = lax.axis_index("lat")
    upper = sub_iota((8, width)) < HALO
    from_high = (here < lax.axis_size("lat") - 1).astype(jnp.int32)
    from_low = (here > 0).astype(jnp.int32)
    inside = jnp.where(upper, from_high, from_low) > 0

    def clear(field):
        return jnp.concatenate([field[:rows], jnp.where(inside, field[rows:], 0.0)], axis=0)

    return clear


def north(x):
    return pltpu.roll(x, x.shape[0] - 1, 0)


def south(x):
    return pltpu.roll(x, 1, 0)


def east_of(x):
    return pltpu.roll(x, x.shape[1] - 1, 1)


def west_of(x):
    return pltpu.roll(x, 1, 1)


def mixing(spread, fields):
    return lambda f, g: spread[f * fields + g : f * fields + g + 1]


def blend(mix, field, f):
    total = None
    for g in range(len(field)):
        factor = mix(f, g)
        if f == g:
            factor = factor + (1.0 - 4.0 * DIFFUSION)
        term = factor * field[g]
        total = term if total is None else total + term
    return total


def tangent(field, u, v, mix):
    kn, ks, ke, kw = DIFFUSION - v, DIFFUSION + v, DIFFUSION - u, DIFFUSION + u
    return [
        blend(mix, field, f)
        + (kn * north(x) + ks * south(x))
        + (ke * east_of(x) + kw * west_of(x))
        for f, x in enumerate(field)
    ]


def adjoint(field, u, v, mix):
    kn, ks, ke, kw = DIFFUSION + v, DIFFUSION - v, DIFFUSION + u, DIFFUSION - u
    return [
        blend(lambda a, b: mix(b, a), field, f)
        + (north(kn * x) + south(ks * x))
        + (east_of(ke * x) + west_of(kw * x))
        for f, x in enumerate(field)
    ]


def forward_kernel(inc, wind, mixrows, halo_rows, halo_cols, fwd):
    fields, rows, _ = inc.shape
    field = [extended(inc[f], halo_rows[f], halo_cols[f]) for f in range(fields)]
    u, v = [extended(wind[i], halo_rows[fields + i], halo_cols[fields + i]) for i in range(2)]
    clear = row_mask(rows, field[0].shape[1])
    mixer = mixing(mixrows[...], fields)
    field = [clear(x) for x in tangent(field, u, v, mixer)]
    field = tangent(field, u, v, mixer)
    for f in range(fields):
        fwd[f] = field[f]


def finish_kernel(fwd, inc, wgt, wind, mixrows, hmap, halo_rows, halo_cols, above, below, ring_above, ring_below, out):
    fields, rows, cols = inc.shape
    blocks = cols // LANES
    total = halo_cols.shape[1]
    here = lax.axis_index("win")
    clear = row_mask(rows, cols + LANES)

    def unpack(bulk, msg, j):
        m, second = j // 2, j % 2
        base = total + 8 * m * blocks
        block = jnp.concatenate([msg[pl.ds(base + 8 * h, 8), :] for h in range(blocks)], axis=1)
        if second:
            block = pltpu.roll(block, 4, 0)
        side = msg[pl.ds(0, total), :]
        if j:
            side = pltpu.roll(side, LANES - 4 * j, 1)
        return extended(bulk[j], block, side)

    has_later = here < lax.axis_size("win") - 1
    source = []
    for f in range(fields):
        x = fwd[f]
        later = unpack(above, ring_above, fields + f) * (unpack(above, ring_above, f) - x)
        h = extended(hmap[f], halo_rows[fields + 2 + f], halo_cols[fields + 2 + f])
        source.append(clear(h * x - jnp.where(has_later, later, 0.0)))
    u, v = [extended(wind[i], halo_rows[fields + i], halo_cols[fields + i]) for i in range(2)]
    mixer = mixing(mixrows[...], fields)
    back = [clear(x) for x in adjoint(source, u, v, mixer)]
    back = adjoint(back, u, v, mixer)

    has_earlier = here > 0
    prior = [clear(unpack(below, ring_below, f)) for f in range(fields)]
    u, v = [unpack(below, ring_below, fields + i) for i in range(2)]
    spread = below[2 * fields - 1, :16]
    prior_mix = mixing(jnp.concatenate([spread, spread[:, :LANES]], axis=1), fields)
    prior = [clear(x) for x in tangent(prior, u, v, prior_mix)]
    prior = tangent(prior, u, v, prior_mix)
    for f in range(fields):
        earlier = jnp.where(has_earlier, prior[f][:rows, :cols], 0.0)
        out[f] = wgt[f] * (inc[f] - earlier) + back[f][:rows, :cols]


def vmem():
    return pl.BlockSpec(memory_space=pltpu.VMEM)


def hbm():
    return pl.BlockSpec(memory_space=pltpu.HBM)


def far(array):
    return pltpu.with_memory_space_constraint(array, pltpu.HBM)


def call(kernel, name, in_specs, shapes, flops, scratch=()):
    return pl.pallas_call(
        kernel,
        name=name,
        scratch_shapes=scratch,
        compiler_params=pltpu.CompilerParams(vmem_limit_bytes=8 << 20),
        out_shape=[jax.ShapeDtypeStruct(s, F32) for s in shapes],
        in_specs=in_specs,
        out_specs=[vmem()] * len(shapes),
        cost_estimate=pl.CostEstimate(flops=flops, bytes_accessed=1 << 20, transcendentals=0),
    )


def per_device(increment, model_weight, winds, reaction, obs_cells, obs_weight):
    inc = increment[0]
    wgt = model_weight[0]
    wind = winds[0]
    mix = reaction.transpose(1, 0, 2)
    fields, rows, cols = inc.shape
    nobs = obs_cells.shape[-1]
    cells = obs_cells.reshape(1, nobs)
    scale = obs_weight.reshape(fields, 1, nobs)
    count = 3 * fields + 2
    pairs = (count + 1) // 2
    tall = rows + 2 * HALO
    swap2 = lax.axis_size("win") == 2
    copies = 1 if swap2 else 2

    tile = (fields, rows, cols)
    inc, wgt, wind, hmap, row_even, row_odd, col_low, col_high, mixrows, *bulk = call(
        functools.partial(start_kernel, swap2, copies),
        "start",
        [hbm()] * 6,
        [tile, tile, (2, rows, cols), tile]
        + [(8 * pairs, cols)] * 2
        + [(rows, LANES)] * 2
        + [(16, cols + LANES)]
        + [(2 * fields, rows, cols)] * copies,
        1 << 24,
        [pltpu.VMEM((1, nobs), jnp.int32), pltpu.VMEM((fields, 1, nobs), F32), pltpu.SMEM(mix.shape, F32), pltpu.SemaphoreType.DMA((6,))],
    )(far(inc), far(wgt), far(wind), far(mix), far(cells), far(scale))
    got_even, got_odd = neighbour_swap(row_even, row_odd, "lat")
    above, below = window_swap(bulk[0], bulk[-1])

    halo_rows, msg_even, msg_odd = call(
        functools.partial(rows_kernel, count),
        "rows",
        [vmem()] * 4,
        [(count, 8, cols), (tall, LANES), (tall, LANES)],
        1 << 16,
    )(got_even, got_odd, col_low, col_high)
    got_even, got_odd = neighbour_swap(msg_even, msg_odd, "lon")

    ring_shape = (tall + 8 * fields * (cols // LANES), LANES)
    halo_cols, *rings = call(
        functools.partial(columns_kernel, swap2, fields, count),
        "columns",
        [vmem()] * 3,
        [(count, tall, LANES)] + [ring_shape] * copies,
        1 << 16,
    )(got_even, got_odd, halo_rows)
    ring_above, ring_below = window_swap(rings[0], rings[-1])

    (fwd,) = call(
        forward_kernel,
        "forward",
        [vmem()] * 5,
        [(fields, tall, cols + LANES)],
        1 << 24,
    )(inc, wind, mixrows, halo_rows, halo_cols)

    (out,) = call(
        finish_kernel,
        "finish",
        [vmem()] * 12,
        [(fields, rows, cols)],
        1 << 25,
    )(fwd, inc, wgt, wind, mixrows, hmap, halo_rows, halo_cols, above, below, ring_above, ring_below)
    return out[None]


def solution(mesh):
    in_specs = (
        P("win", None, "lat", "lon"),
        P("win", None, "lat", "lon"),
        P("win", None, "lat", "lon"),
        P("win", None, None),
        P("win", "lat", "lon", None),
        P("win", None, "lat", "lon", None),
    )
    out_specs = P("win", None, "lat", "lon")
    return jax.shard_map(
        per_device, mesh=mesh, in_specs=in_specs, out_specs=out_specs, check_vma=False
    )
```

```python
import functools

import jax
import jax.numpy as jnp
from jax import lax
from jax.experimental import pallas as pl
from jax.experimental.pallas import tpu as pltpu
from jax.sharding import PartitionSpec as P


DIFFUSION = 0.15
HALO = 4
RIM = 2
LANES = 128
F32 = jnp.float32


def even_pairs(n):
    return [(i, i ^ 1) for i in range(n)]


def odd_pairs(n):
    return [(i, (i + 1 if i % 2 else i - 1) % n) for i in range(n)]


def ring(n, step):
    return [(i, (i + step) % n) for i in range(n)]


def neighbour_swap(even_msg, odd_msg, axis):
    n = lax.axis_size(axis)
    from_even = lax.ppermute(even_msg, axis, even_pairs(n))
    from_odd = lax.ppermute(odd_msg, axis, odd_pairs(n))
    return from_even, from_odd


def window_swap(down, up):
    n = lax.axis_size("win")
    if n == 2:
        got = lax.ppermute(down, "win", even_pairs(n))
        return got, got
    return lax.ppermute(down, "win", ring(n, -1)), lax.ppermute(up, "win", ring(n, 1))


def sub_iota(shape):
    return lax.broadcasted_iota(jnp.int32, shape, len(shape) - 2)


def lane_iota(shape):
    return lax.broadcasted_iota(jnp.int32, shape, len(shape) - 1)


def turn(x, shift, axis):
    shift %= x.shape[axis]
    return pltpu.roll(x, shift, axis) if shift else x


def axis_even(axis):
    return lax.axis_index(axis) % 2 == 0


class Layout:
    def __init__(self, fields, copies):
        self.fields, self.copies = fields, copies
        self.own = 2 + 2 * fields
        self.packet = 2 * fields
        self.depths = [HALO] * (fields + 2) + [RIM] * (fields + self.packet * copies)
        self.count = len(self.depths)
        self.starts = [sum(self.depths[:j]) for j in range(self.count)]
        self.used = sum(self.depths)
        self.row_blocks = -(-self.used // 8)

    def groups(self, blocks, width):
        per = -(-blocks // (LANES // width))
        return -(-blocks // per), per


def squeeze_lanes(wide, width, lay):
    blocks = wide.shape[0] // 8
    groups, per = lay.groups(blocks, width)
    lane = lane_iota((8, LANES))
    out = []
    for i in range(per):
        block = None
        for g in range(groups):
            if g * per + i < blocks:
                part = turn(wide[8 * (g * per + i) : 8 * (g * per + i) + 8], width * g, 1)
                block = part if block is None else jnp.where(lane >= width * g, part, block)
        out.append(block)
    return out


def spread_lanes(tight, blocks, width, lay):
    _, per = lay.groups(blocks, width)
    out = []
    for b in range(blocks):
        g, i = b // per, b % per
        out.append(turn(tight[i], -width * g, 1))
    return jnp.concatenate(out, axis=0)


def pack_rows(pieces, blocks):
    out = [None] * blocks
    for block, first, at, depth in pieces:
        b, s = at // 8, at % 8
        moved = turn(block, s - first, 0)
        sub = sub_iota(moved.shape)
        out[b] = moved if out[b] is None else jnp.where((sub >= s) & (sub < s + depth), moved, out[b])
    return out


def pack_lanes(pieces, out=None):
    for block, first, at, depth in pieces:
        moved = turn(block, at - first, 1)
        lane = lane_iota(moved.shape)
        out = moved if out is None else jnp.where((lane >= at) & (lane < at + depth), moved, out)
    return out


def load_kernel(swap2, copies, *refs):
    inc_far, wgt_far, wind_far, mix_far, cells_far, scale_far = refs[:6]
    inc, wgt, wind, cells, scale, mixrows = refs[6:12]
    bulk = refs[12 : 12 + copies]
    strips = refs[12 + copies : 12 + 2 * copies]
    mix, sems = refs[12 + 2 * copies :]
    fields, rows, cols = inc.shape
    lay = Layout(fields, copies)
    sends_up = lax.axis_index("win") == 0
    moves = [
        pltpu.make_async_copy(src, dst, sems.at[i])
        for i, (src, dst) in enumerate(
            [
                (inc_far, inc),
                (wgt_far, wgt),
                (wind_far, wind),
                (mix_far, mix),
                (cells_far, cells),
                (scale_far, scale),
                (inc_far, bulk[0].at[pl.ds(0, fields)]),
            ]
        )
    ]
    to_down = pltpu.make_async_copy(wgt_far, bulk[0].at[pl.ds(fields, fields)], sems.at[7])
    to_up = pltpu.make_async_copy(wind_far, bulk[-1].at[pl.ds(fields, 2)], sems.at[8])
    for move in moves:
        move.start()
    if swap2:

        @pl.when(sends_up)
        def _():
            to_up.start()

        @pl.when(jnp.logical_not(sends_up))
        def _():
            to_down.start()

    else:
        moves.append(pltpu.make_async_copy(inc_far, bulk[1].at[pl.ds(0, fields)], sems.at[9]))
        moves[-1].start()
        to_up.start()
        to_down.start()
    for move in moves[:4]:
        move.wait()

    first = [inc[f] for f in range(fields)]
    down = first + [wgt[f] for f in range(fields)]
    up = first + [wind[0], wind[1]] + [wind[1]] * (fields - 2)

    def choose(a, b):
        return jnp.where(sends_up, a, b) if swap2 else b

    for k, ref in enumerate(strips):
        planes = [choose(u, d) for u, d in zip(up, down)] if k == 0 else up
        pieces = []
        for j, x in enumerate(planes):
            pieces.append((x[:8], 0, 4 * j, RIM))
            pieces.append((x[-8:], 8 - RIM, 4 * j + 2, RIM))
        blocks = pack_rows(pieces, -(-4 * lay.packet // 8))
        halves = cols // LANES
        for m, block in enumerate(blocks):
            for h in range(halves):
                ref[pl.ds(8 * (m * halves + h), 8), :] = block[:, h * LANES : (h + 1) * LANES]
        pieces = []
        for j, x in enumerate(planes):
            pieces.append((x[:, :LANES], 0, 4 * j, RIM))
            pieces.append((x[:, -LANES:], LANES - RIM, 4 * j + 2, RIM))
        for m, block in enumerate(squeeze_lanes(pack_lanes(pieces), 4 * lay.packet, lay)):
            ref[pl.ds(8 * (len(blocks) * halves + m), 8), :] = block

    which = sub_iota(mixrows.shape)
    spread = jnp.zeros(mixrows.shape, F32)
    for f in range(fields):
        for g in range(fields):
            spread = jnp.where(which == f * fields + g, mix[f, 0, g], spread)
    mixrows[...] = spread

    def finish_up():
        to_up.wait()
        used = mixrows.shape[0]
        bulk[-1][2 * fields - 1, pl.ds(0, used), :] = spread[:, :cols]
        bulk[-1][2 * fields - 1, pl.ds(used, rows - used), :] = jnp.zeros((rows - used, cols), F32)

    if swap2:

        @pl.when(sends_up)
        def _():
            finish_up()

        @pl.when(jnp.logical_not(sends_up))
        def _():
            to_down.wait()

    else:
        to_down.wait()
        finish_up()
    for move in moves[4:]:
        move.wait()


def own_kernel(copies, inc, wind, cells, scale, hmap, row_first, row_last, col_low, col_high):
    fields, rows, cols = inc.shape
    lay = Layout(fields, copies)
    nobs = cells.shape[-1]
    index = cells[...]
    row_hot = sub_iota((rows, nobs)) == index // cols
    col_hot = (sub_iota((cols, nobs)) == index % cols).astype(F32).astype(jnp.bfloat16)
    terms = []
    for f in range(fields):
        rest = scale[f]
        for _ in range(3):
            part = rest.astype(jnp.bfloat16)
            rest = rest - part.astype(F32)
            terms.append(jnp.where(row_hot, part.astype(F32), 0.0).astype(jnp.bfloat16))
    sums = lax.dot_general(
        jnp.concatenate(terms, axis=0), col_hot, (((1,), (1,)), ((), ())), preferred_element_type=F32
    )
    planes = [inc[f] for f in range(fields)] + [wind[0], wind[1]]
    for f in range(fields):
        base = 3 * f * rows
        value = sums[base : base + rows] + (
            sums[base + rows : base + 2 * rows] + sums[base + 2 * rows : base + 3 * rows]
        )
        hmap[f] = value
        planes.append(value)
    where = list(zip(planes, lay.starts, lay.depths))
    first = pack_rows([(x[:8], 0, at, d) for x, at, d in where], lay.row_blocks)
    last = pack_rows([(x[-8:], 8 - d, at, d) for x, at, d in where], lay.row_blocks)
    for m in range(lay.row_blocks):
        blank = jnp.zeros((8, cols), F32)
        row_first[pl.ds(8 * m, 8), :] = blank if first[m] is None else first[m]
        row_last[pl.ds(8 * m, 8), :] = blank if last[m] is None else last[m]
    col_low[...] = pack_lanes([(x[:, :LANES], 0, at, d) for x, at, d in where])
    col_high[...] = pack_lanes([(x[:, -LANES:], LANES - d, at, d) for x, at, d in where])


def join_kernel(fields, copies, *refs):
    row_first, row_last, col_low, col_high = refs[:4]
    strips = refs[4 : 4 + copies]
    row_even, row_odd, low_out, high_out = refs[4 + copies :]
    lay = Layout(fields, copies)
    rows, cols = col_low.shape[0], row_first.shape[1]
    halves = cols // LANES
    strip_blocks = -(-4 * lay.packet // 8)
    first_pieces, last_pieces, low_pieces, high_pieces = [], [], [], []
    for k, ref in enumerate(strips):
        blocks = [
            jnp.concatenate([ref[pl.ds(8 * (m * halves + h), 8), :] for h in range(halves)], axis=1)
            for m in range(strip_blocks)
        ]
        _, per = lay.groups(rows // 8, 4 * lay.packet)
        base = 8 * strip_blocks * halves
        tight = [ref[pl.ds(base + 8 * i, 8), :] for i in range(per)]
        wide = spread_lanes(tight, rows // 8, 4 * lay.packet, lay)
        for j in range(lay.packet):
            at = lay.starts[lay.own + k * lay.packet + j]
            first_pieces.append((blocks[4 * j // 8], 4 * j % 8, at, RIM))
            last_pieces.append((blocks[4 * j // 8], 4 * j % 8 + 2, at, RIM))
            low_pieces.append((wide, 4 * j, at, RIM))
            high_pieces.append((wide, 4 * j + 2, at, RIM))
    is_even = axis_even("lat")
    own_used = lay.starts[lay.own]
    first = pack_rows(first_pieces, lay.row_blocks)
    last = pack_rows(last_pieces, lay.row_blocks)
    for m in range(lay.row_blocks):
        a, b = row_first[pl.ds(8 * m, 8), :], row_last[pl.ds(8 * m, 8), :]
        if first[m] is not None:
            other = sub_iota(a.shape) + 8 * m >= own_used
            a, b = jnp.where(other, first[m], a), jnp.where(other, last[m], b)
        row_even[pl.ds(8 * m, 8), :] = jnp.where(is_even, b, a)
        row_odd[pl.ds(8 * m, 8), :] = jnp.where(is_even, a, b)
    low_out[...] = pack_lanes(low_pieces, col_low[...])
    high_out[...] = pack_lanes(high_pieces, col_high[...])


def lat_inside(width):
    here = lax.axis_index("lat")
    upper = sub_iota((8, width)) < HALO
    from_high = (here < lax.axis_size("lat") - 1).astype(jnp.int32)
    from_low = (here > 0).astype(jnp.int32)
    return jnp.where(upper, from_high, from_low) > 0


def rows_kernel(fields, copies, got_even, got_odd, col_low, col_high, halo_rows, msg_even, msg_odd):
    lay = Layout(fields, copies)
    cols = got_even.shape[-1]
    is_even = axis_even("lat")
    inside = lat_inside(cols)
    sub = sub_iota((8, cols))
    high, low = [], []
    for m in range(lay.row_blocks):
        a = got_even[pl.ds(8 * m, 8), :]
        b = got_odd[pl.ds(8 * m, 8), :]
        high.append(jnp.where(is_even, a, b))
        low.append(jnp.where(is_even, b, a))
    blocks = []
    for j, (at, d) in enumerate(zip(lay.starts, lay.depths)):
        above = turn(high[at // 8], -(at % 8), 0)
        below = turn(low[at // 8], 8 - d - at % 8, 0)
        block = jnp.where(sub < d, above, jnp.where(sub >= 8 - d, below, 0.0))
        block = jnp.where(inside, block, 0.0)
        halo_rows[j] = block
        blocks.append(block)
    where = list(zip(blocks, lay.starts, lay.depths))
    low_tail = pack_lanes([(x[:, :LANES], 0, at, d) for x, at, d in where])
    high_tail = pack_lanes([(x[:, -LANES:], LANES - d, at, d) for x, at, d in where])
    low_all = squeeze_lanes(jnp.concatenate([col_low[...], low_tail], axis=0), lay.used, lay)
    high_all = squeeze_lanes(jnp.concatenate([col_high[...], high_tail], axis=0), lay.used, lay)
    lon_even = axis_even("lon")
    for m, (a, b) in enumerate(zip(low_all, high_all)):
        msg_even[pl.ds(8 * m, 8), :] = jnp.where(lon_even, b, a)
        msg_odd[pl.ds(8 * m, 8), :] = jnp.where(lon_even, a, b)


def row_mask(rows, width):
    inside = lat_inside(width)

    def clear(field):
        return jnp.concatenate([field[:rows], jnp.where(inside, field[rows:], 0.0)], axis=0)

    return clear


def north(x):
    return pltpu.roll(x, x.shape[0] - 1, 0)


def south(x):
    return pltpu.roll(x, 1, 0)


def east_of(x):
    return pltpu.roll(x, x.shape[1] - 1, 1)


def west_of(x):
    return pltpu.roll(x, 1, 1)


def mixing(spread, fields):
    return lambda f, g: spread[f * fields + g : f * fields + g + 1]


def blend(mix, field, f):
    total = None
    for g in range(len(field)):
        factor = mix(f, g)
        if f == g:
            factor = factor + (1.0 - 4.0 * DIFFUSION)
        term = factor * field[g]
        total = term if total is None else total + term
    return total


def tangent(field, u, v, mix):
    kn, ks, ke, kw = DIFFUSION - v, DIFFUSION + v, DIFFUSION - u, DIFFUSION + u
    return [
        blend(mix, field, f)
        + (kn * north(x) + ks * south(x))
        + (ke * east_of(x) + kw * west_of(x))
        for f, x in enumerate(field)
    ]


def adjoint(field, u, v, mix):
    kn, ks, ke, kw = DIFFUSION + v, DIFFUSION - v, DIFFUSION + u, DIFFUSION - u
    return [
        blend(lambda a, b: mix(b, a), field, f)
        + (north(kn * x) + south(ks * x))
        + (east_of(ke * x) + west_of(kw * x))
        for f, x in enumerate(field)
    ]


def product(own, above, below, wgt, mix, prior_mix, fields, rows):
    clear = row_mask(rows, own[0].shape[1])
    here = lax.axis_index("win")
    has_later = here < lax.axis_size("win") - 1
    has_earlier = here > 0
    inc, wind, hmap = own[:fields], own[fields : fields + 2], own[fields + 2 :]
    fwd = [clear(x) for x in tangent(inc, *wind, mix)]
    fwd = tangent(fwd, *wind, mix)
    source = []
    for f in range(fields):
        later = above[fields + f] * (above[f] - fwd[f])
        source.append(clear(hmap[f] * fwd[f] - jnp.where(has_later, later, 0.0)))
    back = [clear(x) for x in adjoint(source, *wind, mix)]
    back = adjoint(back, *wind, mix)
    prior_wind = below[fields : fields + 2]
    prior = [clear(x) for x in tangent(below[:fields], *prior_wind, prior_mix)]
    prior = tangent(prior, *prior_wind, prior_mix)
    return [
        wgt[f] * (inc[f][:rows] - jnp.where(has_earlier, prior[f][:rows], 0.0)) + back[f][:rows]
        for f in range(fields)
    ]


EDGE = 12


def edge_lanes(block_low, block_high):
    low = turn(block_low, HALO, 1)
    high = turn(block_high, HALO + 2 * EDGE, 1)
    return jnp.where(lane_iota(low.shape) < HALO + EDGE, low, high)


def inner_kernel(copies, inc, wgt, wind, hmap, mixrows, halo_rows, *refs):
    bulk = refs[:copies]
    part, edges, wgt_edges, prior_rows = refs[copies:]
    fields, rows, cols = inc.shape
    lay = Layout(fields, copies)
    tiles = [inc[f] for f in range(fields)] + [wind[0], wind[1]] + [hmap[f] for f in range(fields)]
    for ref in bulk:
        tiles += [ref[j] for j in range(lay.packet)]
    planes = []
    for j, tile in enumerate(tiles):
        planes.append(jnp.concatenate([tile, halo_rows[j]], axis=0))
        edges[j] = edge_lanes(planes[-1][:, :LANES], planes[-1][:, -LANES:])
    for f in range(fields):
        wgt_edges[f] = edge_lanes(wgt[f, :, :LANES], wgt[f, :, cols - LANES :])
    above = planes[lay.own : lay.own + lay.packet]
    below = planes[-lay.packet :]
    spread = bulk[-1][2 * fields - 1, :16]
    prior_rows[...] = spread[:, :LANES]
    mix = mixing(mixrows[:, :cols], fields)
    result = product(planes[: lay.own], above, below, wgt, mix, mixing(spread, fields), fields, rows)
    for f in range(fields):
        part[f] = result[f]


def edge_kernel(copies, got_even, got_odd, edges, wgt_edges, part, mixrows, prior_rows, out):
    fields, rows, cols = part.shape
    lay = Layout(fields, copies)
    blocks = rows // 8 + 1
    _, per = lay.groups(blocks, lay.used)
    lon_even = axis_even("lon")
    even = [got_even[pl.ds(8 * i, 8), :] for i in range(per)]
    odd = [got_odd[pl.ds(8 * i, 8), :] for i in range(per)]
    east = spread_lanes([jnp.where(lon_even, a, b) for a, b in zip(even, odd)], blocks, lay.used, lay)
    west = spread_lanes([jnp.where(lon_even, b, a) for a, b in zip(even, odd)], blocks, lay.used, lay)
    lane = lane_iota(east.shape)
    end = HALO + 2 * EDGE
    planes = []
    for j, (at, d) in enumerate(zip(lay.starts, lay.depths)):
        left = turn(west, HALO - d - at, 1)
        right = turn(east, end - at, 1)
        planes.append(
            jnp.where(lane < HALO, left, jnp.where((lane >= end) & (lane < end + d), right, edges[j]))
        )
    above = planes[lay.own : lay.own + lay.packet]
    below = planes[-lay.packet :]
    mix = mixing(mixrows[:, :LANES], fields)
    result = product(
        planes[: lay.own], above, below, wgt_edges, mix, mixing(prior_rows[...], fields), fields, rows
    )
    lane = lane_iota((rows, LANES))
    for f in range(fields):
        low = turn(result[f], -HALO, 1)
        high = turn(result[f], -(HALO + 2 * EDGE), 1)
        whole = part[f]
        if cols == LANES:
            out[f] = jnp.where(lane < HALO, low, jnp.where(lane >= LANES - HALO, high, whole))
        else:
            out[f, :, pl.ds(0, LANES)] = jnp.where(lane < HALO, low, whole[:, :LANES])
            for h in range(1, cols // LANES - 1):
                out[f, :, pl.ds(h * LANES, LANES)] = whole[:, h * LANES : (h + 1) * LANES]
            out[f, :, pl.ds(cols - LANES, LANES)] = jnp.where(lane >= LANES - HALO, high, whole[:, -LANES:])


def vmem():
    return pl.BlockSpec(memory_space=pltpu.VMEM)


def hbm():
    return pl.BlockSpec(memory_space=pltpu.HBM)


def far(array):
    return pltpu.with_memory_space_constraint(array, pltpu.HBM)


def call(kernel, in_specs, shapes, flops, scratch=()):
    return pl.pallas_call(
        kernel,
        scratch_shapes=scratch,
        compiler_params=pltpu.CompilerParams(vmem_limit_bytes=VMEM_LIMIT),
        out_shape=[s if isinstance(s, jax.ShapeDtypeStruct) else jax.ShapeDtypeStruct(s, F32) for s in shapes],
        in_specs=in_specs,
        out_specs=[vmem()] * len(shapes),
        cost_estimate=pl.CostEstimate(flops=flops, bytes_accessed=1 << 20, transcendentals=0),
    )


VMEM_LIMIT = 12 << 20


def per_device(increment, model_weight, winds, reaction, obs_cells, obs_weight):
    inc = increment[0]
    wgt = model_weight[0]
    wind = winds[0]
    mix = reaction.transpose(1, 0, 2)
    fields, rows, cols = inc.shape
    nobs = obs_cells.shape[-1]
    cells = obs_cells.reshape(1, nobs)
    scale = obs_weight.reshape(fields, 1, nobs)
    tall = rows + 2 * HALO
    swap2 = lax.axis_size("win") == 2
    copies = 1 if swap2 else 2
    lay = Layout(fields, copies)
    tile = (fields, rows, cols)
    packet = (lay.packet, rows, cols)
    strip_rows = 8 * (-(-4 * lay.packet // 8) * (cols // LANES) + lay.groups(rows // 8, 4 * lay.packet)[1])
    row_msg = (8 * lay.row_blocks, cols)
    col_msg = (8 * lay.groups(tall // 8, lay.used)[1], LANES)

    inc, wgt, wind, cells, scale, mixrows, *rest = call(
        functools.partial(load_kernel, swap2, copies),
        [hbm()] * 6,
        [tile, tile, wind.shape, jax.ShapeDtypeStruct(cells.shape, jnp.int32), scale.shape, (16, cols)]
        + [packet] * copies
        + [(strip_rows, LANES)] * copies,
        1 << 20,
        [pltpu.SMEM(mix.shape, F32), pltpu.SemaphoreType.DMA((10,))],
    )(far(inc), far(wgt), far(wind), far(mix), far(cells), far(scale))
    bulk, strips = rest[:copies], rest[copies:]
    strips = window_swap(strips[0], strips[-1])[:copies]
    bulk = window_swap(bulk[0], bulk[-1])[:copies]

    hmap, row_first, row_last, col_low, col_high = call(
        functools.partial(own_kernel, copies),
        [vmem()] * 4,
        [tile, row_msg, row_msg, (rows, LANES), (rows, LANES)],
        1 << 29,
    )(inc, wind, cells, scale)

    row_even, row_odd, col_low, col_high = call(
        functools.partial(join_kernel, fields, copies),
        [vmem()] * (4 + copies),
        [row_msg, row_msg, (rows, LANES), (rows, LANES)],
        1 << 16,
    )(row_first, row_last, col_low, col_high, *strips)
    got_even, got_odd = neighbour_swap(row_even, row_odd, "lat")

    halo_rows, msg_even, msg_odd = call(
        functools.partial(rows_kernel, fields, copies), [vmem()] * 4, [(lay.count, 8, cols), col_msg, col_msg], 1 << 16
    )(got_even, got_odd, col_low, col_high)
    got_even, got_odd = neighbour_swap(msg_even, msg_odd, "lon")

    part, edges, wgt_edges, prior_rows = call(
        functools.partial(inner_kernel, copies),
        [vmem()] * (6 + copies),
        [tile, (lay.count, tall, LANES), (fields, rows, LANES), (16, LANES)],
        1 << 29,
    )(inc, wgt, wind, hmap, mixrows, halo_rows, *bulk)

    (out,) = call(
        functools.partial(edge_kernel, copies), [vmem()] * 7, [tile], 1 << 25
    )(got_even, got_odd, edges, wgt_edges, part, mixrows, prior_rows)
    return out[None]


def solution(mesh):
    in_specs = (
        P("win", None, "lat", "lon"),
        P("win", None, "lat", "lon"),
        P("win", None, "lat", "lon"),
        P("win", None, None),
        P("win", "lat", "lon", None),
        P("win", None, "lat", "lon", None),
    )
    out_specs = P("win", None, "lat", "lon")

    return jax.shard_map(per_device, mesh=mesh, in_specs=in_specs, out_specs=out_specs, check_vma=False)
```

```python
import functools

import jax
import jax.numpy as jnp
from jax import lax
from jax.experimental import pallas as pl
from jax.experimental.pallas import tpu as pltpu
from jax.sharding import PartitionSpec as P


DIFFUSION = 0.15
HALO = 4
RIM = 2
LANES = 128
F32 = jnp.float32


def even_pairs(n):
    return [(i, i ^ 1) for i in range(n)]


def odd_pairs(n):
    return [(i, (i + 1 if i % 2 else i - 1) % n) for i in range(n)]


def ring(n, step):
    return [(i, (i + step) % n) for i in range(n)]


def neighbour_swap(even_msg, odd_msg, axis):
    n = lax.axis_size(axis)
    from_even = lax.ppermute(even_msg, axis, even_pairs(n))
    from_odd = lax.ppermute(odd_msg, axis, odd_pairs(n))
    return from_even, from_odd


def window_swap(down, up):
    n = lax.axis_size("win")
    if n == 2:
        got = lax.ppermute(down, "win", even_pairs(n))
        return got, got
    return lax.ppermute(down, "win", ring(n, -1)), lax.ppermute(up, "win", ring(n, 1))


def sub_iota(shape):
    return lax.broadcasted_iota(jnp.int32, shape, len(shape) - 2)


def lane_iota(shape):
    return lax.broadcasted_iota(jnp.int32, shape, len(shape) - 1)


def turn(x, shift, axis):
    shift %= x.shape[axis]
    return pltpu.roll(x, shift, axis) if shift else x


def axis_even(axis):
    return lax.axis_index(axis) % 2 == 0


def line_planes(lay):
    fields = lay.fields
    lines = [range(fields), range(fields, fields + 2), range(fields + 2, lay.own)]
    for k in range(lay.copies):
        base = lay.own + k * lay.packet
        lines += [range(base, base + fields), range(base + fields, base + lay.packet)]
    return lines


class Layout:
    def __init__(self, fields, copies):
        self.fields, self.copies = fields, copies
        self.own = 2 + 2 * fields
        self.packet = 2 * fields
        self.depths = [HALO] * (fields + 2) + [RIM] * (fields + self.packet * copies)
        self.count = len(self.depths)
        self.starts = [sum(self.depths[:j]) for j in range(self.count)]
        self.used = sum(self.depths)
        self.row_blocks = -(-self.used // 8)
        spots = [0, HALO] + [2 * HALO + RIM * k for k in range(1 + 2 * copies)]
        self.group = 2 * HALO + RIM * (1 + 2 * copies)
        self.wide = self.group * fields
        self.lanes = [0] * self.count
        for spot, members in zip(spots, line_planes(self)):
            for f, j in enumerate(members):
                self.lanes[j] = self.group * f + spot
        self.spots = spots

    def groups(self, blocks, width):
        per = -(-blocks // (LANES // width))
        return -(-blocks // per), per


def squeeze_lanes(wide, width, lay):
    blocks = wide.shape[0] // 8
    groups, per = lay.groups(blocks, width)
    lane = lane_iota((8, LANES))
    out = []
    for i in range(per):
        block = None
        for g in range(groups):
            if g * per + i < blocks:
                part = turn(wide[8 * (g * per + i) : 8 * (g * per + i) + 8], width * g, 1)
                block = part if block is None else jnp.where(lane >= width * g, part, block)
        out.append(block)
    return out


def spread_lanes(tight, blocks, width, lay):
    _, per = lay.groups(blocks, width)
    out = []
    for b in range(blocks):
        g, i = b // per, b % per
        out.append(turn(tight[i], -width * g, 1))
    return jnp.concatenate(out, axis=0)


def pack_rows(pieces, blocks):
    out = [None] * blocks
    for block, first, at, depth in pieces:
        b, s = at // 8, at % 8
        moved = turn(block, s - first, 0)
        sub = sub_iota(moved.shape)
        out[b] = moved if out[b] is None else jnp.where((sub >= s) & (sub < s + depth), moved, out[b])
    return out


def pack_lanes(pieces, out=None):
    for block, first, at, depth in pieces:
        moved = turn(block, at - first, 1)
        lane = lane_iota(moved.shape)
        out = moved if out is None else jnp.where((lane >= at) & (lane < at + depth), moved, out)
    return out


def load_kernel(swap2, copies, *refs):
    inc_far, wgt_far, wind_far, mix_far, mixrows = refs[:5]
    bulk = refs[5 : 5 + copies]
    strips = refs[5 + copies : 5 + 2 * copies]
    mix, sems = refs[5 + 2 * copies :]
    packet, rows, cols = bulk[0].shape
    fields = packet // 2
    lay = Layout(fields, copies)
    sends_up = lax.axis_index("win") == 0
    moves = [
        pltpu.make_async_copy(inc_far, ref.at[pl.ds(0, fields)], sems.at[i]) for i, ref in enumerate(bulk)
    ]
    moves.append(pltpu.make_async_copy(mix_far, mix, sems.at[2]))
    to_down = pltpu.make_async_copy(wgt_far, bulk[0].at[pl.ds(fields, fields)], sems.at[3])
    to_up = pltpu.make_async_copy(wind_far, bulk[-1].at[pl.ds(fields, 2)], sems.at[4])

    def on(condition, action):
        if swap2:
            pl.when(condition)(action)
        else:
            action()

    for move in moves:
        move.start()
    on(sends_up, lambda: to_up.start())
    on(jnp.logical_not(sends_up), lambda: to_down.start())
    for move in moves:
        move.wait()
    which = sub_iota(mixrows.shape)
    spread = jnp.zeros(mixrows.shape, F32)
    for f in range(fields):
        for g in range(fields):
            spread = jnp.where(which == f * fields + g, mix[f, 0, g], spread)
    mixrows[...] = spread

    def fill_up():
        to_up.wait()
        used = mixrows.shape[0]
        bulk[-1][packet - 1, pl.ds(0, used), :] = spread[:, :cols]
        bulk[-1][packet - 1, pl.ds(used, rows - used), :] = jnp.zeros((rows - used, cols), F32)

    on(sends_up, fill_up)
    on(jnp.logical_not(sends_up), lambda: to_down.wait())

    for k, ref in enumerate(strips):
        planes = [bulk[k][j] for j in range(packet)]
        pieces = []
        for j, x in enumerate(planes):
            pieces.append((x[:8], 0, 4 * j, RIM))
            pieces.append((x[-8:], 8 - RIM, 4 * j + 2, RIM))
        blocks = pack_rows(pieces, -(-4 * lay.packet // 8))
        halves = cols // LANES
        for m, block in enumerate(blocks):
            for h in range(halves):
                ref[pl.ds(8 * (m * halves + h), 8), :] = block[:, h * LANES : (h + 1) * LANES]
        pieces = []
        for j, x in enumerate(planes):
            pieces.append((x[:, :LANES], 0, 4 * j, RIM))
            pieces.append((x[:, -LANES:], LANES - RIM, 4 * j + 2, RIM))
        for m, block in enumerate(squeeze_lanes(pack_lanes(pieces), 4 * lay.packet, lay)):
            ref[pl.ds(8 * (len(blocks) * halves + m), 8), :] = block


def own_kernel(copies, bulk, wind_far, wgt_far, cells_far, scale_far, *refs):
    wind, wgt, hmap, row_first, row_last, col_low, col_high, cells, scale, sems = refs
    moves = [
        pltpu.make_async_copy(src, dst, sems.at[i])
        for i, (src, dst) in enumerate(
            [(cells_far, cells), (scale_far, scale), (wind_far, wind), (wgt_far, wgt)]
        )
    ]
    for move in moves:
        move.start()
    packet, rows, cols = bulk.shape
    fields = packet // 2
    inc = bulk
    lay = Layout(fields, copies)
    moves[0].wait()
    moves[1].wait()
    nobs = cells.shape[-1]
    index = cells[...]
    row_hot = sub_iota((rows, nobs)) == index // cols
    col_hot = (sub_iota((cols, nobs)) == index % cols).astype(F32).astype(jnp.bfloat16)
    terms = []
    for f in range(fields):
        rest = scale[f]
        for _ in range(3):
            part = rest.astype(jnp.bfloat16)
            rest = rest - part.astype(F32)
            terms.append(jnp.where(row_hot, part.astype(F32), 0.0).astype(jnp.bfloat16))
    sums = lax.dot_general(
        jnp.concatenate(terms, axis=0), col_hot, (((1,), (1,)), ((), ())), preferred_element_type=F32
    )
    moves[2].wait()
    planes = [inc[f] for f in range(fields)] + [wind[0], wind[1]]
    for f in range(fields):
        base = 3 * f * rows
        value = sums[base : base + rows] + (
            sums[base + rows : base + 2 * rows] + sums[base + 2 * rows : base + 3 * rows]
        )
        hmap[f] = value
        planes.append(value)
    where = list(zip(planes, lay.starts, lay.depths))
    first = pack_rows([(x[:8], 0, at, d) for x, at, d in where], lay.row_blocks)
    last = pack_rows([(x[-8:], 8 - d, at, d) for x, at, d in where], lay.row_blocks)
    for m in range(lay.row_blocks):
        blank = jnp.zeros((8, cols), F32)
        row_first[pl.ds(8 * m, 8), :] = blank if first[m] is None else first[m]
        row_last[pl.ds(8 * m, 8), :] = blank if last[m] is None else last[m]
    where = list(zip(planes, lay.lanes, lay.depths))
    col_low[...] = pack_lanes([(x[:, :LANES], 0, at, d) for x, at, d in where])
    col_high[...] = pack_lanes([(x[:, -LANES:], LANES - d, at, d) for x, at, d in where])
    moves[3].wait()


def join_kernel(fields, copies, *refs):
    row_first, row_last, col_low, col_high = refs[:4]
    strips = refs[4 : 4 + copies]
    row_even, row_odd, low_out, high_out = refs[4 + copies :]
    lay = Layout(fields, copies)
    rows, cols = col_low.shape[0], row_first.shape[1]
    halves = cols // LANES
    strip_blocks = -(-4 * lay.packet // 8)
    first_pieces, last_pieces, low_pieces, high_pieces = [], [], [], []
    for k, ref in enumerate(strips):
        blocks = [
            jnp.concatenate([ref[pl.ds(8 * (m * halves + h), 8), :] for h in range(halves)], axis=1)
            for m in range(strip_blocks)
        ]
        _, per = lay.groups(rows // 8, 4 * lay.packet)
        base = 8 * strip_blocks * halves
        tight = [ref[pl.ds(base + 8 * i, 8), :] for i in range(per)]
        wide = spread_lanes(tight, rows // 8, 4 * lay.packet, lay)
        for j in range(lay.packet):
            at = lay.starts[lay.own + k * lay.packet + j]
            first_pieces.append((blocks[4 * j // 8], 4 * j % 8, at, RIM))
            last_pieces.append((blocks[4 * j // 8], 4 * j % 8 + 2, at, RIM))
            at = lay.lanes[lay.own + k * lay.packet + j]
            low_pieces.append((wide, 4 * j, at, RIM))
            high_pieces.append((wide, 4 * j + 2, at, RIM))
    is_even = axis_even("lat")
    own_used = lay.starts[lay.own]
    first = pack_rows(first_pieces, lay.row_blocks)
    last = pack_rows(last_pieces, lay.row_blocks)
    for m in range(lay.row_blocks):
        a, b = row_first[pl.ds(8 * m, 8), :], row_last[pl.ds(8 * m, 8), :]
        if first[m] is not None:
            other = sub_iota(a.shape) + 8 * m >= own_used
            a, b = jnp.where(other, first[m], a), jnp.where(other, last[m], b)
        row_even[pl.ds(8 * m, 8), :] = jnp.where(is_even, b, a)
        row_odd[pl.ds(8 * m, 8), :] = jnp.where(is_even, a, b)
    low_out[...] = pack_lanes(low_pieces, col_low[...])
    high_out[...] = pack_lanes(high_pieces, col_high[...])


def lat_inside(width):
    here = lax.axis_index("lat")
    upper = sub_iota((8, width)) < HALO
    from_high = (here < lax.axis_size("lat") - 1).astype(jnp.int32)
    from_low = (here > 0).astype(jnp.int32)
    return jnp.where(upper, from_high, from_low) > 0


def rows_kernel(fields, copies, got_even, got_odd, col_low, col_high, halo_rows, msg_even, msg_odd):
    lay = Layout(fields, copies)
    cols = got_even.shape[-1]
    is_even = axis_even("lat")
    inside = lat_inside(cols)
    sub = sub_iota((8, cols))
    high, low = [], []
    for m in range(lay.row_blocks):
        a = got_even[pl.ds(8 * m, 8), :]
        b = got_odd[pl.ds(8 * m, 8), :]
        high.append(jnp.where(is_even, a, b))
        low.append(jnp.where(is_even, b, a))
    blocks = []
    for j, (at, d) in enumerate(zip(lay.starts, lay.depths)):
        above = turn(high[at // 8], -(at % 8), 0)
        below = turn(low[at // 8], 8 - d - at % 8, 0)
        block = jnp.where(sub < d, above, jnp.where(sub >= 8 - d, below, 0.0))
        block = jnp.where(inside, block, 0.0)
        halo_rows[j] = block
        blocks.append(block)
    where = list(zip(blocks, lay.lanes, lay.depths))
    low_tail = pack_lanes([(x[:, :LANES], 0, at, d) for x, at, d in where])
    high_tail = pack_lanes([(x[:, -LANES:], LANES - d, at, d) for x, at, d in where])
    low_all = squeeze_lanes(jnp.concatenate([col_low[...], low_tail], axis=0), lay.wide, lay)
    high_all = squeeze_lanes(jnp.concatenate([col_high[...], high_tail], axis=0), lay.wide, lay)
    lon_even = axis_even("lon")
    for m, (a, b) in enumerate(zip(low_all, high_all)):
        msg_even[pl.ds(8 * m, 8), :] = jnp.where(lon_even, b, a)
        msg_odd[pl.ds(8 * m, 8), :] = jnp.where(lon_even, a, b)


def row_mask(rows, width):
    inside = lat_inside(width)

    def clear(field):
        return jnp.concatenate([field[:rows], jnp.where(inside, field[rows:], 0.0)], axis=0)

    return clear


def north(x):
    return pltpu.roll(x, x.shape[0] - 1, 0)


def south(x):
    return pltpu.roll(x, 1, 0)


def east_of(x):
    return pltpu.roll(x, x.shape[1] - 1, 1)


def west_of(x):
    return pltpu.roll(x, 1, 1)


def mixing(spread, fields):
    return lambda f, g: spread[f * fields + g : f * fields + g + 1]


def blend(mix, field, f):
    total = None
    for g in range(len(field)):
        factor = mix(f, g)
        if f == g:
            factor = factor + (1.0 - 4.0 * DIFFUSION)
        term = factor * field[g]
        total = term if total is None else total + term
    return total


def tangent(field, u, v, mix):
    kn, ks, ke, kw = DIFFUSION - v, DIFFUSION + v, DIFFUSION - u, DIFFUSION + u
    return [
        blend(mix, field, f)
        + (kn * north(x) + ks * south(x))
        + (ke * east_of(x) + kw * west_of(x))
        for f, x in enumerate(field)
    ]


def adjoint(field, u, v, mix):
    kn, ks, ke, kw = DIFFUSION + v, DIFFUSION - v, DIFFUSION + u, DIFFUSION - u
    return [
        blend(lambda a, b: mix(b, a), field, f)
        + (north(kn * x) + south(ks * x))
        + (east_of(ke * x) + west_of(kw * x))
        for f, x in enumerate(field)
    ]


def product(own, above, below, wgt, mix, prior_mix, fields, rows):
    clear = row_mask(rows, own[0].shape[1])
    here = lax.axis_index("win")
    has_later = here < lax.axis_size("win") - 1
    has_earlier = here > 0
    inc, wind, hmap = own[:fields], own[fields : fields + 2], own[fields + 2 :]
    fwd = [clear(x) for x in tangent(inc, *wind, mix)]
    fwd = tangent(fwd, *wind, mix)
    source = []
    for f in range(fields):
        later = above[fields + f] * (above[f] - fwd[f])
        source.append(clear(hmap[f] * fwd[f] - jnp.where(has_later, later, 0.0)))
    back = [clear(x) for x in adjoint(source, *wind, mix)]
    back = adjoint(back, *wind, mix)
    prior_wind = below[fields : fields + 2]
    prior = [clear(x) for x in tangent(below[:fields], *prior_wind, prior_mix)]
    prior = tangent(prior, *prior_wind, prior_mix)
    return [
        wgt[f] * (inc[f][:rows] - jnp.where(has_earlier, prior[f][:rows], 0.0)) + back[f][:rows]
        for f in range(fields)
    ]


SIDE = LANES // 2


def edge_line(tiles, group):
    out = None
    lane = None
    for f, x in enumerate(tiles):
        base = group * f
        low = turn(x[:, :LANES], base + HALO, 1)
        high = turn(x[:, -LANES:], SIDE + base + group - HALO, 1)
        if lane is None:
            lane = lane_iota(low.shape)
        both = jnp.where(lane < SIDE, low, high)
        out = both if out is None else jnp.where(lane % SIDE >= base, both, out)
    return out


def line_offsets(fields):
    return [o for o in range(1 - fields, fields)]


def line_factors(mix, fields, group):
    lane = lane_iota((1, LANES)) % SIDE
    rows = []
    for o in line_offsets(fields):
        row = jnp.zeros((1, LANES), F32)
        for f in range(fields):
            if 0 <= f - o < fields:
                factor = mix(f, f - o)[:, :LANES]
                if o == 0:
                    factor = factor + (1.0 - 4.0 * DIFFUSION)
                row = jnp.where((lane >= group * f) & (lane < group * (f + 1)), factor, row)
        rows.append(row)
    return rows


def line_blend(factors, x, fields, group):
    total = None
    for o, factor in zip(line_offsets(fields), factors):
        term = factor * turn(x, group * o, 1)
        total = term if total is None else total + term
    return total


def line_wind(pair, group):
    lane = lane_iota(pair.shape) % SIDE
    up, down = turn(pair, group, 1), turn(pair, -group, 1)
    far_up = turn(pair, 2 * group, 1)
    u = jnp.where(lane < group, pair, jnp.where(lane < 2 * group, up, far_up))
    v = jnp.where(lane < group, down, jnp.where(lane < 2 * group, pair, up))
    return u, v


def line_tangent(x, u, v, factors, fields, group):
    kn, ks, ke, kw = DIFFUSION - v, DIFFUSION + v, DIFFUSION - u, DIFFUSION + u
    return (
        line_blend(factors, x, fields, group)
        + (kn * north(x) + ks * south(x))
        + (ke * east_of(x) + kw * west_of(x))
    )


def line_adjoint(x, u, v, factors, fields, group):
    kn, ks, ke, kw = DIFFUSION + v, DIFFUSION - v, DIFFUSION + u, DIFFUSION - u
    return (
        line_blend(factors, x, fields, group)
        + (north(kn * x) + south(ks * x))
        + (east_of(ke * x) + west_of(kw * x))
    )


def inner_kernel(copies, inc, wgt, wind, hmap, mixrows, halo_rows, *refs):
    bulk = refs[:copies]
    part, edges, wgt_edges, factors = refs[copies:]
    fields, rows, cols = wgt.shape
    lay = Layout(fields, copies)
    tiles = [inc[f] for f in range(fields)] + [wind[0], wind[1]] + [hmap[f] for f in range(fields)]
    for ref in bulk:
        tiles += [ref[j] for j in range(lay.packet)]
    planes = [jnp.concatenate([tile, halo_rows[j]], axis=0) for j, tile in enumerate(tiles)]
    for k, members in enumerate(line_planes(lay)):
        edges[k] = edge_line([planes[j] for j in members], lay.group)
    wgt_edges[...] = edge_line([wgt[f] for f in range(fields)], lay.group)
    above = planes[lay.own : lay.own + lay.packet]
    below = planes[-lay.packet :]
    spread = bulk[-1][2 * fields - 1, :16]
    mix, prior_mix = mixing(mixrows[:, :cols], fields), mixing(spread, fields)
    lists = []
    for maker in (mix, lambda f, g: mix(g, f), prior_mix):
        lists += line_factors(maker, fields, lay.group)
    for i, row in enumerate(lists):
        factors[i : i + 1] = row
    result = product(planes[: lay.own], above, below, wgt, mix, prior_mix, fields, rows)
    for f in range(fields):
        part[f] = result[f]


def edge_kernel(copies, got_even, got_odd, edges, wgt_edges, factors, part, out):
    fields, rows, cols = part.shape
    lay = Layout(fields, copies)
    blocks = rows // 8 + 1
    group = lay.group
    _, per = lay.groups(blocks, lay.wide)
    lon_even = axis_even("lon")
    even = [got_even[pl.ds(8 * i, 8), :] for i in range(per)]
    odd = [got_odd[pl.ds(8 * i, 8), :] for i in range(per)]
    east = spread_lanes([jnp.where(lon_even, a, b) for a, b in zip(even, odd)], blocks, lay.wide, lay)
    west = spread_lanes([jnp.where(lon_even, b, a) for a, b in zip(even, odd)], blocks, lay.wide, lay)
    lane = lane_iota(east.shape)
    within = lane % SIDE % group
    on_west = (lane < SIDE) & (within < HALO)
    on_east = (lane >= SIDE) & (within >= group - HALO)
    lines = []
    for k, (spot, members) in enumerate(zip(lay.spots, line_planes(lay))):
        depth = lay.depths[members[0]]
        left = turn(west, HALO - depth - spot, 1)
        right = turn(east, SIDE + group - HALO - spot, 1)
        lines.append(jnp.where(on_west, left, jnp.where(on_east, right, edges[k])))
    clear = row_mask(rows, LANES)
    here = lax.axis_index("win")
    has_later = here < lax.axis_size("win") - 1
    has_earlier = here > 0
    count = 2 * fields - 1
    every = factors[...]
    mix, mix_back, mix_prior = [
        [every[g * count + i : g * count + i + 1] for i in range(count)] for g in range(3)
    ]
    inc, hmap = lines[0], lines[2]
    u, v = line_wind(lines[1], group)
    fwd = clear(line_tangent(inc, u, v, mix, fields, group))
    fwd = line_tangent(fwd, u, v, mix, fields, group)
    later = lines[4] * (lines[3] - fwd)
    back = clear(hmap * fwd - jnp.where(has_later, later, 0.0))
    back = clear(line_adjoint(back, u, v, mix_back, fields, group))
    back = line_adjoint(back, u, v, mix_back, fields, group)
    u, v = line_wind(lines[-1], group)
    prior = clear(line_tangent(lines[-2], u, v, mix_prior, fields, group))
    prior = line_tangent(prior, u, v, mix_prior, fields, group)[:rows]
    result = wgt_edges[...] * (inc[:rows] - jnp.where(has_earlier, prior, 0.0)) + back[:rows]
    lane = lane_iota((rows, LANES))
    for f in range(fields):
        low = turn(result, -(group * f + HALO), 1)
        high = turn(result, LANES - HALO - (SIDE + group * f + group - 2 * HALO), 1)
        whole = part[f]
        if cols == LANES:
            out[f] = jnp.where(lane < HALO, low, jnp.where(lane >= LANES - HALO, high, whole))
        else:
            out[f, :, pl.ds(0, LANES)] = jnp.where(lane < HALO, low, whole[:, :LANES])
            for h in range(1, cols // LANES - 1):
                out[f, :, pl.ds(h * LANES, LANES)] = whole[:, h * LANES : (h + 1) * LANES]
            out[f, :, pl.ds(cols - LANES, LANES)] = jnp.where(lane >= LANES - HALO, high, whole[:, -LANES:])


def vmem():
    return pl.BlockSpec(memory_space=pltpu.VMEM)


def hbm():
    return pl.BlockSpec(memory_space=pltpu.HBM)


def far(array):
    return pltpu.with_memory_space_constraint(array, pltpu.HBM)


def call(kernel, in_specs, shapes, flops, scratch=()):
    return pl.pallas_call(
        kernel,
        scratch_shapes=scratch,
        compiler_params=pltpu.CompilerParams(vmem_limit_bytes=VMEM_LIMIT),
        out_shape=[s if isinstance(s, jax.ShapeDtypeStruct) else jax.ShapeDtypeStruct(s, F32) for s in shapes],
        in_specs=in_specs,
        out_specs=[vmem()] * len(shapes),
        cost_estimate=pl.CostEstimate(flops=flops, bytes_accessed=1 << 20, transcendentals=0),
    )


VMEM_LIMIT = 12 << 20


def per_device(increment, model_weight, winds, reaction, obs_cells, obs_weight):
    inc = increment[0]
    wgt = model_weight[0]
    wind = winds[0]
    mix = reaction.transpose(1, 0, 2)
    fields, rows, cols = inc.shape
    nobs = obs_cells.shape[-1]
    cells = obs_cells.reshape(1, nobs)
    scale = obs_weight.reshape(fields, 1, nobs)
    tall = rows + 2 * HALO
    swap2 = lax.axis_size("win") == 2
    copies = 1 if swap2 else 2
    lay = Layout(fields, copies)
    tile = (fields, rows, cols)
    packet = (lay.packet, rows, cols)
    strip_rows = 8 * (-(-4 * lay.packet // 8) * (cols // LANES) + lay.groups(rows // 8, 4 * lay.packet)[1])
    row_msg = (8 * lay.row_blocks, cols)
    col_msg = (8 * lay.groups(tall // 8, lay.wide)[1], LANES)

    mixrows, *rest = call(
        functools.partial(load_kernel, swap2, copies),
        [hbm()] * 4,
        [(16, cols)] + [packet] * copies + [(strip_rows, LANES)] * copies,
        1 << 20,
        [pltpu.SMEM(mix.shape, F32), pltpu.SemaphoreType.DMA((5,))],
    )(far(inc), far(wgt), far(wind), far(mix))
    sent, strips = rest[:copies], rest[copies:]
    strips = window_swap(strips[0], strips[-1])[:copies]
    bulk = window_swap(sent[0], sent[-1])[:copies]

    wind_near, wgt_near, hmap, row_first, row_last, col_low, col_high = call(
        functools.partial(own_kernel, copies),
        [vmem()] + [hbm()] * 4,
        [wind.shape, tile, tile, row_msg, row_msg, (rows, LANES), (rows, LANES)],
        1 << 29,
        [pltpu.VMEM(cells.shape, jnp.int32), pltpu.VMEM(scale.shape, F32), pltpu.SemaphoreType.DMA((4,))],
    )(sent[0], far(wind), far(wgt), far(cells), far(scale))

    row_even, row_odd, col_low, col_high = call(
        functools.partial(join_kernel, fields, copies),
        [vmem()] * (4 + copies),
        [row_msg, row_msg, (rows, LANES), (rows, LANES)],
        1 << 16,
    )(row_first, row_last, col_low, col_high, *strips)
    got_even, got_odd = neighbour_swap(row_even, row_odd, "lat")

    halo_rows, msg_even, msg_odd = call(
        functools.partial(rows_kernel, fields, copies), [vmem()] * 4, [(lay.count, 8, cols), col_msg, col_msg], 1 << 16
    )(got_even, got_odd, col_low, col_high)
    got_even, got_odd = neighbour_swap(msg_even, msg_odd, "lon")

    lines = len(line_planes(lay))
    part, edges, wgt_edges, factors = call(
        functools.partial(inner_kernel, copies),
        [vmem()] * (6 + copies),
        [tile, (lines, tall, LANES), (rows, LANES), (8 * -(-3 * (2 * fields - 1) // 8), LANES)],
        1 << 29,
    )(sent[0], wgt_near, wind_near, hmap, mixrows, halo_rows, *bulk)

    (out,) = call(
        functools.partial(edge_kernel, copies), [vmem()] * 6, [tile], 1 << 25
    )(got_even, got_odd, edges, wgt_edges, factors, part)
    return out[None]


def solution(mesh):
    in_specs = (
        P("win", None, "lat", "lon"),
        P("win", None, "lat", "lon"),
        P("win", None, "lat", "lon"),
        P("win", None, None),
        P("win", "lat", "lon", None),
        P("win", None, "lat", "lon", None),
    )
    out_specs = P("win", None, "lat", "lon")

    return jax.shard_map(per_device, mesh=mesh, in_specs=in_specs, out_specs=out_specs, check_vma=False)
```

```python
import functools

import jax
import jax.numpy as jnp
from jax import lax
from jax.experimental import pallas as pl
from jax.experimental.pallas import tpu as pltpu
from jax.sharding import PartitionSpec as P


DIFFUSION = 0.15
HALO = 4
RIM = 2
LANES = 128
F32 = jnp.float32


def even_pairs(n):
    return [(i, i ^ 1) for i in range(n)]


def odd_pairs(n):
    return [(i, (i + 1 if i % 2 else i - 1) % n) for i in range(n)]


def ring(n, step):
    return [(i, (i + step) % n) for i in range(n)]


def neighbour_swap(even_msg, odd_msg, axis):
    n = lax.axis_size(axis)
    from_even = lax.ppermute(even_msg, axis, even_pairs(n))
    from_odd = lax.ppermute(odd_msg, axis, odd_pairs(n))
    return from_even, from_odd


def window_swap(down, up):
    n = lax.axis_size("win")
    if n == 2:
        got = lax.ppermute(down, "win", even_pairs(n))
        return got, got
    return lax.ppermute(down, "win", ring(n, -1)), lax.ppermute(up, "win", ring(n, 1))


def sub_iota(shape):
    return lax.broadcasted_iota(jnp.int32, shape, len(shape) - 2)


def lane_iota(shape):
    return lax.broadcasted_iota(jnp.int32, shape, len(shape) - 1)


def turn(x, shift, axis):
    shift %= x.shape[axis]
    return pltpu.roll(x, shift, axis) if shift else x


def axis_even(axis):
    return lax.axis_index(axis) % 2 == 0


def line_planes(lay):
    fields = lay.fields
    lines = [range(fields), range(fields, fields + 2), range(fields + 2, lay.own)]
    for k in range(lay.copies):
        base = lay.own + k * lay.packet
        lines += [range(base, base + fields), range(base + fields, base + lay.packet)]
    return lines


class Layout:
    def __init__(self, fields, copies):
        self.fields, self.copies = fields, copies
        self.own = 2 + 2 * fields
        self.packet = 2 * fields
        self.depths = [HALO] * (fields + 2) + [RIM] * (fields + self.packet * copies)
        self.count = len(self.depths)
        self.starts = [sum(self.depths[:j]) for j in range(self.count)]
        self.used = sum(self.depths)
        self.row_blocks = -(-self.used // 8)
        spots = [0, HALO] + [2 * HALO + RIM * k for k in range(1 + 2 * copies)]
        self.group = 2 * HALO + RIM * (1 + 2 * copies)
        self.wide = self.group * fields
        self.lanes = [0] * self.count
        for spot, members in zip(spots, line_planes(self)):
            for f, j in enumerate(members):
                self.lanes[j] = self.group * f + spot
        self.spots = spots

    def groups(self, blocks, width):
        per = -(-blocks // (LANES // width))
        return -(-blocks // per), per


def squeeze_lanes(wide, width, lay):
    blocks = wide.shape[0] // 8
    groups, per = lay.groups(blocks, width)
    lane = lane_iota((8, LANES))
    out = []
    for i in range(per):
        block = None
        for g in range(groups):
            if g * per + i < blocks:
                part = turn(wide[8 * (g * per + i) : 8 * (g * per + i) + 8], width * g, 1)
                block = part if block is None else jnp.where(lane >= width * g, part, block)
        out.append(block)
    return out


def spread_lanes(tight, blocks, width, lay):
    _, per = lay.groups(blocks, width)
    out = []
    for b in range(blocks):
        g, i = b // per, b % per
        out.append(turn(tight[i], -width * g, 1))
    return jnp.concatenate(out, axis=0)


def pack_rows(pieces, blocks):
    out = [None] * blocks
    for block, first, at, depth in pieces:
        b, s = at // 8, at % 8
        moved = turn(block, s - first, 0)
        sub = sub_iota(moved.shape)
        out[b] = moved if out[b] is None else jnp.where((sub >= s) & (sub < s + depth), moved, out[b])
    return out


def pack_lanes(pieces, out=None):
    for block, first, at, depth in pieces:
        moved = turn(block, at - first, 1)
        lane = lane_iota(moved.shape)
        out = moved if out is None else jnp.where((lane >= at) & (lane < at + depth), moved, out)
    return out


def load_kernel(swap2, copies, *refs):
    inc_far, wgt_far, wind_far, mix_far, mixrows = refs[:5]
    bulk = refs[5 : 5 + copies]
    strips = refs[5 + copies : 5 + 2 * copies]
    mix, sems = refs[5 + 2 * copies :]
    packet, rows, cols = bulk[0].shape
    fields = packet // 2
    lay = Layout(fields, copies)
    sends_up = lax.axis_index("win") == 0
    moves = [
        pltpu.make_async_copy(inc_far, ref.at[pl.ds(0, fields)], sems.at[i]) for i, ref in enumerate(bulk)
    ]
    moves.append(pltpu.make_async_copy(mix_far, mix, sems.at[2]))
    to_down = pltpu.make_async_copy(wgt_far, bulk[0].at[pl.ds(fields, fields)], sems.at[3])
    to_up = pltpu.make_async_copy(wind_far, bulk[-1].at[pl.ds(fields, 2)], sems.at[4])

    def on(condition, action):
        if swap2:
            pl.when(condition)(action)
        else:
            action()

    for move in moves:
        move.start()
    on(sends_up, lambda: to_up.start())
    on(jnp.logical_not(sends_up), lambda: to_down.start())
    for move in moves:
        move.wait()
    which = sub_iota(mixrows.shape)
    spread = jnp.zeros(mixrows.shape, F32)
    for f in range(fields):
        for g in range(fields):
            spread = jnp.where(which == f * fields + g, mix[f, 0, g], spread)
    mixrows[...] = spread

    def fill_up():
        to_up.wait()
        used = mixrows.shape[0]
        bulk[-1][packet - 1, pl.ds(0, used), :] = spread[:, :cols]
        bulk[-1][packet - 1, pl.ds(used, rows - used), :] = jnp.zeros((rows - used, cols), F32)

    on(sends_up, fill_up)
    on(jnp.logical_not(sends_up), lambda: to_down.wait())

    for k, ref in enumerate(strips):
        planes = [bulk[k][j] for j in range(packet)]
        pieces = []
        for j, x in enumerate(planes):
            pieces.append((x[:8], 0, 4 * j, RIM))
            pieces.append((x[-8:], 8 - RIM, 4 * j + 2, RIM))
        blocks = pack_rows(pieces, -(-4 * lay.packet // 8))
        halves = cols // LANES
        for m, block in enumerate(blocks):
            for h in range(halves):
                ref[pl.ds(8 * (m * halves + h), 8), :] = block[:, h * LANES : (h + 1) * LANES]
        pieces = []
        for j, x in enumerate(planes):
            pieces.append((x[:, :LANES], 0, 4 * j, RIM))
            pieces.append((x[:, -LANES:], LANES - RIM, 4 * j + 2, RIM))
        for m, block in enumerate(squeeze_lanes(pack_lanes(pieces), 4 * lay.packet, lay)):
            ref[pl.ds(8 * (len(blocks) * halves + m), 8), :] = block


def own_kernel(copies, bulk, wind_far, wgt_far, cells_far, scale_far, *refs):
    wind, wgt, hmap, row_first, row_last, col_low, col_high, cells, scale, sems = refs
    moves = [
        pltpu.make_async_copy(src, dst, sems.at[i])
        for i, (src, dst) in enumerate(
            [(cells_far, cells), (scale_far, scale), (wind_far, wind), (wgt_far, wgt)]
        )
    ]
    for move in moves:
        move.start()
    packet, rows, cols = bulk.shape
    fields = packet // 2
    inc = bulk
    lay = Layout(fields, copies)
    moves[0].wait()
    moves[1].wait()
    nobs = cells.shape[-1]
    index = cells[...]
    row_hot = sub_iota((rows, nobs)) == index // cols
    col_hot = (sub_iota((cols, nobs)) == index % cols).astype(F32).astype(jnp.bfloat16)
    terms = []
    for f in range(fields):
        rest = scale[f]
        for _ in range(3):
            part = rest.astype(jnp.bfloat16)
            rest = rest - part.astype(F32)
            terms.append(jnp.where(row_hot, part.astype(F32), 0.0).astype(jnp.bfloat16))
    sums = lax.dot_general(
        jnp.concatenate(terms, axis=0), col_hot, (((1,), (1,)), ((), ())), preferred_element_type=F32
    )
    moves[2].wait()
    planes = [inc[f] for f in range(fields)] + [wind[0], wind[1]]
    for f in range(fields):
        base = 3 * f * rows
        value = sums[base : base + rows] + (
            sums[base + rows : base + 2 * rows] + sums[base + 2 * rows : base + 3 * rows]
        )
        hmap[f] = value
        planes.append(value)
    where = list(zip(planes, lay.starts, lay.depths))
    first = pack_rows([(x[:8], 0, at, d) for x, at, d in where], lay.row_blocks)
    last = pack_rows([(x[-8:], 8 - d, at, d) for x, at, d in where], lay.row_blocks)
    for m in range(lay.row_blocks):
        blank = jnp.zeros((8, cols), F32)
        row_first[pl.ds(8 * m, 8), :] = blank if first[m] is None else first[m]
        row_last[pl.ds(8 * m, 8), :] = blank if last[m] is None else last[m]
    where = list(zip(planes, lay.lanes, lay.depths))
    col_low[...] = pack_lanes([(x[:, :LANES], 0, at, d) for x, at, d in where])
    col_high[...] = pack_lanes([(x[:, -LANES:], LANES - d, at, d) for x, at, d in where])
    moves[3].wait()


def join_kernel(fields, copies, *refs):
    row_first, row_last, col_low, col_high = refs[:4]
    strips = refs[4 : 4 + copies]
    row_even, row_odd, low_out, high_out = refs[4 + copies :]
    lay = Layout(fields, copies)
    rows, cols = col_low.shape[0], row_first.shape[1]
    halves = cols // LANES
    strip_blocks = -(-4 * lay.packet // 8)
    first_pieces, last_pieces, low_pieces, high_pieces = [], [], [], []
    for k, ref in enumerate(strips):
        blocks = [
            jnp.concatenate([ref[pl.ds(8 * (m * halves + h), 8), :] for h in range(halves)], axis=1)
            for m in range(strip_blocks)
        ]
        _, per = lay.groups(rows // 8, 4 * lay.packet)
        base = 8 * strip_blocks * halves
        tight = [ref[pl.ds(base + 8 * i, 8), :] for i in range(per)]
        wide = spread_lanes(tight, rows // 8, 4 * lay.packet, lay)
        for j in range(lay.packet):
            at = lay.starts[lay.own + k * lay.packet + j]
            first_pieces.append((blocks[4 * j // 8], 4 * j % 8, at, RIM))
            last_pieces.append((blocks[4 * j // 8], 4 * j % 8 + 2, at, RIM))
            at = lay.lanes[lay.own + k * lay.packet + j]
            low_pieces.append((wide, 4 * j, at, RIM))
            high_pieces.append((wide, 4 * j + 2, at, RIM))
    is_even = axis_even("lat")
    own_used = lay.starts[lay.own]
    first = pack_rows(first_pieces, lay.row_blocks)
    last = pack_rows(last_pieces, lay.row_blocks)
    for m in range(lay.row_blocks):
        a, b = row_first[pl.ds(8 * m, 8), :], row_last[pl.ds(8 * m, 8), :]
        if first[m] is not None:
            other = sub_iota(a.shape) + 8 * m >= own_used
            a, b = jnp.where(other, first[m], a), jnp.where(other, last[m], b)
        row_even[pl.ds(8 * m, 8), :] = jnp.where(is_even, b, a)
        row_odd[pl.ds(8 * m, 8), :] = jnp.where(is_even, a, b)
    low_out[...] = pack_lanes(low_pieces, col_low[...])
    high_out[...] = pack_lanes(high_pieces, col_high[...])


def lat_inside(width):
    here = lax.axis_index("lat")
    upper = sub_iota((8, width)) < HALO
    from_high = (here < lax.axis_size("lat") - 1).astype(jnp.int32)
    from_low = (here > 0).astype(jnp.int32)
    return jnp.where(upper, from_high, from_low) > 0


def rows_kernel(fields, copies, got_even, got_odd, col_low, col_high, halo_rows, msg_even, msg_odd):
    lay = Layout(fields, copies)
    cols = got_even.shape[-1]
    is_even = axis_even("lat")
    inside = lat_inside(cols)
    sub = sub_iota((8, cols))
    high, low = [], []
    for m in range(lay.row_blocks):
        a = got_even[pl.ds(8 * m, 8), :]
        b = got_odd[pl.ds(8 * m, 8), :]
        high.append(jnp.where(is_even, a, b))
        low.append(jnp.where(is_even, b, a))
    blocks = []
    for j, (at, d) in enumerate(zip(lay.starts, lay.depths)):
        above = turn(high[at // 8], -(at % 8), 0)
        below = turn(low[at // 8], 8 - d - at % 8, 0)
        block = jnp.where(sub < d, above, jnp.where(sub >= 8 - d, below, 0.0))
        block = jnp.where(inside, block, 0.0)
        halo_rows[j] = block
        blocks.append(block)
    where = list(zip(blocks, lay.lanes, lay.depths))
    low_tail = pack_lanes([(x[:, :LANES], 0, at, d) for x, at, d in where])
    high_tail = pack_lanes([(x[:, -LANES:], LANES - d, at, d) for x, at, d in where])
    low_all = squeeze_lanes(jnp.concatenate([col_low[...], low_tail], axis=0), lay.wide, lay)
    high_all = squeeze_lanes(jnp.concatenate([col_high[...], high_tail], axis=0), lay.wide, lay)
    lon_even = axis_even("lon")
    for m, (a, b) in enumerate(zip(low_all, high_all)):
        msg_even[pl.ds(8 * m, 8), :] = jnp.where(lon_even, b, a)
        msg_odd[pl.ds(8 * m, 8), :] = jnp.where(lon_even, a, b)


def row_mask(rows, width):
    inside = lat_inside(width)

    def clear(field):
        return jnp.concatenate([field[:rows], jnp.where(inside, field[rows:], 0.0)], axis=0)

    return clear


def north(x):
    return pltpu.roll(x, x.shape[0] - 1, 0)


def south(x):
    return pltpu.roll(x, 1, 0)


def east_of(x):
    return pltpu.roll(x, x.shape[1] - 1, 1)


def west_of(x):
    return pltpu.roll(x, 1, 1)


def mixing(spread, fields):
    return lambda f, g: spread[f * fields + g : f * fields + g + 1]


def blend(mix, field, f):
    total = None
    for g in range(len(field)):
        factor = mix(f, g)
        if f == g:
            factor = factor + (1.0 - 4.0 * DIFFUSION)
        term = factor * field[g]
        total = term if total is None else total + term
    return total


def tangent(field, u, v, mix):
    kn, ks, ke, kw = DIFFUSION - v, DIFFUSION + v, DIFFUSION - u, DIFFUSION + u
    return [
        blend(mix, field, f)
        + (kn * north(x) + ks * south(x))
        + (ke * east_of(x) + kw * west_of(x))
        for f, x in enumerate(field)
    ]


def adjoint(field, u, v, mix):
    kn, ks, ke, kw = DIFFUSION + v, DIFFUSION - v, DIFFUSION + u, DIFFUSION - u
    return [
        blend(lambda a, b: mix(b, a), field, f)
        + (north(kn * x) + south(ks * x))
        + (east_of(ke * x) + west_of(kw * x))
        for f, x in enumerate(field)
    ]


def product(own, above, below, wgt, mix, prior_mix, fields, rows):
    clear = row_mask(rows, own[0].shape[1])
    here = lax.axis_index("win")
    has_later = here < lax.axis_size("win") - 1
    has_earlier = here > 0
    inc, wind, hmap = own[:fields], own[fields : fields + 2], own[fields + 2 :]
    fwd = [clear(x) for x in tangent(inc, *wind, mix)]
    fwd = tangent(fwd, *wind, mix)
    source = []
    for f in range(fields):
        later = above[fields + f] * (above[f] - fwd[f])
        source.append(clear(hmap[f] * fwd[f] - jnp.where(has_later, later, 0.0)))
    back = [clear(x) for x in adjoint(source, *wind, mix)]
    back = adjoint(back, *wind, mix)
    prior_wind = below[fields : fields + 2]
    prior = [clear(x) for x in tangent(below[:fields], *prior_wind, prior_mix)]
    prior = tangent(prior, *prior_wind, prior_mix)
    return [
        wgt[f] * (inc[f][:rows] - jnp.where(has_earlier, prior[f][:rows], 0.0)) + back[f][:rows]
        for f in range(fields)
    ]


def strip_lines(tiles, group):
    west, east = None, None
    for f, x in enumerate(tiles):
        low = turn(x[:, :LANES], group * f + HALO, 1)
        high = turn(x[:, -LANES:], group * f + group - HALO, 1)
        lane = lane_iota(low.shape)
        west = low if f == 0 else jnp.where(lane >= group * f, low, west)
        east = high if f == 0 else jnp.where(lane >= group * f, high, east)
    return west, east


def line_offsets(fields):
    return [o for o in range(1 - fields, fields)]


def line_factors(mix, lay):
    fields = lay.fields
    lane = lane_iota((1, LANES)) % lay.wide
    rows = []
    for o in line_offsets(fields):
        row = jnp.zeros((1, LANES), F32)
        for f in range(fields):
            if 0 <= f - o < fields:
                factor = mix(f, f - o)[:, :LANES]
                if o == 0:
                    factor = factor + (1.0 - 4.0 * DIFFUSION)
                row = jnp.where((lane >= lay.group * f) & (lane < lay.group * (f + 1)), factor, row)
        rows.append(row)
    return rows


def line_blend(factors, x, fields, group):
    total = None
    for o, factor in zip(line_offsets(fields), factors):
        term = factor * turn(x, group * o, 1)
        total = term if total is None else total + term
    return total


def line_wind(pair, lay):
    group = lay.group
    lane = lane_iota(pair.shape) % lay.wide
    up, down = turn(pair, group, 1), turn(pair, -group, 1)
    far_up = turn(pair, 2 * group, 1)
    u = jnp.where(lane < group, pair, jnp.where(lane < 2 * group, up, far_up))
    v = jnp.where(lane < group, down, jnp.where(lane < 2 * group, pair, up))
    return u, v


def folded(lay, blocks):
    groups, per = lay.groups(blocks, lay.wide)
    end = (blocks - 1) % per
    far = lay.wide * (groups - 1)
    sub, part = sub_iota((8, LANES)), lane_iota((8, LANES)) // lay.wide

    def put(x, i, block):
        pieces = [x[8 * j : 8 * j + 8] for j in range(per)]
        pieces[i] = block
        return jnp.concatenate(pieces, axis=0)

    def up(x):
        y = pltpu.roll(x, x.shape[0] - 1, 0)
        last = y[8 * (per - 1) :]
        y = put(y, per - 1, jnp.where((sub == 7) & (part < groups - 1), turn(last, -lay.wide, 1), last))
        wrap = turn(turn(x[:8], 7, 0), far, 1)
        here = y[8 * end : 8 * end + 8]
        return put(y, end, jnp.where((sub == 7) & (part == groups - 1), wrap, here))

    def down(x):
        y = pltpu.roll(x, 1, 0)
        first = y[:8]
        wrap = turn(turn(x[8 * end : 8 * end + 8], 1, 0), -far, 1)
        fixed = jnp.where(part == 0, wrap, turn(first, lay.wide, 1))
        return put(y, 0, jnp.where(sub == 0, fixed, first))

    return up, down


def line_tangent(x, u, v, factors, lay, up, down):
    kn, ks, ke, kw = DIFFUSION - v, DIFFUSION + v, DIFFUSION - u, DIFFUSION + u
    return (
        line_blend(factors, x, lay.fields, lay.group)
        + (kn * up(x) + ks * down(x))
        + (ke * east_of(x) + kw * west_of(x))
    )


def line_adjoint(x, u, v, factors, lay, up, down):
    kn, ks, ke, kw = DIFFUSION + v, DIFFUSION - v, DIFFUSION + u, DIFFUSION - u
    return (
        line_blend(factors, x, lay.fields, lay.group)
        + (up(kn * x) + down(ks * x))
        + (east_of(ke * x) + west_of(kw * x))
    )


def inner_kernel(copies, inc, wgt, wind, hmap, mixrows, halo_rows, *refs):
    bulk = refs[:copies]
    part, even_base, odd_base, even_wgt, odd_wgt, factors = refs[copies:]
    fields, rows, cols = wgt.shape
    lay = Layout(fields, copies)
    tiles = [inc[f] for f in range(fields)] + [wind[0], wind[1]] + [hmap[f] for f in range(fields)]
    for ref in bulk:
        tiles += [ref[j] for j in range(lay.packet)]
    planes = [jnp.concatenate([tile, halo_rows[j]], axis=0) for j, tile in enumerate(tiles)]
    lon_even = axis_even("lon")

    def store(even_ref, odd_ref, tiles):
        west, east = strip_lines(tiles, lay.group)
        west, east = squeeze_lanes(west, lay.wide, lay), squeeze_lanes(east, lay.wide, lay)
        for i, (w, e) in enumerate(zip(west, east)):
            even_ref[pl.ds(8 * i, 8), :] = jnp.where(lon_even, e, w)
            odd_ref[pl.ds(8 * i, 8), :] = jnp.where(lon_even, w, e)

    for k, members in enumerate(line_planes(lay)):
        store(even_base.at[k], odd_base.at[k], [planes[j] for j in members])
    blank = jnp.zeros((2 * HALO, cols), F32)
    store(even_wgt, odd_wgt, [jnp.concatenate([wgt[f], blank], axis=0) for f in range(fields)])
    above = planes[lay.own : lay.own + lay.packet]
    below = planes[-lay.packet :]
    spread = bulk[-1][2 * fields - 1, :16]
    mix, prior_mix = mixing(mixrows[:, :cols], fields), mixing(spread, fields)
    lists = []
    for maker in (mix, lambda f, g: mix(g, f), prior_mix):
        lists += line_factors(maker, lay)
    for i, row in enumerate(lists):
        factors[i : i + 1] = row
    result = product(planes[: lay.own], above, below, wgt, mix, prior_mix, fields, rows)
    for f in range(fields):
        part[f] = result[f]


def side_kernel(copies, is_odd, got, base, wgt_line, factors, part, *refs):
    fields, rows, cols = part.shape
    lay = Layout(fields, copies)
    group, wide = lay.group, lay.wide
    out = refs[1] if is_odd else refs[0]
    on_east = axis_even("lon") != is_odd
    msg = got[...]
    lane, sub = lane_iota(msg.shape), sub_iota(msg.shape)
    within = lane % wide % group
    side = jnp.where(on_east, (within >= group - HALO).astype(jnp.int32), (within < HALO).astype(jnp.int32)) > 0
    lines = []
    for k, (spot, members) in enumerate(zip(lay.spots, line_planes(lay))):
        depth = lay.depths[members[0]]
        moved = jnp.where(
            on_east, turn(msg, group - HALO - spot, 1), turn(msg, HALO - depth - spot, 1)
        )
        lines.append(jnp.where(side, moved, base[k]))
    row = sub + msg.shape[0] * (lane // wide)
    here = lax.axis_index("lat")
    from_high = (here < lax.axis_size("lat") - 1).astype(jnp.int32)
    from_low = (here > 0).astype(jnp.int32)
    inside = jnp.where(row < rows, 1, jnp.where(row < rows + HALO, from_high, from_low)) > 0

    def clear(x):
        return jnp.where(inside, x, 0.0)

    up, down = folded(lay, rows // 8 + 1)
    win = lax.axis_index("win")
    has_later = win < lax.axis_size("win") - 1
    has_earlier = win > 0
    count = 2 * fields - 1
    every = factors[...]
    mix, mix_back, mix_prior = [
        [every[g * count + i : g * count + i + 1] for i in range(count)] for g in range(3)
    ]
    inc, hmap = lines[0], lines[2]
    u, v = line_wind(lines[1], lay)
    fwd = clear(line_tangent(inc, u, v, mix, lay, up, down))
    fwd = line_tangent(fwd, u, v, mix, lay, up, down)
    later = lines[4] * (lines[3] - fwd)
    back = clear(hmap * fwd - jnp.where(has_later, later, 0.0))
    back = clear(line_adjoint(back, u, v, mix_back, lay, up, down))
    back = line_adjoint(back, u, v, mix_back, lay, up, down)
    u, v = line_wind(lines[-1], lay)
    prior = clear(line_tangent(lines[-2], u, v, mix_prior, lay, up, down))
    prior = line_tangent(prior, u, v, mix_prior, lay, up, down)
    result = wgt_line[...] * (inc - jnp.where(has_earlier, prior, 0.0)) + back
    per = msg.shape[0] // 8
    lane = lane_iota((8, LANES))
    to_west = jnp.where(on_east, 0, HALO)
    to_east = jnp.where(on_east, LANES - HALO, LANES)
    moves = []
    for f in range(fields):
        for m in range(rows // 8):
            i, at = m % per, wide * (m // per) + group * f
            block = result[8 * i : 8 * i + 8]
            low = turn(block, -(at + HALO), 1)
            high = turn(block, LANES - (at + group - HALO), 1)
            spot = pl.ds(8 * m, 8)
            if cols == LANES:
                whole = jnp.where(lane < to_west, low, part[f, spot, :])
                out[f, spot, :] = jnp.where(lane >= to_east, high, whole)
            else:
                out[f, spot, pl.ds(0, LANES)] = jnp.where(lane < to_west, low, part[f, spot, :LANES])
                for h in range(1, cols // LANES - 1):
                    out[f, spot, pl.ds(h * LANES, LANES)] = part[f, spot, h * LANES : (h + 1) * LANES]
                out[f, spot, pl.ds(cols - LANES, LANES)] = jnp.where(
                    lane >= to_east, high, part[f, spot, cols - LANES :]
                )
        if is_odd:
            moves.append(pltpu.make_async_copy(out.at[f], refs[0].at[f], refs[2].at[f]))
            moves[-1].start()
    for move in moves:
        move.wait()


def vmem():
    return pl.BlockSpec(memory_space=pltpu.VMEM)


def hbm():
    return pl.BlockSpec(memory_space=pltpu.HBM)


def far(array):
    return pltpu.with_memory_space_constraint(array, pltpu.HBM)


def call(kernel, in_specs, shapes, flops, scratch=(), out_spec=None):
    return pl.pallas_call(
        kernel,
        scratch_shapes=scratch,
        compiler_params=pltpu.CompilerParams(vmem_limit_bytes=VMEM_LIMIT),
        out_shape=[s if isinstance(s, jax.ShapeDtypeStruct) else jax.ShapeDtypeStruct(s, F32) for s in shapes],
        in_specs=in_specs,
        out_specs=[out_spec or vmem()] * len(shapes),
        cost_estimate=pl.CostEstimate(flops=flops, bytes_accessed=1 << 20, transcendentals=0),
    )


VMEM_LIMIT = 12 << 20


def per_device(increment, model_weight, winds, reaction, obs_cells, obs_weight):
    inc = increment[0]
    wgt = model_weight[0]
    wind = winds[0]
    mix = reaction.transpose(1, 0, 2)
    fields, rows, cols = inc.shape
    nobs = obs_cells.shape[-1]
    cells = obs_cells.reshape(1, nobs)
    scale = obs_weight.reshape(fields, 1, nobs)
    tall = rows + 2 * HALO
    swap2 = lax.axis_size("win") == 2
    copies = 1 if swap2 else 2
    lay = Layout(fields, copies)
    tile = (fields, rows, cols)
    packet = (lay.packet, rows, cols)
    strip_rows = 8 * (-(-4 * lay.packet // 8) * (cols // LANES) + lay.groups(rows // 8, 4 * lay.packet)[1])
    row_msg = (8 * lay.row_blocks, cols)
    col_msg = (8 * lay.groups(tall // 8, lay.wide)[1], LANES)

    mixrows, *rest = call(
        functools.partial(load_kernel, swap2, copies),
        [hbm()] * 4,
        [(16, cols)] + [packet] * copies + [(strip_rows, LANES)] * copies,
        1 << 20,
        [pltpu.SMEM(mix.shape, F32), pltpu.SemaphoreType.DMA((5,))],
    )(far(inc), far(wgt), far(wind), far(mix))
    sent, strips = rest[:copies], rest[copies:]
    strips = window_swap(strips[0], strips[-1])[:copies]
    bulk = window_swap(sent[0], sent[-1])[:copies]

    wind_near, wgt_near, hmap, row_first, row_last, col_low, col_high = call(
        functools.partial(own_kernel, copies),
        [vmem()] + [hbm()] * 4,
        [wind.shape, tile, tile, row_msg, row_msg, (rows, LANES), (rows, LANES)],
        1 << 29,
        [pltpu.VMEM(cells.shape, jnp.int32), pltpu.VMEM(scale.shape, F32), pltpu.SemaphoreType.DMA((4,))],
    )(sent[0], far(wind), far(wgt), far(cells), far(scale))

    row_even, row_odd, col_low, col_high = call(
        functools.partial(join_kernel, fields, copies),
        [vmem()] * (4 + copies),
        [row_msg, row_msg, (rows, LANES), (rows, LANES)],
        1 << 16,
    )(row_first, row_last, col_low, col_high, *strips)
    got_even, got_odd = neighbour_swap(row_even, row_odd, "lat")

    halo_rows, msg_even, msg_odd = call(
        functools.partial(rows_kernel, fields, copies), [vmem()] * 4, [(lay.count, 8, cols), col_msg, col_msg], 1 << 16
    )(got_even, got_odd, col_low, col_high)
    got_even, got_odd = neighbour_swap(msg_even, msg_odd, "lon")

    base_shape = (len(line_planes(lay)),) + col_msg
    part, even_base, odd_base, even_wgt, odd_wgt, factors = call(
        functools.partial(inner_kernel, copies),
        [vmem()] * (6 + copies),
        [tile, base_shape, base_shape, col_msg, col_msg, (8 * -(-3 * (2 * fields - 1) // 8), LANES)],
        1 << 29,
    )(sent[0], wgt_near, wind_near, hmap, mixrows, halo_rows, *bulk)
    (part,) = call(
        functools.partial(side_kernel, copies, False), [vmem()] * 5, [tile], 1 << 28
    )(got_even, even_base, even_wgt, factors, part)
    (out,) = call(
        functools.partial(side_kernel, copies, True),
        [vmem()] * 5,
        [tile],
        1 << 25,
        [pltpu.VMEM(tile, F32), pltpu.SemaphoreType.DMA((fields,))],
        hbm(),
    )(got_odd, odd_base, odd_wgt, factors, part)
    return out[None]


def solution(mesh):
    in_specs = (
        P("win", None, "lat", "lon"),
        P("win", None, "lat", "lon"),
        P("win", None, "lat", "lon"),
        P("win", None, None),
        P("win", "lat", "lon", None),
        P("win", None, "lat", "lon", None),
    )
    out_specs = P("win", None, "lat", "lon")

    return jax.shard_map(per_device, mesh=mesh, in_specs=in_specs, out_specs=out_specs, check_vma=False)
```

```python
import functools

import jax
import jax.numpy as jnp
from jax import lax
from jax.experimental import pallas as pl
from jax.experimental.pallas import tpu as pltpu
from jax.sharding import PartitionSpec as P


DIFFUSION = 0.15
HALO = 4
RIM = 2
LANES = 128
F32 = jnp.float32


def even_pairs(n):
    return [(i, i ^ 1) for i in range(n)]


def odd_pairs(n):
    return [(i, (i + 1 if i % 2 else i - 1) % n) for i in range(n)]


def ring(n, step):
    return [(i, (i + step) % n) for i in range(n)]


def neighbour_swap(even_msg, odd_msg, axis):
    n = lax.axis_size(axis)
    from_even = lax.ppermute(even_msg, axis, even_pairs(n))
    from_odd = lax.ppermute(odd_msg, axis, odd_pairs(n))
    return from_even, from_odd


def window_swap(down, up):
    n = lax.axis_size("win")
    if n == 2:
        got = lax.ppermute(down, "win", even_pairs(n))
        return got, got
    return lax.ppermute(down, "win", ring(n, -1)), lax.ppermute(up, "win", ring(n, 1))


def sub_iota(shape):
    return lax.broadcasted_iota(jnp.int32, shape, len(shape) - 2)


def lane_iota(shape):
    return lax.broadcasted_iota(jnp.int32, shape, len(shape) - 1)


def turn(x, shift, axis):
    shift %= x.shape[axis]
    return pltpu.roll(x, shift, axis) if shift else x


def axis_even(axis):
    return lax.axis_index(axis) % 2 == 0


def line_planes(lay):
    fields = lay.fields
    lines = [range(fields), range(fields, fields + 2), range(fields + 2, lay.own)]
    for k in range(lay.copies):
        base = lay.own + k * lay.packet
        lines += [range(base, base + fields), range(base + fields, base + lay.packet)]
    return lines


class Layout:
    def __init__(self, fields, copies):
        self.fields, self.copies = fields, copies
        self.own = 2 + 2 * fields
        self.packet = 2 * fields
        self.depths = [HALO] * (fields + 2) + [RIM] * (fields + self.packet * copies)
        self.count = len(self.depths)
        self.starts = [sum(self.depths[:j]) for j in range(self.count)]
        self.used = sum(self.depths)
        self.row_blocks = -(-self.used // 8)
        spots = [0, HALO] + [2 * HALO + RIM * k for k in range(1 + 2 * copies)]
        self.group = 2 * HALO + RIM * (1 + 2 * copies)
        self.wide = self.group * fields
        self.lanes = [0] * self.count
        for spot, members in zip(spots, line_planes(self)):
            for f, j in enumerate(members):
                self.lanes[j] = self.group * f + spot
        self.spots = spots

    def groups(self, blocks, width):
        per = -(-blocks // (LANES // width))
        return -(-blocks // per), per


def squeeze_lanes(wide, width, lay):
    blocks = wide.shape[0] // 8
    groups, per = lay.groups(blocks, width)
    lane = lane_iota((8, LANES))
    out = []
    for i in range(per):
        block = None
        for g in range(groups):
            if g * per + i < blocks:
                part = turn(wide[8 * (g * per + i) : 8 * (g * per + i) + 8], width * g, 1)
                block = part if block is None else jnp.where(lane >= width * g, part, block)
        out.append(block)
    return out


def spread_lanes(tight, blocks, width, lay):
    _, per = lay.groups(blocks, width)
    out = []
    for b in range(blocks):
        g, i = b // per, b % per
        out.append(turn(tight[i], -width * g, 1))
    return jnp.concatenate(out, axis=0)


def pack_rows(pieces, blocks):
    out = [None] * blocks
    for block, first, at, depth in pieces:
        b, s = at // 8, at % 8
        moved = turn(block, s - first, 0)
        sub = sub_iota(moved.shape)
        out[b] = moved if out[b] is None else jnp.where((sub >= s) & (sub < s + depth), moved, out[b])
    return out


def pack_lanes(pieces, out=None):
    for block, first, at, depth in pieces:
        moved = turn(block, at - first, 1)
        lane = lane_iota(moved.shape)
        out = moved if out is None else jnp.where((lane >= at) & (lane < at + depth), moved, out)
    return out


def load_kernel(swap2, copies, *refs):
    inc_far, wgt_far, wind_far, mix_far, mixrows = refs[:5]
    bulk = refs[5 : 5 + copies]
    strips = refs[5 + copies : 5 + 2 * copies]
    mix, sems = refs[5 + 2 * copies :]
    packet, rows, cols = bulk[0].shape
    fields = packet // 2
    lay = Layout(fields, copies)
    sends_up = lax.axis_index("win") == 0
    moves = [
        pltpu.make_async_copy(inc_far, ref.at[pl.ds(0, fields)], sems.at[i]) for i, ref in enumerate(bulk)
    ]
    moves.append(pltpu.make_async_copy(mix_far, mix, sems.at[2]))
    to_down = pltpu.make_async_copy(wgt_far, bulk[0].at[pl.ds(fields, fields)], sems.at[3])
    to_up = pltpu.make_async_copy(wind_far, bulk[-1].at[pl.ds(fields, 2)], sems.at[4])

    def on(condition, action):
        if swap2:
            pl.when(condition)(action)
        else:
            action()

    for move in moves:
        move.start()
    on(sends_up, lambda: to_up.start())
    on(jnp.logical_not(sends_up), lambda: to_down.start())
    for move in moves:
        move.wait()
    which = sub_iota(mixrows.shape)
    spread = jnp.zeros(mixrows.shape, F32)
    for f in range(fields):
        for g in range(fields):
            spread = jnp.where(which == f * fields + g, mix[f, 0, g], spread)
    mixrows[...] = spread

    def fill_up():
        to_up.wait()
        used = mixrows.shape[0]
        bulk[-1][packet - 1, pl.ds(0, used), :] = spread[:, :cols]
        bulk[-1][packet - 1, pl.ds(used, rows - used), :] = jnp.zeros((rows - used, cols), F32)

    on(sends_up, fill_up)
    on(jnp.logical_not(sends_up), lambda: to_down.wait())

    for k, ref in enumerate(strips):
        planes = [bulk[k][j] for j in range(packet)]
        pieces = []
        for j, x in enumerate(planes):
            pieces.append((x[:8], 0, 4 * j, RIM))
            pieces.append((x[-8:], 8 - RIM, 4 * j + 2, RIM))
        blocks = pack_rows(pieces, -(-4 * lay.packet // 8))
        halves = cols // LANES
        for m, block in enumerate(blocks):
            for h in range(halves):
                ref[pl.ds(8 * (m * halves + h), 8), :] = block[:, h * LANES : (h + 1) * LANES]
        pieces = []
        for j, x in enumerate(planes):
            pieces.append((x[:, :LANES], 0, 4 * j, RIM))
            pieces.append((x[:, -LANES:], LANES - RIM, 4 * j + 2, RIM))
        for m, block in enumerate(squeeze_lanes(pack_lanes(pieces), 4 * lay.packet, lay)):
            ref[pl.ds(8 * (len(blocks) * halves + m), 8), :] = block


def own_kernel(copies, bulk, wind_far, wgt_far, cells_far, scale_far, *refs):
    wind, wgt, hmap, row_first, row_last, col_low, col_high, cells, scale, sems = refs
    moves = [
        pltpu.make_async_copy(src, dst, sems.at[i])
        for i, (src, dst) in enumerate(
            [(cells_far, cells), (scale_far, scale), (wind_far, wind), (wgt_far, wgt)]
        )
    ]
    for move in moves:
        move.start()
    packet, rows, cols = bulk.shape
    fields = packet // 2
    inc = bulk
    lay = Layout(fields, copies)
    moves[0].wait()
    moves[1].wait()
    nobs = cells.shape[-1]
    index = cells[...]
    row_hot = sub_iota((rows, nobs)) == index // cols
    col_hot = (sub_iota((cols, nobs)) == index % cols).astype(F32).astype(jnp.bfloat16)
    terms = []
    for f in range(fields):
        rest = scale[f]
        for _ in range(3):
            part = rest.astype(jnp.bfloat16)
            rest = rest - part.astype(F32)
            terms.append(jnp.where(row_hot, part.astype(F32), 0.0).astype(jnp.bfloat16))
    sums = lax.dot_general(
        jnp.concatenate(terms, axis=0), col_hot, (((1,), (1,)), ((), ())), preferred_element_type=F32
    )
    moves[2].wait()
    planes = [inc[f] for f in range(fields)] + [wind[0], wind[1]]
    for f in range(fields):
        base = 3 * f * rows
        value = sums[base : base + rows] + (
            sums[base + rows : base + 2 * rows] + sums[base + 2 * rows : base + 3 * rows]
        )
        hmap[f] = value
        planes.append(value)
    where = list(zip(planes, lay.starts, lay.depths))
    first = pack_rows([(x[:8], 0, at, d) for x, at, d in where], lay.row_blocks)
    last = pack_rows([(x[-8:], 8 - d, at, d) for x, at, d in where], lay.row_blocks)
    for m in range(lay.row_blocks):
        blank = jnp.zeros((8, cols), F32)
        row_first[pl.ds(8 * m, 8), :] = blank if first[m] is None else first[m]
        row_last[pl.ds(8 * m, 8), :] = blank if last[m] is None else last[m]
    where = list(zip(planes, lay.lanes, lay.depths))
    col_low[...] = pack_lanes([(x[:, :LANES], 0, at, d) for x, at, d in where])
    col_high[...] = pack_lanes([(x[:, -LANES:], LANES - d, at, d) for x, at, d in where])
    moves[3].wait()


def join_kernel(fields, copies, *refs):
    row_first, row_last = refs[:2]
    strips = refs[2 : 2 + copies]
    row_even, row_odd = refs[2 + copies :]
    lay = Layout(fields, copies)
    cols = row_first.shape[1]
    halves = cols // LANES
    first_pieces, last_pieces = [], []
    for k, ref in enumerate(strips):
        blocks = [
            jnp.concatenate([ref[pl.ds(8 * (m * halves + h), 8), :] for h in range(halves)], axis=1)
            for m in range(-(-4 * lay.packet // 8))
        ]
        for j in range(lay.packet):
            at = lay.starts[lay.own + k * lay.packet + j]
            first_pieces.append((blocks[4 * j // 8], 4 * j % 8, at, RIM))
            last_pieces.append((blocks[4 * j // 8], 4 * j % 8 + 2, at, RIM))
    is_even = axis_even("lat")
    own_used = lay.starts[lay.own]
    first = pack_rows(first_pieces, lay.row_blocks)
    last = pack_rows(last_pieces, lay.row_blocks)
    for m in range(lay.row_blocks):
        a, b = row_first[pl.ds(8 * m, 8), :], row_last[pl.ds(8 * m, 8), :]
        if first[m] is not None:
            other = sub_iota(a.shape) + 8 * m >= own_used
            a, b = jnp.where(other, first[m], a), jnp.where(other, last[m], b)
        row_even[pl.ds(8 * m, 8), :] = jnp.where(is_even, b, a)
        row_odd[pl.ds(8 * m, 8), :] = jnp.where(is_even, a, b)


def cols_kernel(fields, copies, *refs):
    col_low, col_high = refs[:2]
    strips = refs[2 : 2 + copies]
    even_out, odd_out = refs[2 + copies :]
    lay = Layout(fields, copies)
    rows = col_low.shape[0]
    low_pieces, high_pieces = [], []
    for k, ref in enumerate(strips):
        _, per = lay.groups(rows // 8, 4 * lay.packet)
        base = ref.shape[0] - 8 * per
        tight = [ref[pl.ds(base + 8 * i, 8), :] for i in range(per)]
        wide = spread_lanes(tight, rows // 8, 4 * lay.packet, lay)
        for j in range(lay.packet):
            at = lay.lanes[lay.own + k * lay.packet + j]
            low_pieces.append((wide, 4 * j, at, RIM))
            high_pieces.append((wide, 4 * j + 2, at, RIM))
    lon_even = axis_even("lon")
    low = pack_lanes(low_pieces, col_low[...])
    high = pack_lanes(high_pieces, col_high[...])
    blank = jnp.zeros((8, LANES), F32)
    for ref, x in ((even_out, jnp.where(lon_even, high, low)), (odd_out, jnp.where(lon_even, low, high))):
        for i, block in enumerate(squeeze_lanes(jnp.concatenate([x, blank], axis=0), lay.wide, lay)):
            ref[pl.ds(8 * i, 8), :] = block


def lat_inside(width):
    here = lax.axis_index("lat")
    upper = sub_iota((8, width)) < HALO
    from_high = (here < lax.axis_size("lat") - 1).astype(jnp.int32)
    from_low = (here > 0).astype(jnp.int32)
    return jnp.where(upper, from_high, from_low) > 0


def rows_kernel(fields, copies, tail, got_even, got_odd, even_tile, odd_tile, halo_rows, msg_even, msg_odd):
    lay = Layout(fields, copies)
    cols = got_even.shape[-1]
    is_even = axis_even("lat")
    inside = lat_inside(cols)
    sub = sub_iota((8, cols))
    high, low = [], []
    for m in range(lay.row_blocks):
        a = got_even[pl.ds(8 * m, 8), :]
        b = got_odd[pl.ds(8 * m, 8), :]
        high.append(jnp.where(is_even, a, b))
        low.append(jnp.where(is_even, b, a))
    blocks = []
    for j, (at, d) in enumerate(zip(lay.starts, lay.depths)):
        above = turn(high[at // 8], -(at % 8), 0)
        below = turn(low[at // 8], 8 - d - at % 8, 0)
        block = jnp.where(sub < d, above, jnp.where(sub >= 8 - d, below, 0.0))
        block = jnp.where(inside, block, 0.0)
        halo_rows[j] = block
        blocks.append(block)
    where = list(zip(blocks, lay.lanes, lay.depths))
    low_tail = pack_lanes([(x[:, :LANES], 0, at, d) for x, at, d in where])
    high_tail = pack_lanes([(x[:, -LANES:], LANES - d, at, d) for x, at, d in where])
    lon_even = axis_even("lon")
    per = even_tile.shape[0] // 8
    shift = lay.wide * (tail // per)
    lane = lane_iota((8, LANES))
    for ref, tile, x in (
        (msg_even, even_tile, jnp.where(lon_even, high_tail, low_tail)),
        (msg_odd, odd_tile, jnp.where(lon_even, low_tail, high_tail)),
    ):
        for i in range(per):
            block = tile[pl.ds(8 * i, 8), :]
            if i == tail % per:
                block = jnp.where((lane >= shift) & (lane < shift + lay.wide), turn(x, shift, 1), block)
            ref[pl.ds(8 * i, 8), :] = block


def row_mask(rows, width):
    inside = lat_inside(width)

    def clear(field):
        return jnp.concatenate([field[:rows], jnp.where(inside, field[rows:], 0.0)], axis=0)

    return clear


def north(x):
    return pltpu.roll(x, x.shape[0] - 1, 0)


def south(x):
    return pltpu.roll(x, 1, 0)


def east_of(x):
    return pltpu.roll(x, x.shape[1] - 1, 1)


def west_of(x):
    return pltpu.roll(x, 1, 1)


def mixing(spread, fields):
    return lambda f, g: spread[f * fields + g : f * fields + g + 1]


def blend(mix, field, f):
    total = None
    for g in range(len(field)):
        factor = mix(f, g)
        if f == g:
            factor = factor + (1.0 - 4.0 * DIFFUSION)
        term = factor * field[g]
        total = term if total is None else total + term
    return total


def tangent(field, u, v, mix):
    kn, ks, ke, kw = DIFFUSION - v, DIFFUSION + v, DIFFUSION - u, DIFFUSION + u
    return [
        blend(mix, field, f)
        + (kn * north(x) + ks * south(x))
        + (ke * east_of(x) + kw * west_of(x))
        for f, x in enumerate(field)
    ]


def adjoint(field, u, v, mix):
    kn, ks, ke, kw = DIFFUSION + v, DIFFUSION - v, DIFFUSION + u, DIFFUSION - u
    return [
        blend(lambda a, b: mix(b, a), field, f)
        + (north(kn * x) + south(ks * x))
        + (east_of(ke * x) + west_of(kw * x))
        for f, x in enumerate(field)
    ]


def product(own, above, below, wgt, mix, prior_mix, fields, rows):
    clear = row_mask(rows, own[0].shape[1])
    here = lax.axis_index("win")
    has_later = here < lax.axis_size("win") - 1
    has_earlier = here > 0
    inc, wind, hmap = own[:fields], own[fields : fields + 2], own[fields + 2 :]
    fwd = [clear(x) for x in tangent(inc, *wind, mix)]
    fwd = tangent(fwd, *wind, mix)
    source = []
    for f in range(fields):
        later = above[fields + f] * (above[f] - fwd[f])
        source.append(clear(hmap[f] * fwd[f] - jnp.where(has_later, later, 0.0)))
    back = [clear(x) for x in adjoint(source, *wind, mix)]
    back = adjoint(back, *wind, mix)
    prior_wind = below[fields : fields + 2]
    prior = [clear(x) for x in tangent(below[:fields], *prior_wind, prior_mix)]
    prior = tangent(prior, *prior_wind, prior_mix)
    return [
        wgt[f] * (inc[f][:rows] - jnp.where(has_earlier, prior[f][:rows], 0.0)) + back[f][:rows]
        for f in range(fields)
    ]


def strip_lines(tiles, group):
    west, east = None, None
    for f, x in enumerate(tiles):
        low = turn(x[:, :LANES], group * f + HALO, 1)
        high = turn(x[:, -LANES:], group * f + group - HALO, 1)
        lane = lane_iota(low.shape)
        west = low if f == 0 else jnp.where(lane >= group * f, low, west)
        east = high if f == 0 else jnp.where(lane >= group * f, high, east)
    return west, east


def line_offsets(fields):
    return [o for o in range(1 - fields, fields)]


def line_factors(mix, lay):
    fields = lay.fields
    lane = lane_iota((1, LANES)) % lay.wide
    rows = []
    for o in line_offsets(fields):
        row = jnp.zeros((1, LANES), F32)
        for f in range(fields):
            if 0 <= f - o < fields:
                factor = mix(f, f - o)[:, :LANES]
                if o == 0:
                    factor = factor + (1.0 - 4.0 * DIFFUSION)
                row = jnp.where((lane >= lay.group * f) & (lane < lay.group * (f + 1)), factor, row)
        rows.append(row)
    return rows


def line_blend(factors, x, fields, group):
    total = None
    for o, factor in zip(line_offsets(fields), factors):
        term = factor * turn(x, group * o, 1)
        total = term if total is None else total + term
    return total


def line_wind(pair, lay):
    group = lay.group
    lane = lane_iota(pair.shape) % lay.wide
    up, down = turn(pair, group, 1), turn(pair, -group, 1)
    far_up = turn(pair, 2 * group, 1)
    u = jnp.where(lane < group, pair, jnp.where(lane < 2 * group, up, far_up))
    v = jnp.where(lane < group, down, jnp.where(lane < 2 * group, pair, up))
    return u, v


def folded(lay, blocks):
    groups, per = lay.groups(blocks, lay.wide)
    end = (blocks - 1) % per
    far = lay.wide * (groups - 1)
    sub, part = sub_iota((8, LANES)), lane_iota((8, LANES)) // lay.wide

    def put(x, i, block):
        pieces = [x[8 * j : 8 * j + 8] for j in range(per)]
        pieces[i] = block
        return jnp.concatenate(pieces, axis=0)

    def up(x):
        y = pltpu.roll(x, x.shape[0] - 1, 0)
        last = y[8 * (per - 1) :]
        y = put(y, per - 1, jnp.where((sub == 7) & (part < groups - 1), turn(last, -lay.wide, 1), last))
        wrap = turn(turn(x[:8], 7, 0), far, 1)
        here = y[8 * end : 8 * end + 8]
        return put(y, end, jnp.where((sub == 7) & (part == groups - 1), wrap, here))

    def down(x):
        y = pltpu.roll(x, 1, 0)
        first = y[:8]
        wrap = turn(turn(x[8 * end : 8 * end + 8], 1, 0), -far, 1)
        fixed = jnp.where(part == 0, wrap, turn(first, lay.wide, 1))
        return put(y, 0, jnp.where(sub == 0, fixed, first))

    return up, down


def line_tangent(x, u, v, factors, lay, up, down):
    kn, ks, ke, kw = DIFFUSION - v, DIFFUSION + v, DIFFUSION - u, DIFFUSION + u
    return (
        line_blend(factors, x, lay.fields, lay.group)
        + (kn * up(x) + ks * down(x))
        + (ke * east_of(x) + kw * west_of(x))
    )


def line_adjoint(x, u, v, factors, lay, up, down):
    kn, ks, ke, kw = DIFFUSION + v, DIFFUSION - v, DIFFUSION + u, DIFFUSION - u
    return (
        line_blend(factors, x, lay.fields, lay.group)
        + (up(kn * x) + down(ks * x))
        + (east_of(ke * x) + west_of(kw * x))
    )


def inner_kernel(copies, inc, wgt, wind, hmap, mixrows, halo_rows, *refs):
    bulk = refs[:copies]
    part, even_base, odd_base, even_wgt, odd_wgt, factors = refs[copies:]
    fields, rows, cols = wgt.shape
    lay = Layout(fields, copies)
    tiles = [inc[f] for f in range(fields)] + [wind[0], wind[1]] + [hmap[f] for f in range(fields)]
    for ref in bulk:
        tiles += [ref[j] for j in range(lay.packet)]
    planes = [jnp.concatenate([tile, halo_rows[j]], axis=0) for j, tile in enumerate(tiles)]
    lon_even = axis_even("lon")

    def store(even_ref, odd_ref, tiles):
        west, east = strip_lines(tiles, lay.group)
        west, east = squeeze_lanes(west, lay.wide, lay), squeeze_lanes(east, lay.wide, lay)
        for i, (w, e) in enumerate(zip(west, east)):
            even_ref[pl.ds(8 * i, 8), :] = jnp.where(lon_even, e, w)
            odd_ref[pl.ds(8 * i, 8), :] = jnp.where(lon_even, w, e)

    for k, members in enumerate(line_planes(lay)):
        store(even_base.at[k], odd_base.at[k], [planes[j] for j in members])
    blank = jnp.zeros((2 * HALO, cols), F32)
    store(even_wgt, odd_wgt, [jnp.concatenate([wgt[f], blank], axis=0) for f in range(fields)])
    above = planes[lay.own : lay.own + lay.packet]
    below = planes[-lay.packet :]
    spread = bulk[-1][2 * fields - 1, :16]
    mix, prior_mix = mixing(mixrows[:, :cols], fields), mixing(spread, fields)
    lists = []
    for maker in (mix, lambda f, g: mix(g, f), prior_mix):
        lists += line_factors(maker, lay)
    for i, row in enumerate(lists):
        factors[i : i + 1] = row
    result = product(planes[: lay.own], above, below, wgt, mix, prior_mix, fields, rows)
    for f in range(fields):
        part[f] = result[f]


def side_kernel(copies, is_odd, got, base, wgt_line, factors, part, *refs):
    fields, rows, cols = part.shape
    lay = Layout(fields, copies)
    group, wide = lay.group, lay.wide
    out = refs[1] if is_odd else refs[0]
    on_east = axis_even("lon") != is_odd
    msg = got[...]
    lane, sub = lane_iota(msg.shape), sub_iota(msg.shape)
    within = lane % wide % group
    side = jnp.where(on_east, (within >= group - HALO).astype(jnp.int32), (within < HALO).astype(jnp.int32)) > 0
    lines = []
    for k, (spot, members) in enumerate(zip(lay.spots, line_planes(lay))):
        depth = lay.depths[members[0]]
        moved = jnp.where(
            on_east, turn(msg, group - HALO - spot, 1), turn(msg, HALO - depth - spot, 1)
        )
        lines.append(jnp.where(side, moved, base[k]))
    row = sub + msg.shape[0] * (lane // wide)
    here = lax.axis_index("lat")
    from_high = (here < lax.axis_size("lat") - 1).astype(jnp.int32)
    from_low = (here > 0).astype(jnp.int32)
    inside = jnp.where(row < rows, 1, jnp.where(row < rows + HALO, from_high, from_low)) > 0

    def clear(x):
        return jnp.where(inside, x, 0.0)

    up, down = folded(lay, rows // 8 + 1)
    win = lax.axis_index("win")
    has_later = win < lax.axis_size("win") - 1
    has_earlier = win > 0
    count = 2 * fields - 1
    every = factors[...]
    mix, mix_back, mix_prior = [
        [every[g * count + i : g * count + i + 1] for i in range(count)] for g in range(3)
    ]
    inc, hmap = lines[0], lines[2]
    u, v = line_wind(lines[1], lay)
    fwd = clear(line_tangent(inc, u, v, mix, lay, up, down))
    fwd = line_tangent(fwd, u, v, mix, lay, up, down)
    later = lines[4] * (lines[3] - fwd)
    back = clear(hmap * fwd - jnp.where(has_later, later, 0.0))
    back = clear(line_adjoint(back, u, v, mix_back, lay, up, down))
    back = line_adjoint(back, u, v, mix_back, lay, up, down)
    u, v = line_wind(lines[-1], lay)
    prior = clear(line_tangent(lines[-2], u, v, mix_prior, lay, up, down))
    prior = line_tangent(prior, u, v, mix_prior, lay, up, down)
    result = wgt_line[...] * (inc - jnp.where(has_earlier, prior, 0.0)) + back
    per = msg.shape[0] // 8
    lane = lane_iota((8, LANES))
    to_west = jnp.where(on_east, 0, HALO)
    to_east = jnp.where(on_east, LANES - HALO, LANES)
    moves = []
    for f in range(fields):
        for m in range(rows // 8):
            i, at = m % per, wide * (m // per) + group * f
            block = result[8 * i : 8 * i + 8]
            low = turn(block, -(at + HALO), 1)
            high = turn(block, LANES - (at + group - HALO), 1)
            spot = pl.ds(8 * m, 8)
            if cols == LANES:
                whole = jnp.where(lane < to_west, low, part[f, spot, :])
                out[f, spot, :] = jnp.where(lane >= to_east, high, whole)
            else:
                out[f, spot, pl.ds(0, LANES)] = jnp.where(lane < to_west, low, part[f, spot, :LANES])
                for h in range(1, cols // LANES - 1):
                    out[f, spot, pl.ds(h * LANES, LANES)] = part[f, spot, h * LANES : (h + 1) * LANES]
                out[f, spot, pl.ds(cols - LANES, LANES)] = jnp.where(
                    lane >= to_east, high, part[f, spot, cols - LANES :]
                )
        if is_odd:
            moves.append(pltpu.make_async_copy(out.at[f], refs[0].at[f], refs[2].at[f]))
            moves[-1].start()
    for move in moves:
        move.wait()


def vmem():
    return pl.BlockSpec(memory_space=pltpu.VMEM)


def hbm():
    return pl.BlockSpec(memory_space=pltpu.HBM)


def far(array):
    return pltpu.with_memory_space_constraint(array, pltpu.HBM)


def call(kernel, in_specs, shapes, flops, scratch=(), out_spec=None):
    return pl.pallas_call(
        kernel,
        scratch_shapes=scratch,
        compiler_params=pltpu.CompilerParams(vmem_limit_bytes=VMEM_LIMIT),
        out_shape=[s if isinstance(s, jax.ShapeDtypeStruct) else jax.ShapeDtypeStruct(s, F32) for s in shapes],
        in_specs=in_specs,
        out_specs=[out_spec or vmem()] * len(shapes),
        cost_estimate=pl.CostEstimate(flops=flops, bytes_accessed=1 << 20, transcendentals=0),
    )


VMEM_LIMIT = 12 << 20


def per_device(increment, model_weight, winds, reaction, obs_cells, obs_weight):
    inc = increment[0]
    wgt = model_weight[0]
    wind = winds[0]
    mix = reaction.transpose(1, 0, 2)
    fields, rows, cols = inc.shape
    nobs = obs_cells.shape[-1]
    cells = obs_cells.reshape(1, nobs)
    scale = obs_weight.reshape(fields, 1, nobs)
    tall = rows + 2 * HALO
    swap2 = lax.axis_size("win") == 2
    copies = 1 if swap2 else 2
    lay = Layout(fields, copies)
    tile = (fields, rows, cols)
    packet = (lay.packet, rows, cols)
    strip_rows = 8 * (-(-4 * lay.packet // 8) * (cols // LANES) + lay.groups(rows // 8, 4 * lay.packet)[1])
    row_msg = (8 * lay.row_blocks, cols)
    col_msg = (8 * lay.groups(tall // 8, lay.wide)[1], LANES)

    mixrows, *rest = call(
        functools.partial(load_kernel, swap2, copies),
        [hbm()] * 4,
        [(16, cols)] + [packet] * copies + [(strip_rows, LANES)] * copies,
        1 << 20,
        [pltpu.SMEM(mix.shape, F32), pltpu.SemaphoreType.DMA((5,))],
    )(far(inc), far(wgt), far(wind), far(mix))
    sent, strips = rest[:copies], rest[copies:]
    strips = window_swap(strips[0], strips[-1])[:copies]
    bulk = window_swap(sent[0], sent[-1])[:copies]

    wind_near, wgt_near, hmap, row_first, row_last, col_low, col_high = call(
        functools.partial(own_kernel, copies),
        [vmem()] + [hbm()] * 4,
        [wind.shape, tile, tile, row_msg, row_msg, (rows, LANES), (rows, LANES)],
        1 << 29,
        [pltpu.VMEM(cells.shape, jnp.int32), pltpu.VMEM(scale.shape, F32), pltpu.SemaphoreType.DMA((4,))],
    )(sent[0], far(wind), far(wgt), far(cells), far(scale))

    row_even, row_odd = call(
        functools.partial(join_kernel, fields, copies), [vmem()] * (2 + copies), [row_msg, row_msg], 1 << 16
    )(row_first, row_last, *strips)
    got_even, got_odd = neighbour_swap(row_even, row_odd, "lat")
    even_tile, odd_tile = call(
        functools.partial(cols_kernel, fields, copies), [vmem()] * (2 + copies), [col_msg, col_msg], 1 << 28
    )(col_low, col_high, *strips)

    halo_rows, msg_even, msg_odd = call(
        functools.partial(rows_kernel, fields, copies, rows // 8),
        [vmem()] * 4,
        [(lay.count, 8, cols), col_msg, col_msg],
        1 << 16,
    )(got_even, got_odd, even_tile, odd_tile)
    got_even, got_odd = neighbour_swap(msg_even, msg_odd, "lon")

    base_shape = (len(line_planes(lay)),) + col_msg
    part, even_base, odd_base, even_wgt, odd_wgt, factors = call(
        functools.partial(inner_kernel, copies),
        [vmem()] * (6 + copies),
        [tile, base_shape, base_shape, col_msg, col_msg, (8 * -(-3 * (2 * fields - 1) // 8), LANES)],
        1 << 29,
    )(sent[0], wgt_near, wind_near, hmap, mixrows, halo_rows, *bulk)
    (part,) = call(
        functools.partial(side_kernel, copies, False), [vmem()] * 5, [tile], 1 << 28
    )(got_even, even_base, even_wgt, factors, part)
    (out,) = call(
        functools.partial(side_kernel, copies, True),
        [vmem()] * 5,
        [tile],
        1 << 25,
        [pltpu.VMEM(tile, F32), pltpu.SemaphoreType.DMA((fields,))],
        hbm(),
    )(got_odd, odd_base, odd_wgt, factors, part)
    return out[None]


def solution(mesh):
    in_specs = (
        P("win", None, "lat", "lon"),
        P("win", None, "lat", "lon"),
        P("win", None, "lat", "lon"),
        P("win", None, None),
        P("win", "lat", "lon", None),
        P("win", None, "lat", "lon", None),
    )
    out_specs = P("win", None, "lat", "lon")

    return jax.shard_map(per_device, mesh=mesh, in_specs=in_specs, out_specs=out_specs, check_vma=False)
```

```python
import functools

import jax
import jax.numpy as jnp
from jax import lax
from jax.experimental import pallas as pl
from jax.experimental.pallas import tpu as pltpu
from jax.sharding import PartitionSpec as P


DIFFUSION = 0.15
HALO = 4
RIM = 2
LANES = 128
F32 = jnp.float32


def even_pairs(n):
    return [(i, i ^ 1) for i in range(n)]


def odd_pairs(n):
    return [(i, (i + 1 if i % 2 else i - 1) % n) for i in range(n)]


def ring(n, step):
    return [(i, (i + step) % n) for i in range(n)]


def neighbour_swap(even_msg, odd_msg, axis):
    n = lax.axis_size(axis)
    from_even = lax.ppermute(even_msg, axis, even_pairs(n))
    from_odd = lax.ppermute(odd_msg, axis, odd_pairs(n))
    return from_even, from_odd


def window_swap(down, up):
    n = lax.axis_size("win")
    if n == 2:
        got = lax.ppermute(down, "win", even_pairs(n))
        return got, got
    return lax.ppermute(down, "win", ring(n, -1)), lax.ppermute(up, "win", ring(n, 1))


def sub_iota(shape):
    return lax.broadcasted_iota(jnp.int32, shape, len(shape) - 2)


def lane_iota(shape):
    return lax.broadcasted_iota(jnp.int32, shape, len(shape) - 1)


def turn(x, shift, axis):
    shift %= x.shape[axis]
    return pltpu.roll(x, shift, axis) if shift else x


def axis_even(axis):
    return lax.axis_index(axis) % 2 == 0


def line_planes(lay):
    fields = lay.fields
    lines = [range(fields), range(fields, fields + 2), range(fields + 2, lay.own)]
    for k in range(lay.copies):
        base = lay.own + k * lay.packet
        lines += [range(base, base + fields), range(base + fields, base + lay.packet)]
    return lines


class Layout:
    def __init__(self, fields, copies):
        self.fields, self.copies = fields, copies
        self.own = 2 + 2 * fields
        self.packet = 2 * fields
        self.depths = [HALO] * (fields + 2) + [RIM] * (fields + self.packet * copies)
        self.count = len(self.depths)
        self.starts = [sum(self.depths[:j]) for j in range(self.count)]
        self.used = sum(self.depths)
        self.row_blocks = -(-self.used // 8)
        spots = [0, HALO] + [2 * HALO + RIM * k for k in range(1 + 2 * copies)]
        self.group = 2 * HALO + RIM * (1 + 2 * copies)
        self.wide = self.group * fields
        self.lanes = [0] * self.count
        for spot, members in zip(spots, line_planes(self)):
            for f, j in enumerate(members):
                self.lanes[j] = self.group * f + spot
        self.spots = spots

    def groups(self, blocks, width):
        per = -(-blocks // (LANES // width))
        return -(-blocks // per), per


def squeeze_lanes(wide, width, lay):
    blocks = wide.shape[0] // 8
    groups, per = lay.groups(blocks, width)
    lane = lane_iota((8, LANES))
    out = []
    for i in range(per):
        block = None
        for g in range(groups):
            if g * per + i < blocks:
                part = turn(wide[8 * (g * per + i) : 8 * (g * per + i) + 8], width * g, 1)
                block = part if block is None else jnp.where(lane >= width * g, part, block)
        out.append(block)
    return out


def spread_lanes(tight, blocks, width, lay):
    _, per = lay.groups(blocks, width)
    out = []
    for b in range(blocks):
        g, i = b // per, b % per
        out.append(turn(tight[i], -width * g, 1))
    return jnp.concatenate(out, axis=0)


def pack_rows(pieces, blocks):
    out = [None] * blocks
    for block, first, at, depth in pieces:
        b, s = at // 8, at % 8
        moved = turn(block, s - first, 0)
        sub = sub_iota(moved.shape)
        out[b] = moved if out[b] is None else jnp.where((sub >= s) & (sub < s + depth), moved, out[b])
    return out


def pack_lanes(pieces, out=None):
    for block, first, at, depth in pieces:
        moved = turn(block, at - first, 1)
        lane = lane_iota(moved.shape)
        out = moved if out is None else jnp.where((lane >= at) & (lane < at + depth), moved, out)
    return out


def load_kernel(swap2, copies, *refs):
    inc_far, wgt_far, wind_far, mix_far, mixrows = refs[:5]
    bulk = refs[5 : 5 + copies]
    strips = refs[5 + copies : 5 + 2 * copies]
    mix, sems = refs[5 + 2 * copies :]
    packet, rows, cols = bulk[0].shape
    fields = packet // 2
    lay = Layout(fields, copies)
    sends_up = lax.axis_index("win") == 0
    moves = [
        pltpu.make_async_copy(inc_far, ref.at[pl.ds(0, fields)], sems.at[i]) for i, ref in enumerate(bulk)
    ]
    moves.append(pltpu.make_async_copy(mix_far, mix, sems.at[2]))
    to_down = pltpu.make_async_copy(wgt_far, bulk[0].at[pl.ds(fields, fields)], sems.at[3])
    to_up = pltpu.make_async_copy(wind_far, bulk[-1].at[pl.ds(fields, 2)], sems.at[4])

    def on(condition, action):
        if swap2:
            pl.when(condition)(action)
        else:
            action()

    for move in moves:
        move.start()
    on(sends_up, lambda: to_up.start())
    on(jnp.logical_not(sends_up), lambda: to_down.start())
    for move in moves:
        move.wait()
    which = sub_iota(mixrows.shape)
    spread = jnp.zeros(mixrows.shape, F32)
    for f in range(fields):
        for g in range(fields):
            spread = jnp.where(which == f * fields + g, mix[f, 0, g], spread)
    mixrows[...] = spread

    def fill_up():
        to_up.wait()
        used = mixrows.shape[0]
        bulk[-1][packet - 1, pl.ds(0, used), :] = spread[:, :cols]
        bulk[-1][packet - 1, pl.ds(used, rows - used), :] = jnp.zeros((rows - used, cols), F32)

    on(sends_up, fill_up)
    on(jnp.logical_not(sends_up), lambda: to_down.wait())

    for k, ref in enumerate(strips):
        planes = [bulk[k][j] for j in range(packet)]
        pieces = []
        for j, x in enumerate(planes):
            pieces.append((x[:8], 0, 4 * j, RIM))
            pieces.append((x[-8:], 8 - RIM, 4 * j + 2, RIM))
        blocks = pack_rows(pieces, -(-4 * lay.packet // 8))
        halves = cols // LANES
        for m, block in enumerate(blocks):
            for h in range(halves):
                ref[pl.ds(8 * (m * halves + h), 8), :] = block[:, h * LANES : (h + 1) * LANES]
        pieces = []
        for j, x in enumerate(planes):
            pieces.append((x[:, :LANES], 0, 4 * j, RIM))
            pieces.append((x[:, -LANES:], LANES - RIM, 4 * j + 2, RIM))
        for m, block in enumerate(squeeze_lanes(pack_lanes(pieces), 4 * lay.packet, lay)):
            ref[pl.ds(8 * (len(blocks) * halves + m), 8), :] = block


def own_kernel(copies, bulk, wind_far, wgt_far, cells_far, scale_far, *refs):
    wind, wgt, hmap, row_first, row_last, col_low, col_high, cells, scale, sems = refs
    moves = [
        pltpu.make_async_copy(src, dst, sems.at[i])
        for i, (src, dst) in enumerate(
            [(cells_far, cells), (scale_far, scale), (wind_far, wind), (wgt_far, wgt)]
        )
    ]
    for move in moves:
        move.start()
    packet, rows, cols = bulk.shape
    fields = packet // 2
    inc = bulk
    lay = Layout(fields, copies)
    moves[0].wait()
    moves[1].wait()
    nobs = cells.shape[-1]
    index = cells[...]
    row_hot = sub_iota((rows, nobs)) == index // cols
    col_hot = (sub_iota((cols, nobs)) == index % cols).astype(F32).astype(jnp.bfloat16)
    terms = []
    for f in range(fields):
        rest = scale[f]
        for _ in range(3):
            part = rest.astype(jnp.bfloat16)
            rest = rest - part.astype(F32)
            terms.append(jnp.where(row_hot, part.astype(F32), 0.0).astype(jnp.bfloat16))
    sums = lax.dot_general(
        jnp.concatenate(terms, axis=0), col_hot, (((1,), (1,)), ((), ())), preferred_element_type=F32
    )
    moves[2].wait()
    planes = [inc[f] for f in range(fields)] + [wind[0], wind[1]]
    for f in range(fields):
        base = 3 * f * rows
        value = sums[base : base + rows] + (
            sums[base + rows : base + 2 * rows] + sums[base + 2 * rows : base + 3 * rows]
        )
        hmap[f] = value
        planes.append(value)
    where = list(zip(planes, lay.starts, lay.depths))
    first = pack_rows([(x[:8], 0, at, d) for x, at, d in where], lay.row_blocks)
    last = pack_rows([(x[-8:], 8 - d, at, d) for x, at, d in where], lay.row_blocks)
    for m in range(lay.row_blocks):
        blank = jnp.zeros((8, cols), F32)
        row_first[pl.ds(8 * m, 8), :] = blank if first[m] is None else first[m]
        row_last[pl.ds(8 * m, 8), :] = blank if last[m] is None else last[m]
    where = list(zip(planes, lay.lanes, lay.depths))
    col_low[...] = pack_lanes([(x[:, :LANES], 0, at, d) for x, at, d in where])
    col_high[...] = pack_lanes([(x[:, -LANES:], LANES - d, at, d) for x, at, d in where])
    moves[3].wait()


def join_kernel(fields, copies, *refs):
    row_first, row_last = refs[:2]
    strips = refs[2 : 2 + copies]
    row_even, row_odd = refs[2 + copies :]
    lay = Layout(fields, copies)
    cols = row_first.shape[1]
    halves = cols // LANES
    first_pieces, last_pieces = [], []
    for k, ref in enumerate(strips):
        blocks = [
            jnp.concatenate([ref[pl.ds(8 * (m * halves + h), 8), :] for h in range(halves)], axis=1)
            for m in range(-(-4 * lay.packet // 8))
        ]
        for j in range(lay.packet):
            at = lay.starts[lay.own + k * lay.packet + j]
            first_pieces.append((blocks[4 * j // 8], 4 * j % 8, at, RIM))
            last_pieces.append((blocks[4 * j // 8], 4 * j % 8 + 2, at, RIM))
    is_even = axis_even("lat")
    own_used = lay.starts[lay.own]
    first = pack_rows(first_pieces, lay.row_blocks)
    last = pack_rows(last_pieces, lay.row_blocks)
    for m in range(lay.row_blocks):
        a, b = row_first[pl.ds(8 * m, 8), :], row_last[pl.ds(8 * m, 8), :]
        if first[m] is not None:
            other = sub_iota(a.shape) + 8 * m >= own_used
            a, b = jnp.where(other, first[m], a), jnp.where(other, last[m], b)
        row_even[pl.ds(8 * m, 8), :] = jnp.where(is_even, b, a)
        row_odd[pl.ds(8 * m, 8), :] = jnp.where(is_even, a, b)


def cols_kernel(fields, copies, *refs):
    col_low, col_high = refs[:2]
    strips = refs[2 : 2 + copies]
    even_out, odd_out = refs[2 + copies :]
    lay = Layout(fields, copies)
    rows = col_low.shape[0]
    low_pieces, high_pieces = [], []
    for k, ref in enumerate(strips):
        _, per = lay.groups(rows // 8, 4 * lay.packet)
        base = ref.shape[0] - 8 * per
        tight = [ref[pl.ds(base + 8 * i, 8), :] for i in range(per)]
        wide = spread_lanes(tight, rows // 8, 4 * lay.packet, lay)
        for j in range(lay.packet):
            at = lay.lanes[lay.own + k * lay.packet + j]
            low_pieces.append((wide, 4 * j, at, RIM))
            high_pieces.append((wide, 4 * j + 2, at, RIM))
    lon_even = axis_even("lon")
    low = pack_lanes(low_pieces, col_low[...])
    high = pack_lanes(high_pieces, col_high[...])
    blank = jnp.zeros((8, LANES), F32)
    for ref, x in ((even_out, jnp.where(lon_even, high, low)), (odd_out, jnp.where(lon_even, low, high))):
        for i, block in enumerate(squeeze_lanes(jnp.concatenate([x, blank], axis=0), lay.wide, lay)):
            ref[pl.ds(8 * i, 8), :] = block


def lat_inside(width):
    here = lax.axis_index("lat")
    upper = sub_iota((8, width)) < HALO
    from_high = (here < lax.axis_size("lat") - 1).astype(jnp.int32)
    from_low = (here > 0).astype(jnp.int32)
    return jnp.where(upper, from_high, from_low) > 0


def rows_kernel(fields, copies, tail, got_even, got_odd, even_tile, odd_tile, halo_rows, msg_even, msg_odd):
    lay = Layout(fields, copies)
    cols = got_even.shape[-1]
    is_even = axis_even("lat")
    inside = lat_inside(cols)
    sub = sub_iota((8, cols))
    high, low = [], []
    for m in range(lay.row_blocks):
        a = got_even[pl.ds(8 * m, 8), :]
        b = got_odd[pl.ds(8 * m, 8), :]
        high.append(jnp.where(is_even, a, b))
        low.append(jnp.where(is_even, b, a))
    blocks = []
    for j, (at, d) in enumerate(zip(lay.starts, lay.depths)):
        above = turn(high[at // 8], -(at % 8), 0)
        below = turn(low[at // 8], 8 - d - at % 8, 0)
        block = jnp.where(sub < d, above, jnp.where(sub >= 8 - d, below, 0.0))
        block = jnp.where(inside, block, 0.0)
        halo_rows[j] = block
        blocks.append(block)
    where = list(zip(blocks, lay.lanes, lay.depths))
    low_tail = pack_lanes([(x[:, :LANES], 0, at, d) for x, at, d in where])
    high_tail = pack_lanes([(x[:, -LANES:], LANES - d, at, d) for x, at, d in where])
    lon_even = axis_even("lon")
    per = even_tile.shape[0] // 8
    shift = lay.wide * (tail // per)
    lane = lane_iota((8, LANES))
    for ref, tile, x in (
        (msg_even, even_tile, jnp.where(lon_even, high_tail, low_tail)),
        (msg_odd, odd_tile, jnp.where(lon_even, low_tail, high_tail)),
    ):
        for i in range(per):
            block = tile[pl.ds(8 * i, 8), :]
            if i == tail % per:
                block = jnp.where((lane >= shift) & (lane < shift + lay.wide), turn(x, shift, 1), block)
            ref[pl.ds(8 * i, 8), :] = block


def row_mask(rows, width):
    inside = lat_inside(width)

    def clear(field):
        return jnp.concatenate([field[:rows], jnp.where(inside, field[rows:], 0.0)], axis=0)

    return clear


def north(x):
    return pltpu.roll(x, x.shape[0] - 1, 0)


def south(x):
    return pltpu.roll(x, 1, 0)


def east_of(x):
    return pltpu.roll(x, x.shape[1] - 1, 1)


def west_of(x):
    return pltpu.roll(x, 1, 1)


def mixing(spread, fields):
    return lambda f, g: spread[f * fields + g : f * fields + g + 1]


def blend(mix, field, f):
    total = None
    for g in range(len(field)):
        factor = mix(f, g)
        if f == g:
            factor = factor + (1.0 - 4.0 * DIFFUSION)
        term = factor * field[g]
        total = term if total is None else total + term
    return total


def tangent(field, u, v, mix):
    kn, ks, ke, kw = DIFFUSION - v, DIFFUSION + v, DIFFUSION - u, DIFFUSION + u
    return [
        blend(mix, field, f)
        + (kn * north(x) + ks * south(x))
        + (ke * east_of(x) + kw * west_of(x))
        for f, x in enumerate(field)
    ]


def adjoint(field, u, v, mix):
    kn, ks, ke, kw = DIFFUSION + v, DIFFUSION - v, DIFFUSION + u, DIFFUSION - u
    return [
        blend(lambda a, b: mix(b, a), field, f)
        + (north(kn * x) + south(ks * x))
        + (east_of(ke * x) + west_of(kw * x))
        for f, x in enumerate(field)
    ]


def product(own, above, below, wgt, mix, prior_mix, fields, rows):
    clear = row_mask(rows, own[0].shape[1])
    here = lax.axis_index("win")
    has_later = here < lax.axis_size("win") - 1
    has_earlier = here > 0
    inc, wind, hmap = own[:fields], own[fields : fields + 2], own[fields + 2 :]
    fwd = [clear(x) for x in tangent(inc, *wind, mix)]
    fwd = tangent(fwd, *wind, mix)
    source = []
    for f in range(fields):
        later = above[fields + f] * (above[f] - fwd[f])
        source.append(clear(hmap[f] * fwd[f] - jnp.where(has_later, later, 0.0)))
    back = [clear(x) for x in adjoint(source, *wind, mix)]
    back = adjoint(back, *wind, mix)
    prior_wind = below[fields : fields + 2]
    prior = [clear(x) for x in tangent(below[:fields], *prior_wind, prior_mix)]
    prior = tangent(prior, *prior_wind, prior_mix)
    return [
        wgt[f] * (inc[f][:rows] - jnp.where(has_earlier, prior[f][:rows], 0.0)) + back[f][:rows]
        for f in range(fields)
    ]


def strip_lines(tiles, group):
    west, east = None, None
    for f, x in enumerate(tiles):
        low = turn(x[:, :LANES], group * f + HALO, 1)
        high = turn(x[:, -LANES:], group * f + group - HALO, 1)
        lane = lane_iota(low.shape)
        west = low if f == 0 else jnp.where(lane >= group * f, low, west)
        east = high if f == 0 else jnp.where(lane >= group * f, high, east)
    return west, east


def line_offsets(fields):
    return [o for o in range(1 - fields, fields)]


def line_factors(mix, lay):
    fields = lay.fields
    lane = lane_iota((1, LANES)) % lay.wide
    rows = []
    for o in line_offsets(fields):
        row = jnp.zeros((1, LANES), F32)
        for f in range(fields):
            if 0 <= f - o < fields:
                factor = mix(f, f - o)[:, :LANES]
                if o == 0:
                    factor = factor + (1.0 - 4.0 * DIFFUSION)
                row = jnp.where((lane >= lay.group * f) & (lane < lay.group * (f + 1)), factor, row)
        rows.append(row)
    return rows


def line_blend(factors, x, fields, group):
    total = None
    for o, factor in zip(line_offsets(fields), factors):
        term = factor * turn(x, group * o, 1)
        total = term if total is None else total + term
    return total


def line_wind(pair, lay):
    group = lay.group
    lane = lane_iota(pair.shape) % lay.wide
    up, down = turn(pair, group, 1), turn(pair, -group, 1)
    far_up = turn(pair, 2 * group, 1)
    u = jnp.where(lane < group, pair, jnp.where(lane < 2 * group, up, far_up))
    v = jnp.where(lane < group, down, jnp.where(lane < 2 * group, pair, up))
    return u, v


def folded(lay, blocks):
    groups, per = lay.groups(blocks, lay.wide)
    end = (blocks - 1) % per
    far = lay.wide * (groups - 1)
    sub, part = sub_iota((8, LANES)), lane_iota((8, LANES)) // lay.wide

    def put(x, i, block):
        pieces = [x[8 * j : 8 * j + 8] for j in range(per)]
        pieces[i] = block
        return jnp.concatenate(pieces, axis=0)

    def up(x):
        y = pltpu.roll(x, x.shape[0] - 1, 0)
        last = y[8 * (per - 1) :]
        y = put(y, per - 1, jnp.where((sub == 7) & (part < groups - 1), turn(last, -lay.wide, 1), last))
        wrap = turn(turn(x[:8], 7, 0), far, 1)
        here = y[8 * end : 8 * end + 8]
        return put(y, end, jnp.where((sub == 7) & (part == groups - 1), wrap, here))

    def down(x):
        y = pltpu.roll(x, 1, 0)
        first = y[:8]
        wrap = turn(turn(x[8 * end : 8 * end + 8], 1, 0), -far, 1)
        fixed = jnp.where(part == 0, wrap, turn(first, lay.wide, 1))
        return put(y, 0, jnp.where(sub == 0, fixed, first))

    return up, down


def line_tangent(x, u, v, factors, lay, up, down):
    kn, ks, ke, kw = DIFFUSION - v, DIFFUSION + v, DIFFUSION - u, DIFFUSION + u
    return (
        line_blend(factors, x, lay.fields, lay.group)
        + (kn * up(x) + ks * down(x))
        + (ke * east_of(x) + kw * west_of(x))
    )


def line_adjoint(x, u, v, factors, lay, up, down):
    kn, ks, ke, kw = DIFFUSION + v, DIFFUSION - v, DIFFUSION + u, DIFFUSION - u
    return (
        line_blend(factors, x, lay.fields, lay.group)
        + (up(kn * x) + down(ks * x))
        + (east_of(ke * x) + west_of(kw * x))
    )


def inner_kernel(copies, inc, wgt, wind, hmap, mixrows, halo_rows, *refs):
    bulk = refs[:copies]
    part, even_base, odd_base, even_wgt, odd_wgt, factors = refs[copies:]
    fields, rows, cols = wgt.shape
    lay = Layout(fields, copies)
    tiles = [inc[f] for f in range(fields)] + [wind[0], wind[1]] + [hmap[f] for f in range(fields)]
    for ref in bulk:
        tiles += [ref[j] for j in range(lay.packet)]
    planes = [jnp.concatenate([tile, halo_rows[j]], axis=0) for j, tile in enumerate(tiles)]
    lon_even = axis_even("lon")

    def store(even_ref, odd_ref, tiles):
        west, east = strip_lines(tiles, lay.group)
        west, east = squeeze_lanes(west, lay.wide, lay), squeeze_lanes(east, lay.wide, lay)
        for i, (w, e) in enumerate(zip(west, east)):
            even_ref[pl.ds(8 * i, 8), :] = jnp.where(lon_even, e, w)
            odd_ref[pl.ds(8 * i, 8), :] = jnp.where(lon_even, w, e)

    for k, members in enumerate(line_planes(lay)):
        store(even_base.at[k], odd_base.at[k], [planes[j] for j in members])
    blank = jnp.zeros((2 * HALO, cols), F32)
    store(even_wgt, odd_wgt, [jnp.concatenate([wgt[f], blank], axis=0) for f in range(fields)])
    above = planes[lay.own : lay.own + lay.packet]
    below = planes[-lay.packet :]
    spread = bulk[-1][2 * fields - 1, :16]
    mix, prior_mix = mixing(mixrows[:, :cols], fields), mixing(spread, fields)
    lists = []
    for maker in (mix, lambda f, g: mix(g, f), prior_mix):
        lists += line_factors(maker, lay)
    for i, row in enumerate(lists):
        factors[i : i + 1] = row
    result = product(planes[: lay.own], above, below, wgt, mix, prior_mix, fields, rows)
    for f in range(fields):
        part[f] = result[f]


def side_kernel(copies, is_odd, got, base, wgt_line, factors, part, *refs):
    fields, rows, cols = part.shape
    lay = Layout(fields, copies)
    group, wide = lay.group, lay.wide
    out = refs[1] if is_odd else refs[0]
    on_east = axis_even("lon") != is_odd
    split = is_odd and cols > LANES
    if split:
        out_far, sems = refs[0], refs[2]

        def ready(start):
            lanes = pl.ds(start, cols - LANES)
            return pltpu.make_async_copy(part.at[:, :, lanes], out_far.at[:, :, lanes], sems.at[fields])

        def changed(f, start):
            return pltpu.make_async_copy(out.at[f], out_far.at[f, :, pl.ds(start, LANES)], sems.at[f])

        def by_side(east, west):
            pl.when(on_east)(east)
            pl.when(jnp.logical_not(on_east))(west)

        by_side(lambda: ready(0).start(), lambda: ready(LANES).start())
    msg = got[...]
    lane, sub = lane_iota(msg.shape), sub_iota(msg.shape)
    within = lane % wide % group
    side = jnp.where(on_east, (within >= group - HALO).astype(jnp.int32), (within < HALO).astype(jnp.int32)) > 0
    lines = []
    for k, (spot, members) in enumerate(zip(lay.spots, line_planes(lay))):
        depth = lay.depths[members[0]]
        moved = jnp.where(
            on_east, turn(msg, group - HALO - spot, 1), turn(msg, HALO - depth - spot, 1)
        )
        lines.append(jnp.where(side, moved, base[k]))
    row = sub + msg.shape[0] * (lane // wide)
    here = lax.axis_index("lat")
    from_high = (here < lax.axis_size("lat") - 1).astype(jnp.int32)
    from_low = (here > 0).astype(jnp.int32)
    inside = jnp.where(row < rows, 1, jnp.where(row < rows + HALO, from_high, from_low)) > 0

    def clear(x):
        return jnp.where(inside, x, 0.0)

    up, down = folded(lay, rows // 8 + 1)
    win = lax.axis_index("win")
    has_later = win < lax.axis_size("win") - 1
    has_earlier = win > 0
    count = 2 * fields - 1
    every = factors[...]
    mix, mix_back, mix_prior = [
        [every[g * count + i : g * count + i + 1] for i in range(count)] for g in range(3)
    ]
    inc, hmap = lines[0], lines[2]
    u, v = line_wind(lines[1], lay)
    fwd = clear(line_tangent(inc, u, v, mix, lay, up, down))
    fwd = line_tangent(fwd, u, v, mix, lay, up, down)
    later = lines[4] * (lines[3] - fwd)
    back = clear(hmap * fwd - jnp.where(has_later, later, 0.0))
    back = clear(line_adjoint(back, u, v, mix_back, lay, up, down))
    back = line_adjoint(back, u, v, mix_back, lay, up, down)
    u, v = line_wind(lines[-1], lay)
    prior = clear(line_tangent(lines[-2], u, v, mix_prior, lay, up, down))
    prior = line_tangent(prior, u, v, mix_prior, lay, up, down)
    result = wgt_line[...] * (inc - jnp.where(has_earlier, prior, 0.0)) + back
    per = msg.shape[0] // 8
    lane = lane_iota((8, LANES))
    to_west = jnp.where(on_east, 0, HALO)
    to_east = jnp.where(on_east, LANES - HALO, LANES)
    moves = []
    for f in range(fields):
        for m in range(rows // 8):
            i, at = m % per, wide * (m // per) + group * f
            block = result[8 * i : 8 * i + 8]
            low = turn(block, -(at + HALO), 1)
            high = turn(block, LANES - (at + group - HALO), 1)
            spot = pl.ds(8 * m, 8)
            if split:
                west = jnp.where(lane < to_west, low, part[f, spot, :LANES])
                east = jnp.where(lane >= to_east, high, part[f, spot, cols - LANES :])
                out[f, spot, :] = jnp.where(on_east, east, west)
            elif cols == LANES:
                whole = jnp.where(lane < to_west, low, part[f, spot, :])
                out[f, spot, :] = jnp.where(lane >= to_east, high, whole)
            else:
                out[f, spot, pl.ds(0, LANES)] = jnp.where(lane < to_west, low, part[f, spot, :LANES])
                for h in range(1, cols // LANES - 1):
                    out[f, spot, pl.ds(h * LANES, LANES)] = part[f, spot, h * LANES : (h + 1) * LANES]
                out[f, spot, pl.ds(cols - LANES, LANES)] = jnp.where(
                    lane >= to_east, high, part[f, spot, cols - LANES :]
                )
        if split:
            by_side(
                lambda f=f: changed(f, cols - LANES).start(), lambda f=f: changed(f, 0).start()
            )
        elif is_odd:
            moves.append(pltpu.make_async_copy(out.at[f], refs[0].at[f], refs[2].at[f]))
            moves[-1].start()
    for move in moves:
        move.wait()
    if split:
        for f in range(fields):
            by_side(lambda f=f: changed(f, cols - LANES).wait(), lambda f=f: changed(f, 0).wait())
        by_side(lambda: ready(0).wait(), lambda: ready(LANES).wait())


def vmem():
    return pl.BlockSpec(memory_space=pltpu.VMEM)


def hbm():
    return pl.BlockSpec(memory_space=pltpu.HBM)


def far(array):
    return pltpu.with_memory_space_constraint(array, pltpu.HBM)


def call(kernel, in_specs, shapes, flops, scratch=(), out_spec=None):
    return pl.pallas_call(
        kernel,
        scratch_shapes=scratch,
        compiler_params=pltpu.CompilerParams(vmem_limit_bytes=VMEM_LIMIT),
        out_shape=[s if isinstance(s, jax.ShapeDtypeStruct) else jax.ShapeDtypeStruct(s, F32) for s in shapes],
        in_specs=in_specs,
        out_specs=[out_spec or vmem()] * len(shapes),
        cost_estimate=pl.CostEstimate(flops=flops, bytes_accessed=1 << 20, transcendentals=0),
    )


VMEM_LIMIT = 12 << 20


def per_device(increment, model_weight, winds, reaction, obs_cells, obs_weight):
    inc = increment[0]
    wgt = model_weight[0]
    wind = winds[0]
    mix = reaction.transpose(1, 0, 2)
    fields, rows, cols = inc.shape
    nobs = obs_cells.shape[-1]
    cells = obs_cells.reshape(1, nobs)
    scale = obs_weight.reshape(fields, 1, nobs)
    tall = rows + 2 * HALO
    swap2 = lax.axis_size("win") == 2
    copies = 1 if swap2 else 2
    lay = Layout(fields, copies)
    tile = (fields, rows, cols)
    packet = (lay.packet, rows, cols)
    strip_rows = 8 * (-(-4 * lay.packet // 8) * (cols // LANES) + lay.groups(rows // 8, 4 * lay.packet)[1])
    row_msg = (8 * lay.row_blocks, cols)
    col_msg = (8 * lay.groups(tall // 8, lay.wide)[1], LANES)

    mixrows, *rest = call(
        functools.partial(load_kernel, swap2, copies),
        [hbm()] * 4,
        [(16, cols)] + [packet] * copies + [(strip_rows, LANES)] * copies,
        1 << 20,
        [pltpu.SMEM(mix.shape, F32), pltpu.SemaphoreType.DMA((5,))],
    )(far(inc), far(wgt), far(wind), far(mix))
    sent, strips = rest[:copies], rest[copies:]
    strips = window_swap(strips[0], strips[-1])[:copies]
    bulk = window_swap(sent[0], sent[-1])[:copies]

    wind_near, wgt_near, hmap, row_first, row_last, col_low, col_high = call(
        functools.partial(own_kernel, copies),
        [vmem()] + [hbm()] * 4,
        [wind.shape, tile, tile, row_msg, row_msg, (rows, LANES), (rows, LANES)],
        1 << 29,
        [pltpu.VMEM(cells.shape, jnp.int32), pltpu.VMEM(scale.shape, F32), pltpu.SemaphoreType.DMA((4,))],
    )(sent[0], far(wind), far(wgt), far(cells), far(scale))

    row_even, row_odd = call(
        functools.partial(join_kernel, fields, copies), [vmem()] * (2 + copies), [row_msg, row_msg], 1 << 16
    )(row_first, row_last, *strips)
    got_even, got_odd = neighbour_swap(row_even, row_odd, "lat")
    even_tile, odd_tile = call(
        functools.partial(cols_kernel, fields, copies), [vmem()] * (2 + copies), [col_msg, col_msg], 1 << 28
    )(col_low, col_high, *strips)

    halo_rows, msg_even, msg_odd = call(
        functools.partial(rows_kernel, fields, copies, rows // 8),
        [vmem()] * 4,
        [(lay.count, 8, cols), col_msg, col_msg],
        1 << 16,
    )(got_even, got_odd, even_tile, odd_tile)
    got_even, got_odd = neighbour_swap(msg_even, msg_odd, "lon")

    base_shape = (len(line_planes(lay)),) + col_msg
    part, even_base, odd_base, even_wgt, odd_wgt, factors = call(
        functools.partial(inner_kernel, copies),
        [vmem()] * (6 + copies),
        [tile, base_shape, base_shape, col_msg, col_msg, (8 * -(-3 * (2 * fields - 1) // 8), LANES)],
        1 << 29,
    )(sent[0], wgt_near, wind_near, hmap, mixrows, halo_rows, *bulk)
    (part,) = call(
        functools.partial(side_kernel, copies, False), [vmem()] * 5, [tile], 1 << 28
    )(got_even, even_base, even_wgt, factors, part)
    (out,) = call(
        functools.partial(side_kernel, copies, True),
        [vmem()] * 5,
        [tile],
        1 << 25,
        [pltpu.VMEM((fields, rows, min(cols, LANES)), F32), pltpu.SemaphoreType.DMA((fields + 1,))],
        hbm(),
    )(got_odd, odd_base, odd_wgt, factors, part)
    return out[None]


def solution(mesh):
    in_specs = (
        P("win", None, "lat", "lon"),
        P("win", None, "lat", "lon"),
        P("win", None, "lat", "lon"),
        P("win", None, None),
        P("win", "lat", "lon", None),
        P("win", None, "lat", "lon", None),
    )
    out_specs = P("win", None, "lat", "lon")

    return jax.shard_map(per_device, mesh=mesh, in_specs=in_specs, out_specs=out_specs, check_vma=False)
```

```python
import functools

import jax
import jax.numpy as jnp
from jax import lax
from jax.experimental import pallas as pl
from jax.experimental.pallas import tpu as pltpu
from jax.sharding import PartitionSpec as P


DIFFUSION = 0.15
HALO = 4
RIM = 2
LANES = 128
F32 = jnp.float32


def even_pairs(n):
    return [(i, i ^ 1) for i in range(n)]


def odd_pairs(n):
    return [(i, (i + 1 if i % 2 else i - 1) % n) for i in range(n)]


def ring(n, step):
    return [(i, (i + step) % n) for i in range(n)]


def neighbour_swap(even_msg, odd_msg, axis):
    n = lax.axis_size(axis)
    from_even = lax.ppermute(even_msg, axis, even_pairs(n))
    from_odd = lax.ppermute(odd_msg, axis, odd_pairs(n))
    return from_even, from_odd


def window_swap(down, up):
    n = lax.axis_size("win")
    if n == 2:
        got = lax.ppermute(down, "win", even_pairs(n))
        return got, got
    return lax.ppermute(down, "win", ring(n, -1)), lax.ppermute(up, "win", ring(n, 1))


def sub_iota(shape):
    return lax.broadcasted_iota(jnp.int32, shape, len(shape) - 2)


def lane_iota(shape):
    return lax.broadcasted_iota(jnp.int32, shape, len(shape) - 1)


def turn(x, shift, axis):
    shift %= x.shape[axis]
    return pltpu.roll(x, shift, axis) if shift else x


def axis_even(axis):
    return lax.axis_index(axis) % 2 == 0


def line_planes(lay):
    fields = lay.fields
    lines = [range(fields), range(fields, fields + 2), range(fields + 2, lay.own)]
    for k in range(lay.copies):
        base = lay.own + k * lay.packet
        lines += [range(base, base + fields), range(base + fields, base + lay.packet)]
    return lines


class Layout:
    def __init__(self, fields, copies):
        self.fields, self.copies = fields, copies
        self.own = 2 + 2 * fields
        self.packet = 2 * fields
        self.depths = [HALO] * (fields + 2) + [RIM] * (fields + self.packet * copies)
        self.count = len(self.depths)
        self.starts = [sum(self.depths[:j]) for j in range(self.count)]
        self.used = sum(self.depths)
        self.row_blocks = -(-self.used // 8)
        spots = [0, HALO] + [2 * HALO + RIM * k for k in range(1 + 2 * copies)]
        self.group = 2 * HALO + RIM * (1 + 2 * copies)
        self.wide = self.group * fields
        self.lanes = [0] * self.count
        for spot, members in zip(spots, line_planes(self)):
            for f, j in enumerate(members):
                self.lanes[j] = self.group * f + spot
        self.spots = spots

    def groups(self, blocks, width):
        per = -(-blocks // (LANES // width))
        return -(-blocks // per), per


def squeeze_lanes(wide, width, lay):
    blocks = wide.shape[0] // 8
    groups, per = lay.groups(blocks, width)
    lane = lane_iota((8, LANES))
    out = []
    for i in range(per):
        block = None
        for g in range(groups):
            if g * per + i < blocks:
                part = turn(wide[8 * (g * per + i) : 8 * (g * per + i) + 8], width * g, 1)
                block = part if block is None else jnp.where(lane >= width * g, part, block)
        out.append(block)
    return out


def spread_lanes(tight, blocks, width, lay):
    _, per = lay.groups(blocks, width)
    out = []
    for b in range(blocks):
        g, i = b // per, b % per
        out.append(turn(tight[i], -width * g, 1))
    return jnp.concatenate(out, axis=0)


def pack_rows(pieces, blocks):
    out = [None] * blocks
    for block, first, at, depth in pieces:
        b, s = at // 8, at % 8
        moved = turn(block, s - first, 0)
        sub = sub_iota(moved.shape)
        out[b] = moved if out[b] is None else jnp.where((sub >= s) & (sub < s + depth), moved, out[b])
    return out


def pack_lanes(pieces, out=None):
    for block, first, at, depth in pieces:
        moved = turn(block, at - first, 1)
        lane = lane_iota(moved.shape)
        out = moved if out is None else jnp.where((lane >= at) & (lane < at + depth), moved, out)
    return out


def load_kernel(swap2, copies, *refs):
    inc_far, wgt_far, wind_far, mix_far, mixrows = refs[:5]
    bulk = refs[5 : 5 + copies]
    strips = refs[5 + copies : 5 + 2 * copies]
    mix, sems = refs[5 + 2 * copies :]
    packet, rows, cols = bulk[0].shape
    fields = packet // 2
    lay = Layout(fields, copies)
    sends_up = lax.axis_index("win") == 0
    moves = [
        pltpu.make_async_copy(inc_far, ref.at[pl.ds(0, fields)], sems.at[i]) for i, ref in enumerate(bulk)
    ]
    moves.append(pltpu.make_async_copy(mix_far, mix, sems.at[2]))
    to_down = pltpu.make_async_copy(wgt_far, bulk[0].at[pl.ds(fields, fields)], sems.at[3])
    to_up = pltpu.make_async_copy(wind_far, bulk[-1].at[pl.ds(fields, 2)], sems.at[4])

    def on(condition, action):
        if swap2:
            pl.when(condition)(action)
        else:
            action()

    for move in moves:
        move.start()
    on(sends_up, lambda: to_up.start())
    on(jnp.logical_not(sends_up), lambda: to_down.start())
    for move in moves:
        move.wait()
    which = sub_iota(mixrows.shape)
    spread = jnp.zeros(mixrows.shape, F32)
    for f in range(fields):
        for g in range(fields):
            spread = jnp.where(which == f * fields + g, mix[f, 0, g], spread)
    mixrows[...] = spread

    def fill_up():
        to_up.wait()
        used = mixrows.shape[0]
        bulk[-1][packet - 1, pl.ds(0, used), :] = spread[:, :cols]
        bulk[-1][packet - 1, pl.ds(used, rows - used), :] = jnp.zeros((rows - used, cols), F32)

    on(sends_up, fill_up)
    on(jnp.logical_not(sends_up), lambda: to_down.wait())

    for k, ref in enumerate(strips):
        planes = [bulk[k][j] for j in range(packet)]
        pieces = []
        for j, x in enumerate(planes):
            pieces.append((x[:8], 0, 4 * j, RIM))
            pieces.append((x[-8:], 8 - RIM, 4 * j + 2, RIM))
        blocks = pack_rows(pieces, -(-4 * lay.packet // 8))
        halves = cols // LANES
        for m, block in enumerate(blocks):
            for h in range(halves):
                ref[pl.ds(8 * (m * halves + h), 8), :] = block[:, h * LANES : (h + 1) * LANES]
        pieces = []
        for j, x in enumerate(planes):
            pieces.append((x[:, :LANES], 0, 4 * j, RIM))
            pieces.append((x[:, -LANES:], LANES - RIM, 4 * j + 2, RIM))
        for m, block in enumerate(squeeze_lanes(pack_lanes(pieces), 4 * lay.packet, lay)):
            ref[pl.ds(8 * (len(blocks) * halves + m), 8), :] = block


def own_kernel(copies, bulk, wind_far, wgt_far, cells_far, scale_far, *refs):
    wind, wgt, hmap, row_first, row_last, col_low, col_high, cells, scale, sems = refs
    moves = [
        pltpu.make_async_copy(src, dst, sems.at[i])
        for i, (src, dst) in enumerate(
            [(cells_far, cells), (scale_far, scale), (wind_far, wind), (wgt_far, wgt)]
        )
    ]
    for move in moves:
        move.start()
    packet, rows, cols = bulk.shape
    fields = packet // 2
    inc = bulk
    lay = Layout(fields, copies)
    moves[0].wait()
    moves[1].wait()
    nobs = cells.shape[-1]
    index = cells[...]
    row_hot = sub_iota((rows, nobs)) == index // cols
    col_hot = (sub_iota((cols, nobs)) == index % cols).astype(F32).astype(jnp.bfloat16)
    terms = []
    for f in range(fields):
        rest = scale[f]
        for _ in range(3):
            part = rest.astype(jnp.bfloat16)
            rest = rest - part.astype(F32)
            terms.append(jnp.where(row_hot, part.astype(F32), 0.0).astype(jnp.bfloat16))
    sums = lax.dot_general(
        jnp.concatenate(terms, axis=0), col_hot, (((1,), (1,)), ((), ())), preferred_element_type=F32
    )
    moves[2].wait()
    planes = [inc[f] for f in range(fields)] + [wind[0], wind[1]]
    for f in range(fields):
        base = 3 * f * rows
        value = sums[base : base + rows] + (
            sums[base + rows : base + 2 * rows] + sums[base + 2 * rows : base + 3 * rows]
        )
        hmap[f] = value
        planes.append(value)
    where = list(zip(planes, lay.starts, lay.depths))
    first = pack_rows([(x[:8], 0, at, d) for x, at, d in where], lay.row_blocks)
    last = pack_rows([(x[-8:], 8 - d, at, d) for x, at, d in where], lay.row_blocks)
    for m in range(lay.row_blocks):
        blank = jnp.zeros((8, cols), F32)
        row_first[pl.ds(8 * m, 8), :] = blank if first[m] is None else first[m]
        row_last[pl.ds(8 * m, 8), :] = blank if last[m] is None else last[m]
    where = list(zip(planes, lay.lanes, lay.depths))
    col_low[...] = pack_lanes([(x[:, :LANES], 0, at, d) for x, at, d in where])
    col_high[...] = pack_lanes([(x[:, -LANES:], LANES - d, at, d) for x, at, d in where])
    moves[3].wait()


def join_kernel(fields, copies, *refs):
    row_first, row_last = refs[:2]
    strips = refs[2 : 2 + copies]
    row_even, row_odd = refs[2 + copies :]
    lay = Layout(fields, copies)
    cols = row_first.shape[1]
    halves = cols // LANES
    first_pieces, last_pieces = [], []
    for k, ref in enumerate(strips):
        blocks = [
            jnp.concatenate([ref[pl.ds(8 * (m * halves + h), 8), :] for h in range(halves)], axis=1)
            for m in range(-(-4 * lay.packet // 8))
        ]
        for j in range(lay.packet):
            at = lay.starts[lay.own + k * lay.packet + j]
            first_pieces.append((blocks[4 * j // 8], 4 * j % 8, at, RIM))
            last_pieces.append((blocks[4 * j // 8], 4 * j % 8 + 2, at, RIM))
    is_even = axis_even("lat")
    own_used = lay.starts[lay.own]
    first = pack_rows(first_pieces, lay.row_blocks)
    last = pack_rows(last_pieces, lay.row_blocks)
    for m in range(lay.row_blocks):
        a, b = row_first[pl.ds(8 * m, 8), :], row_last[pl.ds(8 * m, 8), :]
        if first[m] is not None:
            other = sub_iota(a.shape) + 8 * m >= own_used
            a, b = jnp.where(other, first[m], a), jnp.where(other, last[m], b)
        row_even[pl.ds(8 * m, 8), :] = jnp.where(is_even, b, a)
        row_odd[pl.ds(8 * m, 8), :] = jnp.where(is_even, a, b)


def cols_kernel(fields, copies, *refs):
    col_low, col_high = refs[:2]
    strips = refs[2 : 2 + copies]
    even_out, odd_out = refs[2 + copies :]
    lay = Layout(fields, copies)
    rows = col_low.shape[0]
    low_pieces, high_pieces = [], []
    for k, ref in enumerate(strips):
        _, per = lay.groups(rows // 8, 4 * lay.packet)
        base = ref.shape[0] - 8 * per
        tight = [ref[pl.ds(base + 8 * i, 8), :] for i in range(per)]
        wide = spread_lanes(tight, rows // 8, 4 * lay.packet, lay)
        for j in range(lay.packet):
            at = lay.lanes[lay.own + k * lay.packet + j]
            low_pieces.append((wide, 4 * j, at, RIM))
            high_pieces.append((wide, 4 * j + 2, at, RIM))
    lon_even = axis_even("lon")
    low = pack_lanes(low_pieces, col_low[...])
    high = pack_lanes(high_pieces, col_high[...])
    blank = jnp.zeros((8, LANES), F32)
    for ref, x in ((even_out, jnp.where(lon_even, high, low)), (odd_out, jnp.where(lon_even, low, high))):
        for i, block in enumerate(squeeze_lanes(jnp.concatenate([x, blank], axis=0), lay.wide, lay)):
            ref[pl.ds(8 * i, 8), :] = block


def lat_inside(width):
    here = lax.axis_index("lat")
    upper = sub_iota((8, width)) < HALO
    from_high = (here < lax.axis_size("lat") - 1).astype(jnp.int32)
    from_low = (here > 0).astype(jnp.int32)
    return jnp.where(upper, from_high, from_low) > 0


def halo_blocks(lay, got_even, got_odd):
    cols = got_even.shape[-1]
    is_even = axis_even("lat")
    inside = lat_inside(cols)
    sub = sub_iota((8, cols))
    high, low = [], []
    for m in range(lay.row_blocks):
        a = got_even[pl.ds(8 * m, 8), :]
        b = got_odd[pl.ds(8 * m, 8), :]
        high.append(jnp.where(is_even, a, b))
        low.append(jnp.where(is_even, b, a))
    blocks = []
    for at, d in zip(lay.starts, lay.depths):
        above = turn(high[at // 8], -(at % 8), 0)
        below = turn(low[at // 8], 8 - d - at % 8, 0)
        block = jnp.where(sub < d, above, jnp.where(sub >= 8 - d, below, 0.0))
        block = jnp.where(inside, block, 0.0)
        blocks.append(block)
    return blocks


def rows_kernel(fields, copies, tail, got_even, got_odd, even_tile, odd_tile, msg_even, msg_odd):
    lay = Layout(fields, copies)
    blocks = halo_blocks(lay, got_even, got_odd)
    where = list(zip(blocks, lay.lanes, lay.depths))
    low_tail = pack_lanes([(x[:, :LANES], 0, at, d) for x, at, d in where])
    high_tail = pack_lanes([(x[:, -LANES:], LANES - d, at, d) for x, at, d in where])
    lon_even = axis_even("lon")
    per = even_tile.shape[0] // 8
    shift = lay.wide * (tail // per)
    lane = lane_iota((8, LANES))
    for ref, tile, x in (
        (msg_even, even_tile, jnp.where(lon_even, high_tail, low_tail)),
        (msg_odd, odd_tile, jnp.where(lon_even, low_tail, high_tail)),
    ):
        for i in range(per):
            block = tile[pl.ds(8 * i, 8), :]
            if i == tail % per:
                block = jnp.where((lane >= shift) & (lane < shift + lay.wide), turn(x, shift, 1), block)
            ref[pl.ds(8 * i, 8), :] = block


def row_mask(rows, width):
    inside = lat_inside(width)

    def clear(field):
        return jnp.concatenate([field[:rows], jnp.where(inside, field[rows:], 0.0)], axis=0)

    return clear


def north(x):
    return pltpu.roll(x, x.shape[0] - 1, 0)


def south(x):
    return pltpu.roll(x, 1, 0)


def east_of(x):
    return pltpu.roll(x, x.shape[1] - 1, 1)


def west_of(x):
    return pltpu.roll(x, 1, 1)


def mixing(spread, fields):
    return lambda f, g: spread[f * fields + g : f * fields + g + 1]


def blend(mix, field, f):
    total = None
    for g in range(len(field)):
        factor = mix(f, g)
        if f == g:
            factor = factor + (1.0 - 4.0 * DIFFUSION)
        term = factor * field[g]
        total = term if total is None else total + term
    return total


def tangent(field, u, v, mix):
    kn, ks, ke, kw = DIFFUSION - v, DIFFUSION + v, DIFFUSION - u, DIFFUSION + u
    return [
        blend(mix, field, f)
        + (kn * north(x) + ks * south(x))
        + (ke * east_of(x) + kw * west_of(x))
        for f, x in enumerate(field)
    ]


def adjoint(field, u, v, mix):
    kn, ks, ke, kw = DIFFUSION + v, DIFFUSION - v, DIFFUSION + u, DIFFUSION - u
    return [
        blend(lambda a, b: mix(b, a), field, f)
        + (north(kn * x) + south(ks * x))
        + (east_of(ke * x) + west_of(kw * x))
        for f, x in enumerate(field)
    ]


def product(own, above, below, wgt, mix, prior_mix, fields, rows):
    clear = row_mask(rows, own[0].shape[1])
    here = lax.axis_index("win")
    has_later = here < lax.axis_size("win") - 1
    has_earlier = here > 0
    inc, wind, hmap = own[:fields], own[fields : fields + 2], own[fields + 2 :]
    fwd = [clear(x) for x in tangent(inc, *wind, mix)]
    fwd = tangent(fwd, *wind, mix)
    source = []
    for f in range(fields):
        later = above[fields + f] * (above[f] - fwd[f])
        source.append(clear(hmap[f] * fwd[f] - jnp.where(has_later, later, 0.0)))
    back = [clear(x) for x in adjoint(source, *wind, mix)]
    back = adjoint(back, *wind, mix)
    prior_wind = below[fields : fields + 2]
    prior = [clear(x) for x in tangent(below[:fields], *prior_wind, prior_mix)]
    prior = tangent(prior, *prior_wind, prior_mix)
    return [
        wgt[f] * (inc[f][:rows] - jnp.where(has_earlier, prior[f][:rows], 0.0)) + back[f][:rows]
        for f in range(fields)
    ]


def strip_lines(tiles, group):
    west, east = None, None
    for f, x in enumerate(tiles):
        low = turn(x[:, :LANES], group * f + HALO, 1)
        high = turn(x[:, -LANES:], group * f + group - HALO, 1)
        lane = lane_iota(low.shape)
        west = low if f == 0 else jnp.where(lane >= group * f, low, west)
        east = high if f == 0 else jnp.where(lane >= group * f, high, east)
    return west, east


def line_offsets(fields):
    return [o for o in range(1 - fields, fields)]


def line_factors(mix, lay):
    fields = lay.fields
    lane = lane_iota((1, LANES)) % lay.wide
    rows = []
    for o in line_offsets(fields):
        row = jnp.zeros((1, LANES), F32)
        for f in range(fields):
            if 0 <= f - o < fields:
                factor = mix(f, f - o)[:, :LANES]
                if o == 0:
                    factor = factor + (1.0 - 4.0 * DIFFUSION)
                row = jnp.where((lane >= lay.group * f) & (lane < lay.group * (f + 1)), factor, row)
        rows.append(row)
    return rows


def line_blend(factors, x, fields, group):
    total = None
    for o, factor in zip(line_offsets(fields), factors):
        term = factor * turn(x, group * o, 1)
        total = term if total is None else total + term
    return total


def line_wind(pair, lay):
    group = lay.group
    lane = lane_iota(pair.shape) % lay.wide
    up, down = turn(pair, group, 1), turn(pair, -group, 1)
    far_up = turn(pair, 2 * group, 1)
    u = jnp.where(lane < group, pair, jnp.where(lane < 2 * group, up, far_up))
    v = jnp.where(lane < group, down, jnp.where(lane < 2 * group, pair, up))
    return u, v


def folded(lay, blocks):
    groups, per = lay.groups(blocks, lay.wide)
    end = (blocks - 1) % per
    far = lay.wide * (groups - 1)
    sub, part = sub_iota((8, LANES)), lane_iota((8, LANES)) // lay.wide

    def put(x, i, block):
        pieces = [x[8 * j : 8 * j + 8] for j in range(per)]
        pieces[i] = block
        return jnp.concatenate(pieces, axis=0)

    def up(x):
        y = pltpu.roll(x, x.shape[0] - 1, 0)
        last = y[8 * (per - 1) :]
        y = put(y, per - 1, jnp.where((sub == 7) & (part < groups - 1), turn(last, -lay.wide, 1), last))
        wrap = turn(turn(x[:8], 7, 0), far, 1)
        here = y[8 * end : 8 * end + 8]
        return put(y, end, jnp.where((sub == 7) & (part == groups - 1), wrap, here))

    def down(x):
        y = pltpu.roll(x, 1, 0)
        first = y[:8]
        wrap = turn(turn(x[8 * end : 8 * end + 8], 1, 0), -far, 1)
        fixed = jnp.where(part == 0, wrap, turn(first, lay.wide, 1))
        return put(y, 0, jnp.where(sub == 0, fixed, first))

    return up, down


def line_tangent(x, u, v, factors, lay, up, down):
    kn, ks, ke, kw = DIFFUSION - v, DIFFUSION + v, DIFFUSION - u, DIFFUSION + u
    return (
        line_blend(factors, x, lay.fields, lay.group)
        + (kn * up(x) + ks * down(x))
        + (ke * east_of(x) + kw * west_of(x))
    )


def line_adjoint(x, u, v, factors, lay, up, down):
    kn, ks, ke, kw = DIFFUSION + v, DIFFUSION - v, DIFFUSION + u, DIFFUSION - u
    return (
        line_blend(factors, x, lay.fields, lay.group)
        + (up(kn * x) + down(ks * x))
        + (east_of(ke * x) + west_of(kw * x))
    )


def inner_kernel(copies, inc, wgt, wind, hmap, mixrows, lat_even, lat_odd, *refs):
    bulk = refs[:copies]
    part, even_base, odd_base, even_wgt, odd_wgt, factors = refs[copies:]
    fields, rows, cols = wgt.shape
    lay = Layout(fields, copies)
    tiles = [inc[f] for f in range(fields)] + [wind[0], wind[1]] + [hmap[f] for f in range(fields)]
    for ref in bulk:
        tiles += [ref[j] for j in range(lay.packet)]
    halo_rows = halo_blocks(lay, lat_even, lat_odd)
    planes = [jnp.concatenate([tile, halo_rows[j]], axis=0) for j, tile in enumerate(tiles)]
    lon_even = axis_even("lon")

    def store(even_ref, odd_ref, tiles):
        west, east = strip_lines(tiles, lay.group)
        west, east = squeeze_lanes(west, lay.wide, lay), squeeze_lanes(east, lay.wide, lay)
        for i, (w, e) in enumerate(zip(west, east)):
            even_ref[pl.ds(8 * i, 8), :] = jnp.where(lon_even, e, w)
            odd_ref[pl.ds(8 * i, 8), :] = jnp.where(lon_even, w, e)

    for k, members in enumerate(line_planes(lay)):
        store(even_base.at[k], odd_base.at[k], [planes[j] for j in members])
    blank = jnp.zeros((2 * HALO, cols), F32)
    store(even_wgt, odd_wgt, [jnp.concatenate([wgt[f], blank], axis=0) for f in range(fields)])
    above = planes[lay.own : lay.own + lay.packet]
    below = planes[-lay.packet :]
    spread = bulk[-1][2 * fields - 1, :16]
    mix, prior_mix = mixing(mixrows[:, :cols], fields), mixing(spread, fields)
    lists = []
    for maker in (mix, lambda f, g: mix(g, f), prior_mix):
        lists += line_factors(maker, lay)
    for i, row in enumerate(lists):
        factors[i : i + 1] = row
    result = product(planes[: lay.own], above, below, wgt, mix, prior_mix, fields, rows)
    for f in range(fields):
        part[f] = result[f]


def side_kernel(copies, is_odd, got, base, wgt_line, factors, part, *refs):
    fields, rows, cols = part.shape
    lay = Layout(fields, copies)
    group, wide = lay.group, lay.wide
    out = refs[1] if is_odd else refs[0]
    on_east = axis_even("lon") != is_odd
    msg = got[...]
    lane, sub = lane_iota(msg.shape), sub_iota(msg.shape)
    within = lane % wide % group
    side = jnp.where(on_east, (within >= group - HALO).astype(jnp.int32), (within < HALO).astype(jnp.int32)) > 0
    lines = []
    for k, (spot, members) in enumerate(zip(lay.spots, line_planes(lay))):
        depth = lay.depths[members[0]]
        moved = jnp.where(
            on_east, turn(msg, group - HALO - spot, 1), turn(msg, HALO - depth - spot, 1)
        )
        lines.append(jnp.where(side, moved, base[k]))
    row = sub + msg.shape[0] * (lane // wide)
    here = lax.axis_index("lat")
    from_high = (here < lax.axis_size("lat") - 1).astype(jnp.int32)
    from_low = (here > 0).astype(jnp.int32)
    inside = jnp.where(row < rows, 1, jnp.where(row < rows + HALO, from_high, from_low)) > 0

    def clear(x):
        return jnp.where(inside, x, 0.0)

    up, down = folded(lay, rows // 8 + 1)
    win = lax.axis_index("win")
    has_later = win < lax.axis_size("win") - 1
    has_earlier = win > 0
    count = 2 * fields - 1
    every = factors[...]
    mix, mix_back, mix_prior = [
        [every[g * count + i : g * count + i + 1] for i in range(count)] for g in range(3)
    ]
    inc, hmap = lines[0], lines[2]
    u, v = line_wind(lines[1], lay)
    fwd = clear(line_tangent(inc, u, v, mix, lay, up, down))
    fwd = line_tangent(fwd, u, v, mix, lay, up, down)
    later = lines[4] * (lines[3] - fwd)
    back = clear(hmap * fwd - jnp.where(has_later, later, 0.0))
    back = clear(line_adjoint(back, u, v, mix_back, lay, up, down))
    back = line_adjoint(back, u, v, mix_back, lay, up, down)
    u, v = line_wind(lines[-1], lay)
    prior = clear(line_tangent(lines[-2], u, v, mix_prior, lay, up, down))
    prior = line_tangent(prior, u, v, mix_prior, lay, up, down)
    result = wgt_line[...] * (inc - jnp.where(has_earlier, prior, 0.0)) + back
    per = msg.shape[0] // 8
    lane = lane_iota((8, LANES))
    to_west = jnp.where(on_east, 0, HALO)
    to_east = jnp.where(on_east, LANES - HALO, LANES)
    moves = []
    for f in range(fields):
        for m in range(rows // 8):
            i, at = m % per, wide * (m // per) + group * f
            block = result[8 * i : 8 * i + 8]
            low = turn(block, -(at + HALO), 1)
            high = turn(block, LANES - (at + group - HALO), 1)
            spot = pl.ds(8 * m, 8)
            if cols == LANES:
                whole = jnp.where(lane < to_west, low, part[f, spot, :])
                out[f, spot, :] = jnp.where(lane >= to_east, high, whole)
            else:
                out[f, spot, pl.ds(0, LANES)] = jnp.where(lane < to_west, low, part[f, spot, :LANES])
                for h in range(1, cols // LANES - 1):
                    out[f, spot, pl.ds(h * LANES, LANES)] = part[f, spot, h * LANES : (h + 1) * LANES]
                out[f, spot, pl.ds(cols - LANES, LANES)] = jnp.where(
                    lane >= to_east, high, part[f, spot, cols - LANES :]
                )
        if is_odd:
            moves.append(pltpu.make_async_copy(out.at[f], refs[0].at[f], refs[2].at[f]))
            moves[-1].start()
    for move in moves:
        move.wait()


def vmem():
    return pl.BlockSpec(memory_space=pltpu.VMEM)


def hbm():
    return pl.BlockSpec(memory_space=pltpu.HBM)


def far(array):
    return pltpu.with_memory_space_constraint(array, pltpu.HBM)


def call(kernel, in_specs, shapes, flops, scratch=(), out_spec=None):
    return pl.pallas_call(
        kernel,
        scratch_shapes=scratch,
        compiler_params=pltpu.CompilerParams(vmem_limit_bytes=VMEM_LIMIT),
        out_shape=[s if isinstance(s, jax.ShapeDtypeStruct) else jax.ShapeDtypeStruct(s, F32) for s in shapes],
        in_specs=in_specs,
        out_specs=[out_spec or vmem()] * len(shapes),
        cost_estimate=pl.CostEstimate(flops=flops, bytes_accessed=1 << 20, transcendentals=0),
    )


VMEM_LIMIT = 12 << 20


def per_device(increment, model_weight, winds, reaction, obs_cells, obs_weight):
    inc = increment[0]
    wgt = model_weight[0]
    wind = winds[0]
    mix = reaction.transpose(1, 0, 2)
    fields, rows, cols = inc.shape
    nobs = obs_cells.shape[-1]
    cells = obs_cells.reshape(1, nobs)
    scale = obs_weight.reshape(fields, 1, nobs)
    tall = rows + 2 * HALO
    swap2 = lax.axis_size("win") == 2
    copies = 1 if swap2 else 2
    lay = Layout(fields, copies)
    tile = (fields, rows, cols)
    packet = (lay.packet, rows, cols)
    strip_rows = 8 * (-(-4 * lay.packet // 8) * (cols // LANES) + lay.groups(rows // 8, 4 * lay.packet)[1])
    row_msg = (8 * lay.row_blocks, cols)
    col_msg = (8 * lay.groups(tall // 8, lay.wide)[1], LANES)

    mixrows, *rest = call(
        functools.partial(load_kernel, swap2, copies),
        [hbm()] * 4,
        [(16, cols)] + [packet] * copies + [(strip_rows, LANES)] * copies,
        1 << 20,
        [pltpu.SMEM(mix.shape, F32), pltpu.SemaphoreType.DMA((5,))],
    )(far(inc), far(wgt), far(wind), far(mix))
    sent, strips = rest[:copies], rest[copies:]
    strips = window_swap(strips[0], strips[-1])[:copies]
    bulk = window_swap(sent[0], sent[-1])[:copies]

    wind_near, wgt_near, hmap, row_first, row_last, col_low, col_high = call(
        functools.partial(own_kernel, copies),
        [vmem()] + [hbm()] * 4,
        [wind.shape, tile, tile, row_msg, row_msg, (rows, LANES), (rows, LANES)],
        1 << 29,
        [pltpu.VMEM(cells.shape, jnp.int32), pltpu.VMEM(scale.shape, F32), pltpu.SemaphoreType.DMA((4,))],
    )(sent[0], far(wind), far(wgt), far(cells), far(scale))

    row_even, row_odd = call(
        functools.partial(join_kernel, fields, copies), [vmem()] * (2 + copies), [row_msg, row_msg], 1 << 16
    )(row_first, row_last, *strips)
    lat_even, lat_odd = neighbour_swap(row_even, row_odd, "lat")
    even_tile, odd_tile = call(
        functools.partial(cols_kernel, fields, copies), [vmem()] * (2 + copies), [col_msg, col_msg], 1 << 28
    )(col_low, col_high, *strips)

    msg_even, msg_odd = call(
        functools.partial(rows_kernel, fields, copies, rows // 8), [vmem()] * 4, [col_msg, col_msg], 1 << 16
    )(lat_even, lat_odd, even_tile, odd_tile)
    got_even, got_odd = neighbour_swap(msg_even, msg_odd, "lon")

    base_shape = (len(line_planes(lay)),) + col_msg
    part, even_base, odd_base, even_wgt, odd_wgt, factors = call(
        functools.partial(inner_kernel, copies),
        [vmem()] * (7 + copies),
        [tile, base_shape, base_shape, col_msg, col_msg, (8 * -(-3 * (2 * fields - 1) // 8), LANES)],
        1 << 29,
    )(sent[0], wgt_near, wind_near, hmap, mixrows, lat_even, lat_odd, *bulk)
    (part,) = call(
        functools.partial(side_kernel, copies, False), [vmem()] * 5, [tile], 1 << 28
    )(got_even, even_base, even_wgt, factors, part)
    (out,) = call(
        functools.partial(side_kernel, copies, True),
        [vmem()] * 5,
        [tile],
        1 << 25,
        [pltpu.VMEM(tile, F32), pltpu.SemaphoreType.DMA((fields,))],
        hbm(),
    )(got_odd, odd_base, odd_wgt, factors, part)
    return out[None]


def solution(mesh):
    in_specs = (
        P("win", None, "lat", "lon"),
        P("win", None, "lat", "lon"),
        P("win", None, "lat", "lon"),
        P("win", None, None),
        P("win", "lat", "lon", None),
        P("win", None, "lat", "lon", None),
    )
    out_specs = P("win", None, "lat", "lon")

    return jax.shard_map(per_device, mesh=mesh, in_specs=in_specs, out_specs=out_specs, check_vma=False)
```
